256 devices in a mesh: segment: 4 (over z_lo, core), zero: 64 (over x, y, z_hi).
Axes of the slice: x: 4, y: 4, z: 8 (z_hi: 4, z_lo: 2; z = z_hi * 2 + z_lo), core: 2. Of those that a mesh axis runs over, the one named last changes fastest.
Arguments:
- inputs: bfloat16 [2, 2, 8192, 2048], P(None, None, 'zero'), may hold values from -6 to 6
- cotangent: bfloat16 [2, 2, 8192, 2048], P(None, None, 'zero'), may hold values from -0.078125 to 0.078125
- norm_gain: bfloat16 [4, 2048], P('segment', 'zero'), may hold values from 0.099609375 to 1.8984375
- proj_in: bfloat16 [4, 2048, 256], P('segment', 'zero'), may hold values from -0.125 to 0.125
- proj_out: bfloat16 [4, 256, 2048], P('segment', 'zero'), may hold values from -0.375 to 0.375
Outputs:
- grad_norm_gain: float32 [4, 2048], P('segment', 'zero')
- grad_proj_in: float32 [4, 2048, 256], P('segment', 'zero')
- grad_proj_out: float32 [4, 256, 2048], P('segment', 'zero')
The draws below stay inside these ranges and needn't reach their ends.
All inputs are finite; a program needn't handle non-finite values.
Results may differ from the reference program's by a relative error of at most 0.012.
Values may be sent and summed in bfloat16 or wider, within the bound.
No kernel may reach another device: no remote copies, remote signals or barrier semaphores. Data moves between devices by JAX's collectives and lax.ppermute only.
A program may use at most 64 MiB of HBM per device.

```python
import jax
import jax.numpy as jnp
from jax import lax

D = 2048
R = 256
MB = 2
TOKENS = 8192
LAYERS = 4


def block_scale(key, dims, cuts, smallest, top_value):
    loudness = 1.0
    for dim, shards_of in cuts:
        draws = jax.random.uniform(jax.random.fold_in(jax.random.fold_in(key, 6), dim), (shards_of,), jnp.float32, smallest / len(cuts), top_value / len(cuts))
        loudness = loudness * jnp.repeat(jnp.exp(draws), dims[dim] // shards_of).reshape((-1,) + (1,) * (len(dims) - 1 - dim))
    return loudness


def normal_values(key, extent, deviation, limit, shards=(), kind=jnp.bfloat16):
    level = block_scale(key, extent, shards, -0.22, 0.18) if shards else 1.0
    drawn = jax.random.normal(key, extent, jnp.float32) * deviation * level
    return jnp.minimum(jnp.maximum(drawn, -limit), limit).astype(kind)


def setup_inputs(seed: int = 0) -> dict:
    key_of = jax.random.split(jax.random.key(seed), 6)
    inputs = normal_values(key_of[0], (2, MB, TOKENS, D), 1.0, 6.0, ((2, 64),))
    cotangent = normal_values(key_of[1], (2, MB, TOKENS, D), 0.005, 0.078125, ((2, 64),))
    norm_gain = jnp.clip(1.0 + 0.18 * jax.random.normal(key_of[2], (LAYERS, D), jnp.float32), 0.099609375, 1.8984375).astype(jnp.bfloat16)
    proj_in = normal_values(key_of[3], (LAYERS, D, R), D ** -0.5, 0.125, ((0, 4), (1, 64)))
    proj_out = normal_values(key_of[4], (LAYERS, R, D), R ** -0.5, 0.375, ((0, 4), (1, 64)))
    return dict(inputs=inputs, cotangent=cotangent, norm_gain=norm_gain, proj_in=proj_in, proj_out=proj_out)


gelu_coeff = 0.7978845608028654
cubic_coeff = 0.044715
norm_eps = 1e-05

def gelu_tanh(values):
    return 0.5 * values * (1.0 + jnp.tanh(gelu_coeff * (values + cubic_coeff * values * values * values)))

def gelu_slope(values):
    inner = jnp.tanh(gelu_coeff * (values + cubic_coeff * values * values * values))
    return 0.5 * (1.0 + inner) + 0.5 * values * (1.0 - inner * inner) * gelu_coeff * (1.0 + 3.0 * cubic_coeff * values * values)

def contract(left, right, left_dim, right_dim):
    return lax.dot_general(left, right, (((left_dim,), (right_dim,)), ((), ())), preferred_element_type=jnp.float32)

def layer_forward(state, gain, weight_in, weight_out):
    as_float = state.astype(jnp.float32)
    centered = as_float - lax.optimization_barrier(jnp.mean(as_float, axis=-1, keepdims=True))
    variance = lax.optimization_barrier(jnp.mean(centered * centered, axis=-1, keepdims=True))
    recip_std = lax.rsqrt(variance + norm_eps)
    hatted = centered * recip_std
    normed = (hatted * gain.astype(jnp.float32)).astype(jnp.bfloat16)
    preact = jnp.dot(normed, weight_in, preferred_element_type=jnp.float32)
    gelu_out = gelu_tanh(preact).astype(jnp.bfloat16)
    result = (as_float + jnp.dot(gelu_out, weight_out, preferred_element_type=jnp.float32)).astype(jnp.bfloat16)
    return (result, (hatted, recip_std, normed, preact, gelu_out))

def layer_backward(state, upstream, gain, weight_in, weight_out):
    result, saved = layer_forward(state, gain, weight_in, weight_out)
    hatted, recip_std, normed, preact, gelu_out = saved
    grad_out = contract(gelu_out, upstream, 0, 0)
    grad_act = contract(upstream, weight_out, 1, 1)
    grad_pre = (grad_act * gelu_slope(preact)).astype(jnp.bfloat16)
    grad_in = contract(normed, grad_pre, 0, 0)
    grad_normed = contract(grad_pre, weight_in, 1, 1)
    grad_gain = lax.optimization_barrier(jnp.sum(grad_normed * hatted, axis=0))
    grad_hat = grad_normed * gain.astype(jnp.float32)
    through = recip_std * (grad_hat - lax.optimization_barrier(jnp.mean(grad_hat, axis=-1, keepdims=True)) - hatted * lax.optimization_barrier(jnp.mean(grad_hat * hatted, axis=-1, keepdims=True)))
    grad_state = (upstream.astype(jnp.float32) + through).astype(jnp.bfloat16)
    return (grad_state, grad_in, grad_out, grad_gain)

def reference(inputs, cotangent, norm_gain, proj_in, proj_out):
    layer_count = proj_in.shape[0]
    acc_in = [jnp.zeros(proj_in.shape[1:], jnp.float32) for _ in range(layer_count)]
    acc_out = [jnp.zeros(proj_out.shape[1:], jnp.float32) for _ in range(layer_count)]
    acc_gain = [jnp.zeros(norm_gain.shape[1:], jnp.float32) for _ in range(layer_count)]
    for direction in range(2):
        for micro_index in range(inputs.shape[1]):
            state = inputs[direction, micro_index]
            stored = []
            for layer_index in range(layer_count):
                stored.append(state)
                state, unused = layer_forward(state, norm_gain[layer_index], proj_in[layer_index], proj_out[layer_index])
            upstream = cotangent[direction, micro_index]
            for layer_index in reversed(range(layer_count)):
                upstream, grad_in, grad_out, grad_gain = layer_backward(stored[layer_index], upstream, norm_gain[layer_index], proj_in[layer_index], proj_out[layer_index])
                acc_in[layer_index] = acc_in[layer_index] + grad_in
                acc_out[layer_index] = acc_out[layer_index] + grad_out
                acc_gain[layer_index] = acc_gain[layer_index] + grad_gain
    return (jnp.stack(acc_gain), jnp.stack(acc_in), jnp.stack(acc_out))
```

```python
import functools
import itertools

import jax
import jax.numpy as jnp
import numpy as np
from jax import lax
from jax.experimental import pallas as pl
from jax.experimental.pallas import tpu as pltpu
from jax.sharding import Mesh
from jax.sharding import PartitionSpec as P


gelu_coeff = 0.7978845608028654
cubic_coeff = 0.044715
norm_eps = 1e-05

AXES = ("zl", "c", "x", "y", "zh")
DIMS = (2, 2, 4, 4, 4)
D = 2048
R = 256
ROWS = 128
CHUNK = 16
F32 = jnp.float32
BF16 = jnp.bfloat16


def flat_perm(move):
    pairs = []
    for src, coords in enumerate(itertools.product(*[range(n) for n in DIMS])):
        dst = [v % n for v, n in zip(move(*coords), DIMS)]
        pairs.append((src, int(np.ravel_multi_index(dst, DIMS))))
    return pairs


def send_first(k):
    return flat_perm(
        lambda zl, c, x, y, zh: (zl, c, x + k, y, zh) if c == 0 else (zl, c, x, y + k, zh)
    )


def send_second(k):
    return flat_perm(
        lambda zl, c, x, y, zh: (zl, c, x, y + k, zh) if c == 0 else (zl, c, x + k, y, zh)
    )


SWAP = flat_perm(lambda zl, c, x, y, zh: (zl, c + 1, x, y, zh))


def shift(value, pairs):
    return lax.ppermute(value, AXES, pairs)


def dot(left, right, left_dim=1, right_dim=0):
    return lax.dot_general(
        left, right, (((left_dim,), (right_dim,)), ((), ())), preferred_element_type=F32
    )


def gelu_parts(v):
    inner = jnp.tanh(gelu_coeff * (v + cubic_coeff * v * v * v))
    return inner, (0.5 * v * (1.0 + inner)).astype(BF16)


def gelu_slope(v, inner):
    return 0.5 * (1.0 + inner) + 0.5 * v * (1.0 - inner * inner) * gelu_coeff * (
        1.0 + 3.0 * cubic_coeff * v * v
    )


def weight_copies(s_ref, pieces, win, wout, sems):
    mx, my, c = s_ref[0], s_ref[1], s_ref[2]
    copies = []
    for o in range(2):
        par = c if o == 0 else 1 - c
        for b in range(4):
            for a in range(4):
                x = (mx + jnp.where(par == 0, a, b)) & 3
                y = (my + jnp.where(par == 0, b, a)) & 3
                xy = x * 4 + y
                src = pieces[o * 4 + b]
                n = len(copies)
                copies.append(
                    pltpu.make_async_copy(
                        src.at[a, pl.ds(0, 8)], win.at[par, pl.ds(xy * 8, 8)], sems.at[n]
                    )
                )
                copies.append(
                    pltpu.make_async_copy(
                        src.at[a, pl.ds(8, 9)], wout.at[par, :, xy], sems.at[n + 1]
                    )
                )
    return copies


def gain_row(wout, par):
    return jnp.concatenate(
        [wout[par, 8, xy, 0:1, 0:128] for xy in range(16)], axis=1
    ).astype(F32)


def over_rows(step):
    def body(i, carry):
        step(pl.ds(pl.multiple_of(i * CHUNK, CHUNK), CHUNK))
        return carry

    lax.fori_loop(0, ROWS // CHUNK, body, 0)


def norm_pass(x_ref, gain, normed, hat, stat):
    def step(rows):
        xf = x_ref[rows, :].astype(F32)
        centered = xf - jnp.mean(xf, axis=-1, keepdims=True)
        variance = jnp.mean(centered * centered, axis=-1, keepdims=True)
        recip_std = lax.rsqrt(variance + norm_eps)
        hatted = centered * recip_std
        hat[rows, :] = hatted
        stat[rows, :] = jnp.broadcast_to(recip_std, (CHUNK, 128))
        normed[rows, :] = (hatted * gain).astype(BF16)

    over_rows(step)


def first_product(normed, win, par):
    return dot(normed[...], win[par].reshape(D, R))


def layer_out(x_ref, act, wout, par, out_ref):
    for k in range(8):
        cols = pl.ds(k * 256, 256)
        out_ref[:, cols] = (
            x_ref[:, cols].astype(F32) + dot(act, wout[par, k].reshape(R, 256))
        ).astype(BF16)


def layer_back(
    s_ref, par, up_ref, normed, hat, stat, preact, win, wout, gain, grads, gnorm, gsum, up_out
):
    mx, my, c = s_ref[0], s_ref[1], s_ref[2]
    slot = jnp.where(c == par, 0, 1)
    inner, act = gelu_parts(preact)
    grad_act = jnp.zeros((ROWS, R), F32)
    for k in range(8):
        grad_act += dot(up_ref[:, pl.ds(k * 256, 256)], wout[par, k].reshape(R, 256), 1, 1)
    grad_pre = (grad_act * gelu_slope(preact, inner)).astype(BF16)
    places = []
    for xy in range(16):
        xr = (xy // 4 - mx) & 3
        yr = (xy % 4 - my) & 3
        places.append(xr * 4 + yr if par == 0 else yr * 4 + xr)
    for k in range(8):
        rows = pl.ds(k * 256, 256)
        gnorm[:, rows] = dot(grad_pre, win[par, pl.ds(k * 16, 16)].reshape(256, R), 1, 1)
    gsum[...] = jnp.zeros((CHUNK, D), F32)

    def step(rows):
        grad_normed = gnorm[rows, :]
        hatted = hat[rows, :]
        product = grad_normed * hatted
        gsum[...] += product
        if up_out is not None:
            grad_hat = grad_normed * gain
            mean_hat = jnp.mean(grad_hat, axis=-1, keepdims=True)
            mean_both = jnp.mean(product * gain, axis=-1, keepdims=True)
            through = stat[rows, 0:1] * (grad_hat - mean_hat - hatted * mean_both)
            up_out[rows, :] = (up_ref[rows, :].astype(F32) + through).astype(BF16)

    act_t = act.T
    for k in range(8):
        block = dot(act_t, up_ref[:, pl.ds(k * 256, 256)]).astype(BF16).reshape(16, 16, 256)
        for xy in range(16):
            grads[slot, places[xy], 8 + k] = block[xy]
    for xy in range(16):
        block = dot(normed[:, pl.ds(xy * 128, 128)].T, grad_pre)
        grads[slot, places[xy], 0:8] = block.astype(BF16).reshape(8, 16, 256)
    over_rows(step)
    total = jnp.sum(gsum[...], axis=0, keepdims=True)
    for xy in range(16):
        part = total[:, xy * 128 : (xy + 1) * 128]
        grads[slot, places[xy], 16] = jnp.broadcast_to(
            jnp.concatenate([part, part], axis=1), (16, 256)
        ).astype(BF16)


def start_all(copies):
    for copy in copies:
        copy.start()


def wait_all(copies):
    for copy in copies:
        copy.wait()


def send_grads(s_ref, grads, keep, send, sems):
    out = [
        pltpu.make_async_copy(grads.at[0], keep, sems.at[0]),
        pltpu.make_async_copy(grads.at[1], send, sems.at[1]),
    ]
    start_all(out)
    wait_all(out)


def kernel_low_forward(s_ref, x0, *refs):
    pieces, (x1, x2, win, wout, normed, hat, stat, sems) = refs[:8], refs[8:]
    copies = weight_copies(s_ref, pieces, win, wout, sems)
    start_all(copies)
    wait_all(copies)
    for par, (src, dst) in enumerate(((x0, x1), (x1, x2))):
        norm_pass(src, gain_row(wout, par), normed, hat, stat)
        unused, act = gelu_parts(first_product(normed, win, par))
        layer_out(src, act, wout, par, dst)


def kernel_high(s_ref, x2, cot, *refs):
    pieces = refs[:8]
    (up2, keep, send, win, wout, normed0, hat0, stat0, normed1, hat1, stat1) = refs[8:19]
    x3, up3, pre0, gnorm, gsum, grads, sems = refs[19:]
    copies = weight_copies(s_ref, pieces, win, wout, sems)
    start_all(copies)
    wait_all(copies)
    gain0, gain1 = gain_row(wout, 0), gain_row(wout, 1)
    norm_pass(x2, gain0, normed0, hat0, stat0)
    pre0[...] = first_product(normed0, win, 0)
    layer_out(x2, gelu_parts(pre0[...])[1], wout, 0, x3)
    norm_pass(x3, gain1, normed1, hat1, stat1)
    pre1 = first_product(normed1, win, 1)
    layer_back(
        s_ref, 1, cot, normed1, hat1, stat1, pre1, win, wout, gain1, grads, gnorm, gsum, up3
    )
    layer_back(
        s_ref, 0, up3, normed0, hat0, stat0, pre0[...], win, wout, gain0, grads, gnorm, gsum, up2
    )
    send_grads(s_ref, grads, keep, send, sems)


def kernel_low_back(s_ref, x0, x1, up2, *refs):
    pieces = refs[:8]
    keep, send, win, wout, normed, hat, stat, up1, gnorm, gsum, grads, sems = refs[8:]
    copies = weight_copies(s_ref, pieces, win, wout, sems)
    start_all(copies)
    wait_all(copies)
    for par, x_ref, up_ref, up_out in ((1, x1, up2, up1), (0, x0, up1, None)):
        gain = gain_row(wout, par)
        norm_pass(x_ref, gain, normed, hat, stat)
        preact = first_product(normed, win, par)
        layer_back(
            s_ref, par, up_ref, normed, hat, stat, preact, win, wout, gain, grads, gnorm, gsum, up_out
        )
    send_grads(s_ref, grads, keep, send, sems)


def vmem(*shape, kind=BF16):
    return pltpu.VMEM(shape, kind)


ACT = jax.ShapeDtypeStruct((ROWS, D), BF16)
GRAD = jax.ShapeDtypeStruct((16, 17, 16, 256), BF16)
ANY = pl.BlockSpec(memory_space=pl.ANY)
WHOLE = pl.BlockSpec((ROWS, D), lambda i, s: (0, 0))
PICK = pl.BlockSpec((None, None, ROWS, D), lambda i, s: (s[3], s[2], 0, 0))
WEIGHTS = [vmem(2, 128, 16, 256), vmem(2, 9, 16, 16, 256)]
NORM = [vmem(ROWS, D), vmem(ROWS, D, kind=F32), vmem(ROWS, 128, kind=F32)]
BACK = [vmem(ROWS, D, kind=F32), vmem(CHUNK, D, kind=F32), vmem(2, 16, 17, 16, 256)]
SEMS = pltpu.SemaphoreType.DMA((64,))


def call(body, in_specs, out_specs, out_shape, scratch, name):
    return pl.pallas_call(
        body,
        grid_spec=pltpu.PrefetchScalarGridSpec(
            num_scalar_prefetch=1,
            grid=(1,),
            in_specs=in_specs + [ANY] * 8,
            out_specs=out_specs,
            scratch_shapes=scratch,
        ),
        out_shape=out_shape,
        compiler_params=pltpu.CompilerParams(
            dimension_semantics=("arbitrary",), vmem_limit_bytes=56 * 1024 * 1024
        ),
        name=name,
    )


def reduce_xy(keep, send):
    other = shift(send, SWAP)
    both = (keep.astype(F32) + other.astype(F32)).astype(BF16).reshape(4, 4, 17, 16, 256)
    got = [shift(both[k], send_first(k)) for k in (1, 3, 2)]
    row = functools.reduce(lambda p, q: p + q.astype(F32), got, both[0].astype(F32)).astype(BF16)
    got = [shift(row[k], send_second(k)) for k in (1, 3, 2)]
    return functools.reduce(lambda p, q: p + q.astype(F32), got, row[0].astype(F32)).astype(BF16)


def per_device(inputs, cotangent, norm_gain, proj_in, proj_out):
    where = [lax.axis_index(n).astype(jnp.int32) for n in ("x", "y", "c", "zl")]
    scalars = jnp.stack(where)
    shard = jnp.concatenate(
        [
            proj_in[0],
            proj_out[0].reshape(4, 8, 256).transpose(1, 0, 2).reshape(32, 256),
            jnp.pad(norm_gain, ((0, 7), (0, 224))),
        ],
        axis=0,
    )
    column = lax.all_to_all(
        jnp.broadcast_to(shard[None], (8, 72, 256)), ("zl", "zh"), 0, 0
    ).reshape(2, 4, 72, 256)
    gain = jnp.pad(column[:, :, 64, :32].reshape(2, 1, 1, 128), ((0, 0), (0, 0), (0, 15), (0, 128)))
    block = jnp.concatenate(
        [
            column[:, :, :32].reshape(2, 8, 16, 256),
            column[:, :, 32:64].reshape(2, 4, 8, 4, 256).transpose(0, 2, 1, 3, 4).reshape(2, 8, 16, 256),
            gain,
        ],
        axis=1,
    )
    near = [block] + [shift(block, send_first(-k)) for k in (1, 2, 3)]
    pairs = []
    for p in range(2):
        row = jnp.stack([v[p] for v in near])
        rows = [row] + [shift(row, send_second(-k)) for k in (1, 2, 3)]
        pairs.append(rows + [shift(v, SWAP) for v in rows])
    x1, x2 = call(
        kernel_low_forward, [PICK], [WHOLE, WHOLE], [ACT, ACT], WEIGHTS + NORM + [SEMS], "low_forward"
    )(scalars, inputs, *pairs[0])
    up2, keep1, send1 = call(
        kernel_high,
        [WHOLE, PICK],
        [WHOLE, ANY, ANY],
        [ACT, GRAD, GRAD],
        WEIGHTS
        + NORM
        + NORM
        + [vmem(ROWS, D), vmem(ROWS, D), vmem(ROWS, R, kind=F32)]
        + BACK
        + [SEMS],
        "high",
    )(scalars, x2, cotangent, *pairs[1])
    keep0, send0 = call(
        kernel_low_back,
        [PICK, WHOLE, WHOLE],
        [ANY, ANY],
        [GRAD, GRAD],
        WEIGHTS + NORM + [vmem(ROWS, D)] + BACK + [SEMS],
        "low_back",
    )(scalars, inputs, x1, up2, *pairs[0])
    high = reduce_xy(keep1, send1)
    low = reduce_xy(keep0, send0)
    grads = jnp.stack([low, high])
    parts = jnp.concatenate(
        [
            grads[:, :8].reshape(2, 4, 32, 256),
            grads[:, 8:16].reshape(2, 8, 4, 4, 256).transpose(0, 2, 1, 3, 4).reshape(2, 4, 32, 256),
            jnp.pad(grads[:, 16, 0, :128].reshape(2, 4, 1, 32), ((0, 0), (0, 0), (0, 7), (0, 224))),
        ],
        axis=2,
    ).reshape(8, 72, 256)
    total = jnp.sum(lax.all_to_all(parts, ("zl", "zh"), 0, 0).astype(F32), axis=0)
    grad_in = total[:32]
    grad_out = total[32:64].reshape(8, 4, 256).transpose(1, 0, 2).reshape(4, 2048)
    return (total[64:65, :32], grad_in[None], grad_out[None])


def solution(mesh):
    fine = Mesh(mesh.devices.reshape(DIMS), AXES)
    zero = ("x", "y", "zh")
    segment = ("zl", "c")
    return jax.shard_map(
        per_device,
        mesh=fine,
        in_specs=(
            P(None, None, zero, None),
            P(None, None, zero, None),
            P(segment, zero),
            P(segment, zero, None),
            P(segment, zero, None),
        ),
        out_specs=(P(segment, zero), P(segment, zero, None), P(segment, zero, None)),
        check_vma=False,
    )
```

```python
import functools
import itertools

import jax
import jax.numpy as jnp
import numpy as np
from jax import lax
from jax.experimental import pallas as pl
from jax.experimental.pallas import tpu as pltpu
from jax.sharding import Mesh
from jax.sharding import PartitionSpec as P


gelu_coeff = 0.7978845608028654
cubic_coeff = 0.044715
norm_eps = 1e-05

AXES = ("zl", "c", "x", "y", "zh")
DIMS = (2, 2, 4, 4, 4)
D = 2048
R = 256
ROWS = 128
CHUNK = 16
F32 = jnp.float32
BF16 = jnp.bfloat16


def flat_perm(move):
    pairs = []
    for src, coords in enumerate(itertools.product(*[range(n) for n in DIMS])):
        dst = [v % n for v, n in zip(move(*coords), DIMS)]
        pairs.append((src, int(np.ravel_multi_index(dst, DIMS))))
    return pairs


def send_first(k):
    return flat_perm(
        lambda zl, c, x, y, zh: (zl, c, x + k, y, zh) if c == 0 else (zl, c, x, y + k, zh)
    )


def send_second(k):
    return flat_perm(
        lambda zl, c, x, y, zh: (zl, c, x, y + k, zh) if c == 0 else (zl, c, x + k, y, zh)
    )


SWAP = flat_perm(lambda zl, c, x, y, zh: (zl, c + 1, x, y, zh))


def shift(value, pairs):
    return lax.ppermute(value, AXES, pairs)


def dot(left, right, left_dim=1, right_dim=0):
    return lax.dot_general(
        left, right, (((left_dim,), (right_dim,)), ((), ())), preferred_element_type=F32
    )


def gelu_parts(v):
    inner = jnp.tanh(gelu_coeff * (v + cubic_coeff * v * v * v))
    return inner, (0.5 * v * (1.0 + inner)).astype(BF16)


def gelu_slope(v, inner):
    return 0.5 * (1.0 + inner) + 0.5 * v * (1.0 - inner * inner) * gelu_coeff * (
        1.0 + 3.0 * cubic_coeff * v * v
    )


def weight_copies(s_ref, pieces, win, wout, sems):
    mx, my, c = s_ref[0], s_ref[1], s_ref[2]
    copies = []
    for o in range(2):
        par = c if o == 0 else 1 - c
        for b in range(4):
            for a in range(4):
                x = (mx + jnp.where(par == 0, a, b)) & 3
                y = (my + jnp.where(par == 0, b, a)) & 3
                xy = x * 4 + y
                src = pieces[o * 4 + b]
                n = (b * 4 + a) * 2
                copies.append(
                    pltpu.make_async_copy(
                        src.at[a, pl.ds(0, 8)], win.at[par, pl.ds(xy * 8, 8)], sems.at[par, n]
                    )
                )
                copies.append(
                    pltpu.make_async_copy(
                        src.at[a, pl.ds(8, 9)], wout.at[par, :, xy], sems.at[par, n + 1]
                    )
                )
    return copies


def wait_layer(pieces, win, wout, sems, par):
    src = pieces[0]
    for n in range(16):
        pltpu.make_async_copy(
            src.at[0, pl.ds(0, 8)], win.at[par, pl.ds(0, 8)], sems.at[par, 2 * n]
        ).wait()
        pltpu.make_async_copy(
            src.at[0, pl.ds(8, 9)], wout.at[par, :, 0], sems.at[par, 2 * n + 1]
        ).wait()


def gain_row(wout, par):
    return jnp.concatenate(
        [wout[par, 8, xy, 0:1, 0:128] for xy in range(16)], axis=1
    ).astype(F32)


def over_rows(step):
    def body(i, carry):
        step(pl.ds(pl.multiple_of(i * CHUNK, CHUNK), CHUNK))
        return carry

    lax.fori_loop(0, ROWS // CHUNK, body, 0, unroll=UNROLL)


def hat_pass(x_at, hat, keep_stat):
    def step(rows):
        xf = x_at(rows).astype(F32)
        mean = jnp.mean(xf, axis=-1, keepdims=True)
        centered = xf - mean
        variance = jnp.mean(centered * centered, axis=-1, keepdims=True)
        recip_std = lax.rsqrt(variance + norm_eps)
        hat[rows, :] = centered * recip_std
        keep_stat(rows, mean, recip_std)

    over_rows(step)


def spread(column):
    return jnp.broadcast_to(column, (CHUNK, 128))


def layer_out(x_at, act, wout, par, out_ref):
    for k in range(8):
        cols = pl.ds(k * 256, 256)
        out_ref[:, cols] = (
            x_at(cols).astype(F32) + dot(act, wout[par, k].reshape(R, 256))
        ).astype(BF16)


def layer_back(up_at, acts, slot, hat, rstd_at, preact, win, wout, par, gain, gnorm, gsum, up_out):
    inner, act = gelu_parts(preact)
    grad_act = jnp.zeros((ROWS, R), F32)
    for k in range(8):
        grad_act += dot(
            up_at(pl.ds(0, ROWS), pl.ds(k * 256, 256)), wout[par, k].reshape(R, 256), 1, 1
        )
    grad_pre = (grad_act * gelu_slope(preact, inner)).astype(BF16)
    acts[slot, 0:ROWS, ACT_AT : ACT_AT + R] = act
    acts[slot, 0:ROWS, PRE_AT : PRE_AT + R] = grad_pre
    for k in range(8):
        gnorm[:, pl.ds(k * 256, 256)] = dot(
            grad_pre, win[par, pl.ds(k * 16, 16)].reshape(256, R), 1, 1
        )
    gsum[...] = jnp.zeros((CHUNK, D), F32)

    def step(rows):
        grad_normed = gnorm[rows, :]
        hatted = hat[rows, :]
        product = grad_normed * hatted
        gsum[...] += product
        up = up_at(rows, pl.ds(0, D))
        acts[slot, rows, UP_AT : UP_AT + D] = up
        if up_out is not None:
            grad_hat = grad_normed * gain
            mean_hat = jnp.mean(grad_hat, axis=-1, keepdims=True)
            mean_both = jnp.mean(product * gain, axis=-1, keepdims=True)
            through = rstd_at(rows) * (grad_hat - mean_hat - hatted * mean_both)
            up_out[rows, :] = (up.astype(F32) + through).astype(BF16)

    over_rows(step)
    acts[slot, ROWS : ROWS + 16, 0:D] = jnp.broadcast_to(
        jnp.sum(gsum[...], axis=0, keepdims=True), (16, D)
    ).astype(BF16)


def start_all(copies):
    for copy in copies:
        copy.start()


def kernel_low_forward(s_ref, xs, *refs):
    pieces, (x1, x2, win, wout, stats, pre, normed, hat, sems) = refs[:8], refs[8:]
    start_all(weight_copies(s_ref, pieces, win, wout, sems))
    c, zl = s_ref[2], s_ref[3]
    for par in range(2):

        def x_at(rows=slice(None), cols=slice(None), par=par):
            return xs[zl, c, rows, cols] if par == 0 else x1[rows, cols]

        def keep_stat(rows, mean, recip_std, par=par):
            stats[par, 0, rows, :] = spread(mean)
            stats[par, 1, rows, :] = spread(recip_std)

        hat_pass(x_at, hat, keep_stat)
        wait_layer(pieces, win, wout, sems, par)
        gain = gain_row(wout, par)

        def step(rows, gain=gain):
            normed[rows, :] = (hat[rows, :] * gain).astype(BF16)

        over_rows(step)
        pre[par] = dot(normed[...], win[par].reshape(D, R))
        act = gelu_parts(pre[par])[1]
        layer_out(lambda cols: x_at(slice(None), cols), act, wout, par, x2 if par else x1)


def kernel_high(s_ref, x2, cots, *refs):
    pieces = refs[:8]
    up2, acts, win, wout, hat0, hat1, rstd, x3, up3, pre0, gnorm, gsum, sems = refs[8:]
    start_all(weight_copies(s_ref, pieces, win, wout, sems))
    c, zl = s_ref[2], s_ref[3]
    gains = []
    for par, (src, hat) in enumerate(((x2, hat0), (x3, hat1))):

        def keep_stat(rows, mean, recip_std, par=par):
            rstd[par, rows, :] = spread(recip_std)

        hat_pass(lambda rows, src=src: src[rows, :], hat, keep_stat)
        wait_layer(pieces, win, wout, sems, par)
        gain = gain_row(wout, par)
        slot = jnp.where(c == par, 0, 1)

        def step(rows, gain=gain, hat=hat, slot=slot):
            acts[slot, rows, 0:D] = (hat[rows, :] * gain).astype(BF16)

        over_rows(step)
        preact = dot(acts[slot, 0:ROWS, 0:D], win[par].reshape(D, R))
        gains.append(gain)
        if par == 0:
            pre0[...] = preact
            layer_out(lambda cols: x2[:, cols], gelu_parts(preact)[1], wout, 0, x3)
    layer_back(
        lambda rows, cols: cots[zl, c, rows, cols],
        acts, jnp.where(c == 1, 0, 1), hat1, lambda rows: rstd[1, rows, 0:1],
        preact, win, wout, 1, gains[1], gnorm, gsum, up3,
    )
    layer_back(
        lambda rows, cols: up3[rows, cols],
        acts, jnp.where(c == 0, 0, 1), hat0, lambda rows: rstd[0, rows, 0:1],
        pre0[...], win, wout, 0, gains[0], gnorm, gsum, up2,
    )


def kernel_low_back(s_ref, xs, x1, up2, win, wout, stats, pre, acts, hat, up1, gnorm, gsum):
    c, zl = s_ref[2], s_ref[3]
    for par, up, up_out in ((1, up2, up1), (0, up1, None)):
        gain = gain_row(wout, par)
        slot = jnp.where(c == par, 0, 1)

        def step(rows, par=par, gain=gain, slot=slot):
            xf = (x1[rows, :] if par else xs[zl, c, rows, :]).astype(F32)
            hatted = (xf - stats[par, 0, rows, 0:1]) * stats[par, 1, rows, 0:1]
            hat[rows, :] = hatted
            acts[slot, rows, 0:D] = (hatted * gain).astype(BF16)

        over_rows(step)
        layer_back(
            lambda rows, cols, up=up: up[rows, cols],
            acts, slot, hat, lambda rows, par=par: stats[par, 1, rows, 0:1],
            pre[par], win, wout, par, gain, gnorm, gsum, up_out,
        )


def kernel_grads(s_ref, acts, got, out):
    mx, my, c = s_ref[0], s_ref[1], s_ref[2]
    places = []
    for xy in range(16):
        xr = (xy // 4 - mx) & 3
        yr = (xy % 4 - my) & 3
        places.append(jnp.where(c == 0, xr * 4 + yr, yr * 4 + xr))

    def both(start, size):
        cols = pl.ds(start, size)
        return jnp.concatenate([acts[0, 0:ROWS, cols], got[0:ROWS, cols]], axis=0)

    grad_pre = both(PRE_AT, R)
    for xy in range(16):
        block = dot(both(xy * 128, 128).T, grad_pre)
        out[places[xy], 0:8] = block.astype(BF16).reshape(8, 16, 256)
    act_t = both(ACT_AT, R).T
    for k in range(8):
        block = dot(act_t, both(UP_AT + k * 256, 256)).astype(BF16).reshape(16, 16, 256)
        for xy in range(16):
            out[places[xy], 8 + k] = block[xy]
    for xy in range(16):
        cols = pl.ds(xy * 128, 128)
        part = acts[0, ROWS : ROWS + 16, cols].astype(F32) + got[ROWS : ROWS + 16, cols].astype(F32)
        out[places[xy], 16] = jnp.concatenate([part, part], axis=1).astype(BF16)


def vmem(*shape, kind=BF16):
    return pltpu.VMEM(shape, kind)


def array(*shape, kind=BF16):
    return jax.ShapeDtypeStruct(shape, kind)


UNROLL = 2
UP_AT, ACT_AT, PRE_AT, WIDE = D, 2 * D, 2 * D + R, 2 * D + 2 * R
ACT = (ROWS, D)
WIN, WOUT = (2, 128, 16, 256), (2, 9, 16, 16, 256)
ACTS = (2, ROWS + 16, WIDE)
HAT = vmem(ROWS, D, kind=F32)
GSUM = vmem(CHUNK, D, kind=F32)
SEMS = pltpu.SemaphoreType.DMA((2, 32))
WHOLE = pl.BlockSpec(memory_space=pltpu.VMEM)


def call(body, scalars, args, out_shape, scratch):
    return pl.pallas_call(
        body,
        in_specs=[pl.BlockSpec(memory_space=pltpu.SMEM)] + [WHOLE] * len(args),
        out_specs=jax.tree.map(lambda s: WHOLE, out_shape),
        scratch_shapes=scratch,
        out_shape=out_shape,
        compiler_params=pltpu.CompilerParams(vmem_limit_bytes=20 * 1024 * 1024),
    )(scalars, *args)


def add_up(first, got):
    return functools.reduce(lambda p, q: p + q.astype(F32), got, first.astype(F32)).astype(BF16)


def scatter_first(grads):
    both = grads.reshape(4, 4, 17, 16, 256)
    got = [shift(both[k], send_first(k)) for k in (2, 1, 3)]
    return both[0], got


def scatter_second(row):
    got = [shift(row[k], send_second(k)) for k in (2, 1, 3)]
    return add_up(row[0], got)


def device_body(inputs, cotangent, norm_gain, proj_in, proj_out):
    where = [lax.axis_index(n).astype(jnp.int32) for n in ("x", "y", "c", "zl")]
    scalars = jnp.stack(where)
    shard = jnp.concatenate(
        [
            proj_in[0],
            proj_out[0].reshape(4, 8, 256).transpose(1, 0, 2).reshape(32, 256),
            jnp.pad(norm_gain, ((0, 7), (0, 224))),
        ],
        axis=0,
    )
    column = lax.all_to_all(
        jnp.broadcast_to(shard[None], (8, 72, 256)), ("zl", "zh"), 0, 0
    ).reshape(2, 4, 72, 256)
    gain = jnp.pad(column[:, :, 64, :32].reshape(2, 1, 1, 128), ((0, 0), (0, 0), (0, 15), (0, 128)))
    block = jnp.concatenate(
        [
            column[:, :, :32].reshape(2, 8, 16, 256),
            column[:, :, 32:64].reshape(2, 4, 8, 4, 256).transpose(0, 2, 1, 3, 4).reshape(2, 8, 16, 256),
            gain,
        ],
        axis=1,
    )
    near = [block] + [shift(block, send_first(-k)) for k in (1, 2, 3)]
    pairs = []
    for p in range(2):
        row = jnp.stack([v[p] for v in near])
        rows = [row] + [shift(row, send_second(-k)) for k in (1, 2, 3)]
        pairs.append(rows + [shift(v, SWAP) for v in rows])
    x1, x2, win, wout, stats, pre = call(
        kernel_low_forward,
        scalars,
        [inputs, *pairs[0]],
        [
            array(*ACT), array(*ACT), array(*WIN), array(*WOUT),
            array(2, 2, ROWS, 128, kind=F32), array(2, ROWS, R, kind=F32),
        ],
        [vmem(*ACT), HAT, SEMS],
    )
    up2, acts1 = call(
        kernel_high,
        scalars,
        [x2, cotangent, *pairs[1]],
        [array(*ACT), array(*ACTS)],
        [
            vmem(*WIN), vmem(*WOUT), HAT, HAT, vmem(2, ROWS, 128, kind=F32),
            vmem(*ACT), vmem(*ACT), vmem(ROWS, R, kind=F32), HAT, GSUM, SEMS,
        ],
    )
    got1 = shift(acts1[1], SWAP)
    acts0 = call(
        kernel_low_back,
        scalars,
        [inputs, x1, up2, win, wout, stats, pre],
        array(*ACTS),
        [HAT, vmem(*ACT), HAT, GSUM],
    )
    got0 = shift(acts0[1], SWAP)
    grad = array(16, 17, 16, 256)
    own1, first1 = scatter_first(call(kernel_grads, scalars, [acts1, got1], grad, []))
    own0, first0 = scatter_first(call(kernel_grads, scalars, [acts0, got0], grad, []))
    high = scatter_second(add_up(own1, first1))
    low = scatter_second(add_up(own0, first0))
    grads = jnp.stack([low, high])
    parts = jnp.concatenate(
        [
            grads[:, :8].reshape(2, 4, 32, 256),
            grads[:, 8:16].reshape(2, 8, 4, 4, 256).transpose(0, 2, 1, 3, 4).reshape(2, 4, 32, 256),
            jnp.pad(grads[:, 16, 0, :128].reshape(2, 4, 1, 32), ((0, 0), (0, 0), (0, 7), (0, 224))),
        ],
        axis=2,
    ).reshape(8, 72, 256)
    total = jnp.sum(lax.all_to_all(parts, ("zl", "zh"), 0, 0).astype(F32), axis=0)
    grad_in = total[:32]
    grad_out = total[32:64].reshape(8, 4, 256).transpose(1, 0, 2).reshape(4, 2048)
    return (total[64:65, :32], grad_in[None], grad_out[None])


def solution(mesh):
    fine = Mesh(mesh.devices.reshape(DIMS), AXES)
    zero = ("x", "y", "zh")
    segment = ("zl", "c")
    return jax.shard_map(
        device_body,
        mesh=fine,
        in_specs=(
            P(None, None, zero, None),
            P(None, None, zero, None),
            P(segment, zero),
            P(segment, zero, None),
            P(segment, zero, None),
        ),
        out_specs=(P(segment, zero), P(segment, zero, None), P(segment, zero, None)),
        check_vma=False,
    )
```

```python
import functools
import itertools

import jax
import jax.numpy as jnp
import numpy as np
from jax import lax
from jax.experimental import pallas as pl
from jax.experimental.pallas import tpu as pltpu
from jax.sharding import Mesh
from jax.sharding import PartitionSpec as P


gelu_coeff = 0.7978845608028654
cubic_coeff = 0.044715
norm_eps = 1e-05

AXES = ("zl", "c", "x", "y", "zh")
DIMS = (2, 2, 4, 4, 4)
D = 2048
R = 256
ROWS = 128
CHUNK = 16
F32 = jnp.float32
BF16 = jnp.bfloat16


def flat_perm(move):
    pairs = []
    for src, coords in enumerate(itertools.product(*[range(n) for n in DIMS])):
        dst = [v % n for v, n in zip(move(*coords), DIMS)]
        pairs.append((src, int(np.ravel_multi_index(dst, DIMS))))
    return pairs


def send_first(k):
    return flat_perm(
        lambda zl, c, x, y, zh: (zl, c, x + k, y, zh) if c == 0 else (zl, c, x, y + k, zh)
    )


def send_second(k):
    return flat_perm(
        lambda zl, c, x, y, zh: (zl, c, x, y + k, zh) if c == 0 else (zl, c, x + k, y, zh)
    )


SWAP = flat_perm(lambda zl, c, x, y, zh: (zl, c + 1, x, y, zh))


def shift(value, pairs):
    return lax.ppermute(value, AXES, pairs)


def dot(left, right, left_dim=1, right_dim=0):
    return lax.dot_general(
        left, right, (((left_dim,), (right_dim,)), ((), ())), preferred_element_type=F32
    )


def gelu_parts(v):
    inner = jnp.tanh(gelu_coeff * (v + cubic_coeff * v * v * v))
    return inner, (0.5 * v * (1.0 + inner)).astype(BF16)


def gelu_slope(v, inner):
    return 0.5 * (1.0 + inner) + 0.5 * v * (1.0 - inner * inner) * gelu_coeff * (
        1.0 + 3.0 * cubic_coeff * v * v
    )


def place_weights(s_ref, pieces, win, wout):
    mx, my, c = s_ref[0], s_ref[1], s_ref[2]
    for o in range(2):
        par = c if o == 0 else 1 - c
        for b in range(4):
            for a in range(4):
                x = (mx + jnp.where(par == 0, a, b)) & 3
                y = (my + jnp.where(par == 0, b, a)) & 3
                xy = x * 4 + y
                src = pieces[o * 4 + b]
                win[par, pl.ds(xy * 8, 8)] = src[a, 0:8]
                for k in range(9):
                    wout[par, k, xy] = src[a, 8 + k]


def gain_row(wout, par):
    return jnp.concatenate(
        [wout[par, 8, xy, 0:1, 0:128] for xy in range(16)], axis=1
    ).astype(F32)


def over_rows(step):
    def body(i, carry):
        step(pl.ds(pl.multiple_of(i * CHUNK, CHUNK), CHUNK))
        return carry

    lax.fori_loop(0, ROWS // CHUNK, body, 0, unroll=UNROLL)


def hat_pass(x_at, hat, keep_stat):
    def step(rows):
        xf = x_at(rows).astype(F32)
        mean = jnp.mean(xf, axis=-1, keepdims=True)
        centered = xf - mean
        variance = jnp.mean(centered * centered, axis=-1, keepdims=True)
        recip_std = lax.rsqrt(variance + norm_eps)
        hat[rows, :] = centered * recip_std
        keep_stat(rows, mean, recip_std)

    over_rows(step)


def spread(column):
    return jnp.broadcast_to(column, (CHUNK, 128))


def layer_out(x_at, act, wout, par, out_ref):
    for k in range(8):
        cols = pl.ds(k * 256, 256)
        out_ref[:, cols] = (
            x_at(cols).astype(F32) + dot(act, wout[par, k].reshape(R, 256))
        ).astype(BF16)


def layer_back(up_at, acts, slot, hat, rstd_at, preact, win, wout, par, gain, gnorm, gsum, up_out):
    inner, act = gelu_parts(preact)
    grad_act = jnp.zeros((ROWS, R), F32)
    for k in range(8):
        grad_act += dot(
            up_at(pl.ds(0, ROWS), pl.ds(k * 256, 256)), wout[par, k].reshape(R, 256), 1, 1
        )
    grad_pre = (grad_act * gelu_slope(preact, inner)).astype(BF16)
    acts[slot, 0:ROWS, ACT_AT : ACT_AT + R] = act
    acts[slot, 0:ROWS, PRE_AT : PRE_AT + R] = grad_pre
    for k in range(8):
        gnorm[:, pl.ds(k * 256, 256)] = dot(
            grad_pre, win[par, pl.ds(k * 16, 16)].reshape(256, R), 1, 1
        )
    gsum[...] = jnp.zeros((CHUNK, D), F32)

    def step(rows):
        grad_normed = gnorm[rows, :]
        hatted = hat[rows, :]
        product = grad_normed * hatted
        gsum[...] += product
        up = up_at(rows, pl.ds(0, D))
        acts[slot, rows, UP_AT : UP_AT + D] = up
        if up_out is not None:
            grad_hat = grad_normed * gain
            mean_hat = jnp.mean(grad_hat, axis=-1, keepdims=True)
            mean_both = jnp.mean(product * gain, axis=-1, keepdims=True)
            through = rstd_at(rows) * (grad_hat - mean_hat - hatted * mean_both)
            up_out[rows, :] = (up.astype(F32) + through).astype(BF16)

    over_rows(step)
    acts[slot, ROWS : ROWS + 16, 0:D] = jnp.broadcast_to(
        jnp.sum(gsum[...], axis=0, keepdims=True), (16, D)
    ).astype(BF16)


def kernel_low_forward(s_ref, xs, *refs):
    pieces, (x1, x2, win, wout, stats, pre, normed, hat) = refs[:8], refs[8:]
    place_weights(s_ref, pieces, win, wout)
    c, zl = s_ref[2], s_ref[3]
    for par in range(2):

        def x_at(rows=slice(None), cols=slice(None), par=par):
            return xs[zl, c, rows, cols] if par == 0 else x1[rows, cols]

        def keep_stat(rows, mean, recip_std, par=par):
            stats[par, 0, rows, :] = spread(mean)
            stats[par, 1, rows, :] = spread(recip_std)

        hat_pass(x_at, hat, keep_stat)
        gain = gain_row(wout, par)

        def step(rows, gain=gain):
            normed[rows, :] = (hat[rows, :] * gain).astype(BF16)

        over_rows(step)
        pre[par] = dot(normed[...], win[par].reshape(D, R))
        act = gelu_parts(pre[par])[1]
        layer_out(lambda cols: x_at(slice(None), cols), act, wout, par, x2 if par else x1)


def kernel_high(s_ref, x2, cots, *refs):
    pieces = refs[:8]
    up2, acts, win, wout, hat0, hat1, rstd, x3, up3, pre0, gnorm, gsum = refs[8:]
    place_weights(s_ref, pieces, win, wout)
    c, zl = s_ref[2], s_ref[3]
    gains = []
    for par, (src, hat) in enumerate(((x2, hat0), (x3, hat1))):

        def keep_stat(rows, mean, recip_std, par=par):
            rstd[par, rows, :] = spread(recip_std)

        hat_pass(lambda rows, src=src: src[rows, :], hat, keep_stat)
        gain = gain_row(wout, par)
        slot = jnp.where(c == par, 0, 1)

        def step(rows, gain=gain, hat=hat, slot=slot):
            acts[slot, rows, 0:D] = (hat[rows, :] * gain).astype(BF16)

        over_rows(step)
        preact = dot(acts[slot, 0:ROWS, 0:D], win[par].reshape(D, R))
        gains.append(gain)
        if par == 0:
            pre0[...] = preact
            layer_out(lambda cols: x2[:, cols], gelu_parts(preact)[1], wout, 0, x3)
    layer_back(
        lambda rows, cols: cots[zl, c, rows, cols],
        acts, jnp.where(c == 1, 0, 1), hat1, lambda rows: rstd[1, rows, 0:1],
        preact, win, wout, 1, gains[1], gnorm, gsum, up3,
    )
    layer_back(
        lambda rows, cols: up3[rows, cols],
        acts, jnp.where(c == 0, 0, 1), hat0, lambda rows: rstd[0, rows, 0:1],
        pre0[...], win, wout, 0, gains[0], gnorm, gsum, up2,
    )


def kernel_low_back(s_ref, xs, x1, up2, win, wout, stats, pre, acts, hat, up1, gnorm, gsum):
    c, zl = s_ref[2], s_ref[3]
    for par, up, up_out in ((1, up2, up1), (0, up1, None)):
        gain = gain_row(wout, par)
        slot = jnp.where(c == par, 0, 1)

        def step(rows, par=par, gain=gain, slot=slot):
            xf = (x1[rows, :] if par else xs[zl, c, rows, :]).astype(F32)
            hatted = (xf - stats[par, 0, rows, 0:1]) * stats[par, 1, rows, 0:1]
            hat[rows, :] = hatted
            acts[slot, rows, 0:D] = (hatted * gain).astype(BF16)

        over_rows(step)
        layer_back(
            lambda rows, cols, up=up: up[rows, cols],
            acts, slot, hat, lambda rows, par=par: stats[par, 1, rows, 0:1],
            pre[par], win, wout, par, gain, gnorm, gsum, up_out,
        )


def kernel_grads(s_ref, acts, got, out):
    mx, my, c = s_ref[0], s_ref[1], s_ref[2]
    places = []
    for xy in range(16):
        xr = (xy // 4 - mx) & 3
        yr = (xy % 4 - my) & 3
        places.append(jnp.where(c == 0, xr * 4 + yr, yr * 4 + xr))

    def both(start, size):
        cols = pl.ds(start, size)
        return jnp.concatenate([acts[0, 0:ROWS, cols], got[0:ROWS, cols]], axis=0)

    grad_pre = both(PRE_AT, R)
    for xy in range(16):
        block = dot(both(xy * 128, 128).T, grad_pre)
        out[places[xy], 0:8] = block.astype(BF16).reshape(8, 16, 256)
    act_t = both(ACT_AT, R).T
    for k in range(8):
        block = dot(act_t, both(UP_AT + k * 256, 256)).astype(BF16).reshape(16, 16, 256)
        for xy in range(16):
            out[places[xy], 8 + k] = block[xy]
    for xy in range(16):
        cols = pl.ds(xy * 128, 128)
        part = acts[0, ROWS : ROWS + 16, cols].astype(F32) + got[ROWS : ROWS + 16, cols].astype(F32)
        out[places[xy], 16] = jnp.concatenate([part, part], axis=1).astype(BF16)


def vmem(*shape, kind=BF16):
    return pltpu.VMEM(shape, kind)


def array(*shape, kind=BF16):
    return jax.ShapeDtypeStruct(shape, kind)


UNROLL = 8
UP_AT, ACT_AT, PRE_AT, WIDE = D, 2 * D, 2 * D + R, 2 * D + 2 * R
ACT = (ROWS, D)
WIN, WOUT = (2, 128, 16, 256), (2, 9, 16, 16, 256)
ACTS = (2, ROWS + 16, WIDE)
HAT = vmem(ROWS, D, kind=F32)
GSUM = vmem(CHUNK, D, kind=F32)
LOW_SCRATCH = [vmem(*ACT), HAT]
HIGH_SCRATCH = [
    vmem(*WIN), vmem(*WOUT), HAT, HAT, vmem(2, ROWS, 128, kind=F32),
    vmem(*ACT), vmem(*ACT), vmem(ROWS, R, kind=F32), HAT, GSUM,
]
BACK_SCRATCH = [HAT, vmem(*ACT), HAT, GSUM]
WHOLE = pl.BlockSpec(memory_space=pltpu.VMEM)


def call(body, scalars, args, out_shape, scratch):
    return pl.pallas_call(
        body,
        in_specs=[pl.BlockSpec(memory_space=pltpu.SMEM)] + [WHOLE] * len(args),
        out_specs=jax.tree.map(lambda s: WHOLE, out_shape),
        scratch_shapes=scratch,
        out_shape=out_shape,
        compiler_params=pltpu.CompilerParams(vmem_limit_bytes=20 * 1024 * 1024),
    )(scalars, *args)


def add_up(first, got):
    return functools.reduce(lambda p, q: p + q.astype(F32), got, first.astype(F32)).astype(BF16)


def scatter_first(grads):
    both = grads.reshape(4, 4, 17, 16, 256)
    got = [shift(both[k], send_first(k)) for k in (2, 1, 3)]
    return both[0], got


def scatter_second(row):
    got = [shift(row[k], send_second(k)) for k in (2, 1, 3)]
    return add_up(row[0], got)


def device_body(inputs, cotangent, norm_gain, proj_in, proj_out):
    where = [lax.axis_index(n).astype(jnp.int32) for n in ("x", "y", "c", "zl")]
    scalars = jnp.stack(where)
    shard = jnp.concatenate(
        [
            proj_in[0],
            proj_out[0].reshape(4, 8, 256).transpose(1, 0, 2).reshape(32, 256),
            jnp.pad(norm_gain, ((0, 7), (0, 224))),
        ],
        axis=0,
    )
    column = lax.all_to_all(
        jnp.broadcast_to(shard[None], (8, 72, 256)), ("zl", "zh"), 0, 0
    ).reshape(2, 4, 72, 256)
    gain = jnp.pad(column[:, :, 64, :32].reshape(2, 1, 1, 128), ((0, 0), (0, 0), (0, 15), (0, 128)))
    block = jnp.concatenate(
        [
            column[:, :, :32].reshape(2, 8, 16, 256),
            column[:, :, 32:64].reshape(2, 4, 8, 4, 256).transpose(0, 2, 1, 3, 4).reshape(2, 8, 16, 256),
            gain,
        ],
        axis=1,
    )
    near = []
    for p in range(2):
        near.append([block[p]] + [shift(block[p], send_first(-k)) for k in (1, 2, 3)])
    pairs = []
    for p in range(2):
        row = jnp.stack(near[p])
        rows = [row] + [shift(row, send_second(-k)) for k in (1, 2, 3)]
        pairs.append(rows + [shift(v, SWAP) for v in rows])
    x1, x2, win, wout, stats, pre = call(
        kernel_low_forward,
        scalars,
        [inputs, *pairs[0]],
        [
            array(*ACT), array(*ACT), array(*WIN), array(*WOUT),
            array(2, 2, ROWS, 128, kind=F32), array(2, ROWS, R, kind=F32),
        ],
        LOW_SCRATCH,
    )
    up2, acts1 = call(
        kernel_high, scalars, [x2, cotangent, *pairs[1]], [array(*ACT), array(*ACTS)], HIGH_SCRATCH
    )
    got1 = shift(acts1[1], SWAP)
    acts0 = call(
        kernel_low_back,
        scalars,
        [inputs, x1, up2, win, wout, stats, pre],
        array(*ACTS),
        BACK_SCRATCH,
    )
    got0 = shift(acts0[1], SWAP)
    grad = array(16, 17, 16, 256)
    own1, first1 = scatter_first(call(kernel_grads, scalars, [acts1, got1], grad, []))
    own0, first0 = scatter_first(call(kernel_grads, scalars, [acts0, got0], grad, []))
    high = scatter_second(add_up(own1, first1))
    low = scatter_second(add_up(own0, first0))
    grads = jnp.stack([low, high])
    parts = jnp.concatenate(
        [
            grads[:, :8].reshape(2, 4, 32, 256),
            grads[:, 8:16].reshape(2, 8, 4, 4, 256).transpose(0, 2, 1, 3, 4).reshape(2, 4, 32, 256),
            jnp.pad(grads[:, 16, 0, :128].reshape(2, 4, 1, 32), ((0, 0), (0, 0), (0, 7), (0, 224))),
        ],
        axis=2,
    ).reshape(8, 72, 256)
    total = jnp.sum(lax.all_to_all(parts, ("zl", "zh"), 0, 0).astype(F32), axis=0)
    grad_in = total[:32]
    grad_out = total[32:64].reshape(8, 4, 256).transpose(1, 0, 2).reshape(4, 2048)
    return (total[64:65, :32], grad_in[None], grad_out[None])


def solution(mesh):
    fine = Mesh(mesh.devices.reshape(DIMS), AXES)
    zero = ("x", "y", "zh")
    segment = ("zl", "c")
    return jax.shard_map(
        device_body,
        mesh=fine,
        in_specs=(
            P(None, None, zero, None),
            P(None, None, zero, None),
            P(segment, zero),
            P(segment, zero, None),
            P(segment, zero, None),
        ),
        out_specs=(P(segment, zero), P(segment, zero, None), P(segment, zero, None)),
        check_vma=False,
    )
```

```python
import functools
import itertools

import jax
import jax.numpy as jnp
import numpy as np
from jax import lax
from jax.experimental import pallas as pl
from jax.experimental.pallas import tpu as pltpu
from jax.sharding import Mesh
from jax.sharding import PartitionSpec as P


gelu_coeff = 0.7978845608028654
cubic_coeff = 0.044715
norm_eps = 1e-05

AXES = ("zl", "c", "x", "y", "zh")
DIMS = (2, 2, 4, 4, 4)
D = 2048
R = 256
ROWS = 128
CHUNK = 16
F32 = jnp.float32
BF16 = jnp.bfloat16


def flat_perm(move):
    pairs = []
    for src, coords in enumerate(itertools.product(*[range(n) for n in DIMS])):
        dst = [v % n for v, n in zip(move(*coords), DIMS)]
        pairs.append((src, int(np.ravel_multi_index(dst, DIMS))))
    return pairs


def send_first(k):
    return flat_perm(
        lambda zl, c, x, y, zh: (zl, c, x + k, y, zh) if c == 0 else (zl, c, x, y + k, zh)
    )


def send_second(k):
    return flat_perm(
        lambda zl, c, x, y, zh: (zl, c, x, y + k, zh) if c == 0 else (zl, c, x + k, y, zh)
    )


SWAP = flat_perm(lambda zl, c, x, y, zh: (zl, c + 1, x, y, zh))


def shift(value, pairs):
    return lax.ppermute(value, AXES, pairs)


def dot(left, right, left_dim=1, right_dim=0):
    return lax.dot_general(
        left, right, (((left_dim,), (right_dim,)), ((), ())), preferred_element_type=F32
    )


def gelu_parts(v):
    inner = jnp.tanh(gelu_coeff * (v + cubic_coeff * v * v * v))
    return inner, (0.5 * v * (1.0 + inner)).astype(BF16)


def gelu_slope(v, inner):
    return 0.5 * (1.0 + inner) + 0.5 * v * (1.0 - inner * inner) * gelu_coeff * (
        1.0 + 3.0 * cubic_coeff * v * v
    )


def place_weights(s_ref, pieces, win, wout):
    mx, my, c = s_ref[0], s_ref[1], s_ref[2]
    for o in range(2):
        par = c if o == 0 else 1 - c
        for src, (b, first, count) in zip(pieces[o * PIECES : (o + 1) * PIECES], SPANS):

            def place(i, carry, par=par, src=src, b=b, first=first):
                a = first + i
                x = (mx + jnp.where(par == 0, a, b)) & 3
                y = (my + jnp.where(par == 0, b, a)) & 3
                xy = x * 4 + y
                win[par, pl.ds(xy * 8, 8)] = src[i, 0:8]
                for k in range(9):
                    wout[par, k, xy] = src[i, 8 + k]
                return carry

            lax.fori_loop(0, count, place, 0)


def gain_row(wout, par):
    return jnp.concatenate(
        [wout[par, 8, xy, 0:1, 0:128] for xy in range(16)], axis=1
    ).astype(F32)


def over_rows(step):
    def body(i, carry):
        step(pl.ds(pl.multiple_of(i * CHUNK, CHUNK), CHUNK))
        return carry

    lax.fori_loop(0, ROWS // CHUNK, body, 0, unroll=UNROLL)


def hat_pass(x_at, hat, keep_stat):
    def step(rows):
        xf = x_at(rows).astype(F32)
        mean = jnp.mean(xf, axis=-1, keepdims=True)
        centered = xf - mean
        variance = jnp.mean(centered * centered, axis=-1, keepdims=True)
        recip_std = lax.rsqrt(variance + norm_eps)
        hat[rows, :] = centered * recip_std
        keep_stat(rows, mean, recip_std)

    over_rows(step)


def spread(column):
    return jnp.broadcast_to(column, (CHUNK, 128))


def layer_out(x_at, act, wout, par, out_ref):
    for k in range(8):
        cols = pl.ds(k * 256, 256)
        out_ref[:, cols] = (
            x_at(cols).astype(F32) + dot(act, wout[par, k].reshape(R, 256))
        ).astype(BF16)


def layer_back(up_at, acts, slot, hat, rstd_at, preact, win, wout, par, gain, gnorm, gsum, up_out):
    inner, act = gelu_parts(preact)
    grad_act = jnp.zeros((ROWS, R), F32)
    for k in range(8):
        grad_act += dot(
            up_at(pl.ds(0, ROWS), pl.ds(k * 256, 256)), wout[par, k].reshape(R, 256), 1, 1
        )
    grad_pre = (grad_act * gelu_slope(preact, inner)).astype(BF16)
    acts[slot, 0:ROWS, ACT_AT : ACT_AT + R] = act
    acts[slot, 0:ROWS, PRE_AT : PRE_AT + R] = grad_pre
    for k in range(8):
        gnorm[:, pl.ds(k * 256, 256)] = dot(
            grad_pre, win[par, pl.ds(k * 16, 16)].reshape(256, R), 1, 1
        )
    gsum[...] = jnp.zeros((CHUNK, D), F32)

    def step(rows):
        grad_normed = gnorm[rows, :]
        hatted = hat[rows, :]
        product = grad_normed * hatted
        gsum[...] += product
        up = up_at(rows, pl.ds(0, D))
        acts[slot, rows, UP_AT : UP_AT + D] = up
        if up_out is not None:
            grad_hat = grad_normed * gain
            mean_hat = jnp.mean(grad_hat, axis=-1, keepdims=True)
            mean_both = jnp.mean(product * gain, axis=-1, keepdims=True)
            through = rstd_at(rows) * (grad_hat - mean_hat - hatted * mean_both)
            up_out[rows, :] = (up.astype(F32) + through).astype(BF16)

    over_rows(step)
    acts[slot, ROWS : ROWS + 16, 0:D] = jnp.broadcast_to(
        jnp.sum(gsum[...], axis=0, keepdims=True), (16, D)
    ).astype(BF16)


def kernel_low_forward(s_ref, xs, *refs):
    pieces, (x1, x2, win, wout, stats, pre, normed, hat) = refs[: 2 * PIECES], refs[2 * PIECES :]
    place_weights(s_ref, pieces, win, wout)
    c, zl = s_ref[2], s_ref[3]
    for par in range(2):

        def x_at(rows=slice(None), cols=slice(None), par=par):
            return xs[zl, c, rows, cols] if par == 0 else x1[rows, cols]

        def keep_stat(rows, mean, recip_std, par=par):
            stats[par, 0, rows, :] = spread(mean)
            stats[par, 1, rows, :] = spread(recip_std)

        hat_pass(x_at, hat, keep_stat)
        gain = gain_row(wout, par)

        def step(rows, gain=gain):
            normed[rows, :] = (hat[rows, :] * gain).astype(BF16)

        over_rows(step)
        pre[par] = dot(normed[...], win[par].reshape(D, R))
        act = gelu_parts(pre[par])[1]
        layer_out(lambda cols: x_at(slice(None), cols), act, wout, par, x2 if par else x1)


def kernel_high(s_ref, x2, cots, *refs):
    pieces = refs[: 2 * PIECES]
    up2, acts, win, wout, hat0, hat1, rstd, x3, up3, pre0, gnorm, gsum = refs[2 * PIECES :]
    place_weights(s_ref, pieces, win, wout)
    c, zl = s_ref[2], s_ref[3]
    gains = []
    for par, (src, hat) in enumerate(((x2, hat0), (x3, hat1))):

        def keep_stat(rows, mean, recip_std, par=par):
            rstd[par, rows, :] = spread(recip_std)

        hat_pass(lambda rows, src=src: src[rows, :], hat, keep_stat)
        gain = gain_row(wout, par)
        slot = jnp.where(c == par, 0, 1)

        def step(rows, gain=gain, hat=hat, slot=slot):
            acts[slot, rows, 0:D] = (hat[rows, :] * gain).astype(BF16)

        over_rows(step)
        preact = dot(acts[slot, 0:ROWS, 0:D], win[par].reshape(D, R))
        gains.append(gain)
        if par == 0:
            pre0[...] = preact
            layer_out(lambda cols: x2[:, cols], gelu_parts(preact)[1], wout, 0, x3)
    layer_back(
        lambda rows, cols: cots[zl, c, rows, cols],
        acts, jnp.where(c == 1, 0, 1), hat1, lambda rows: rstd[1, rows, 0:1],
        preact, win, wout, 1, gains[1], gnorm, gsum, up3,
    )
    layer_back(
        lambda rows, cols: up3[rows, cols],
        acts, jnp.where(c == 0, 0, 1), hat0, lambda rows: rstd[0, rows, 0:1],
        pre0[...], win, wout, 0, gains[0], gnorm, gsum, up2,
    )


def kernel_low_back(s_ref, xs, x1, up2, win, wout, stats, pre, acts, hat, up1, gnorm, gsum):
    c, zl = s_ref[2], s_ref[3]
    for par, up, up_out in ((1, up2, up1), (0, up1, None)):
        gain = gain_row(wout, par)
        slot = jnp.where(c == par, 0, 1)

        def step(rows, par=par, gain=gain, slot=slot):
            xf = (x1[rows, :] if par else xs[zl, c, rows, :]).astype(F32)
            hatted = (xf - stats[par, 0, rows, 0:1]) * stats[par, 1, rows, 0:1]
            hat[rows, :] = hatted
            acts[slot, rows, 0:D] = (hatted * gain).astype(BF16)

        over_rows(step)
        layer_back(
            lambda rows, cols, up=up: up[rows, cols],
            acts, slot, hat, lambda rows, par=par: stats[par, 1, rows, 0:1],
            pre[par], win, wout, par, gain, gnorm, gsum, up_out,
        )


def kernel_grads(s_ref, acts, got, out, up, down):
    mx, my, c = s_ref[0], s_ref[1], s_ref[2]
    places = []
    for xy in range(16):
        xr = (xy // 4 - mx) & 3
        yr = (xy % 4 - my) & 3
        places.append(jnp.where(c == 0, xr * 4 + yr, yr * 4 + xr))

    def both(start, size):
        cols = pl.ds(start, size)
        return jnp.concatenate([acts[0, 0:ROWS, cols], got[0:ROWS, cols]], axis=0)

    grad_pre = both(PRE_AT, R)
    for xy in range(16):
        block = dot(both(xy * 128, 128).T, grad_pre)
        out[places[xy], 0:8] = block.astype(BF16).reshape(8, 16, 256)
    act_t = both(ACT_AT, R).T
    for k in range(8):
        block = dot(act_t, both(UP_AT + k * 256, 256)).astype(BF16).reshape(16, 16, 256)
        for xy in range(16):
            out[places[xy], 8 + k] = block[xy]
    for xy in range(16):
        cols = pl.ds(xy * 128, 128)
        part = acts[0, ROWS : ROWS + 16, cols].astype(F32) + got[ROWS : ROWS + 16, cols].astype(F32)
        out[places[xy], 16] = jnp.concatenate([part, part], axis=1).astype(BF16)


    up[...] = out[8:10]
    down[...] = out[10:12]


def over_groups(step):
    def body(g, carry):
        step(g)
        return carry

    lax.fori_loop(0, 17, body, 0)


def kernel_sides(s_ref, grads, up, down, after, before):
    def step(g):
        for i in range(2):
            after[i, g] = (grads[4 + i, g].astype(F32) + up[i, g].astype(F32)).astype(BF16)
            after[2 + i, g] = grads[6 + i, g]
            before[i, g] = grads[12 + i, g]
            before[2 + i, g] = (grads[14 + i, g].astype(F32) + down[i, g].astype(F32)).astype(BF16)

    over_groups(step)


def kernel_sum(s_ref, low, low_a, low_b, high, high_a, high_b, *pieces):
    def step(g):
        for p, (own, a, b) in enumerate(((low, low_a, low_b), (high, high_a, high_b))):
            for k in range(4):
                pieces[k][p, g] = (
                    own[k, g].astype(F32) + a[k, g].astype(F32) + b[k, g].astype(F32)
                ).astype(BF16)

    over_groups(step)


def vmem(*shape, kind=BF16):
    return pltpu.VMEM(shape, kind)


def array(*shape, kind=BF16):
    return jax.ShapeDtypeStruct(shape, kind)


UNROLL = 8
SPANS = ((0, 0, 4), (1, 0, 4), (3, 0, 4), (2, 0, 2), (2, 2, 2))
PIECES = len(SPANS)
UP_AT, ACT_AT, PRE_AT, WIDE = D, 2 * D, 2 * D + R, 2 * D + 2 * R
ACT = (ROWS, D)
WIN, WOUT = (2, 128, 16, 256), (2, 9, 16, 16, 256)
ACTS = (2, ROWS + 16, WIDE)
HAT = vmem(ROWS, D, kind=F32)
GSUM = vmem(CHUNK, D, kind=F32)
LOW_SCRATCH = [vmem(*ACT), HAT]
HIGH_SCRATCH = [
    vmem(*WIN), vmem(*WOUT), HAT, HAT, vmem(2, ROWS, 128, kind=F32),
    vmem(*ACT), vmem(*ACT), vmem(ROWS, R, kind=F32), HAT, GSUM,
]
BACK_SCRATCH = [HAT, vmem(*ACT), HAT, GSUM]
WHOLE = pl.BlockSpec(memory_space=pltpu.VMEM)


def call(body, scalars, args, out_shape, scratch):
    return pl.pallas_call(
        body,
        in_specs=[pl.BlockSpec(memory_space=pltpu.SMEM)] + [WHOLE] * len(args),
        out_specs=jax.tree.map(lambda s: WHOLE, out_shape),
        scratch_shapes=scratch,
        out_shape=out_shape,
        compiler_params=pltpu.CompilerParams(vmem_limit_bytes=20 * 1024 * 1024),
    )(scalars, *args)


def add_up(first, got):
    return functools.reduce(lambda p, q: p + q.astype(F32), got, first.astype(F32)).astype(BF16)


def scatter_first(scalars, acts, got):
    half = array(2, 17, 16, 256)
    grads, up, down = call(
        kernel_grads, scalars, [acts, got], [array(16, 17, 16, 256), half, half], []
    )
    return grads, shift(up, send_first(1)), shift(down, send_first(-1))


def scatter_sides(scalars, grads, up, down):
    row = array(4, 17, 16, 256)
    after, before = call(kernel_sides, scalars, [grads, up, down], [row, row], [])
    return grads, shift(after, send_first(1)), shift(before, send_first(-1))


def scatter_second(scalars, low, high):
    piece = array(2, 17, 16, 256)
    own, *pieces = call(kernel_sum, scalars, [*low, *high], [piece] * 4, [])
    got = [shift(pieces[k - 1], send_second(k)) for k in (2, 1, 3)]
    return add_up(own, got)


def device_body(inputs, cotangent, norm_gain, proj_in, proj_out):
    where = [lax.axis_index(n).astype(jnp.int32) for n in ("x", "y", "c", "zl")]
    scalars = jnp.stack(where)
    shard = jnp.concatenate(
        [
            proj_in[0],
            proj_out[0].reshape(4, 8, 256).transpose(1, 0, 2).reshape(32, 256),
            jnp.pad(norm_gain, ((0, 7), (0, 224))),
        ],
        axis=0,
    )
    column = lax.all_to_all(
        jnp.broadcast_to(shard[None], (8, 72, 256)), ("zl", "zh"), 0, 0
    ).reshape(2, 4, 72, 256)
    gain = jnp.pad(column[:, :, 64, :32].reshape(2, 1, 1, 128), ((0, 0), (0, 0), (0, 15), (0, 128)))
    block = jnp.concatenate(
        [
            column[:, :, :32].reshape(2, 8, 16, 256),
            column[:, :, 32:64].reshape(2, 4, 8, 4, 256).transpose(0, 2, 1, 3, 4).reshape(2, 8, 16, 256),
            gain,
        ],
        axis=1,
    )
    near = []
    for p in range(2):
        near.append([block[p]] + [shift(block[p], send_first(-k)) for k in (1, 2, 3)])
    pairs = []
    for p in range(2):
        row = jnp.stack(near[p])
        after, before = shift(row, send_second(-1)), shift(row, send_second(1))
        rows = [
            row,
            after,
            before,
            shift(after[:2], send_second(-1)),
            shift(before[2:], send_second(1)),
        ]
        pairs.append(rows + [shift(v, SWAP) for v in rows])
    x1, x2, win, wout, stats, pre = call(
        kernel_low_forward,
        scalars,
        [inputs, *pairs[0]],
        [
            array(*ACT), array(*ACT), array(*WIN), array(*WOUT),
            array(2, 2, ROWS, 128, kind=F32), array(2, ROWS, R, kind=F32),
        ],
        LOW_SCRATCH,
    )
    up2, acts1 = call(
        kernel_high, scalars, [x2, cotangent, *pairs[1]], [array(*ACT), array(*ACTS)], HIGH_SCRATCH
    )
    got1 = shift(acts1[1], SWAP)
    acts0 = call(
        kernel_low_back,
        scalars,
        [inputs, x1, up2, win, wout, stats, pre],
        array(*ACTS),
        BACK_SCRATCH,
    )
    got0 = shift(acts0[1], SWAP)
    first1 = scatter_first(scalars, acts1, got1)
    first0 = scatter_first(scalars, acts0, got0)
    high = scatter_sides(scalars, *first1)
    low = scatter_sides(scalars, *first0)
    grads = scatter_second(scalars, low, high)
    parts = jnp.concatenate(
        [
            grads[:, :8].reshape(2, 4, 32, 256),
            grads[:, 8:16].reshape(2, 8, 4, 4, 256).transpose(0, 2, 1, 3, 4).reshape(2, 4, 32, 256),
            jnp.pad(grads[:, 16, 0, :128].reshape(2, 4, 1, 32), ((0, 0), (0, 0), (0, 7), (0, 224))),
        ],
        axis=2,
    ).reshape(8, 72, 256)
    total = jnp.sum(lax.all_to_all(parts, ("zl", "zh"), 0, 0).astype(F32), axis=0)
    grad_in = total[:32]
    grad_out = total[32:64].reshape(8, 4, 256).transpose(1, 0, 2).reshape(4, 2048)
    return (total[64:65, :32], grad_in[None], grad_out[None])


def solution(mesh):
    fine = Mesh(mesh.devices.reshape(DIMS), AXES)
    zero = ("x", "y", "zh")
    segment = ("zl", "c")
    return jax.shard_map(
        device_body,
        mesh=fine,
        in_specs=(
            P(None, None, zero, None),
            P(None, None, zero, None),
            P(segment, zero),
            P(segment, zero, None),
            P(segment, zero, None),
        ),
        out_specs=(P(segment, zero), P(segment, zero, None), P(segment, zero, None)),
        check_vma=False,
    )
```

```python
import functools
import itertools

import jax
import jax.numpy as jnp
import numpy as np
from jax import lax
from jax.experimental import pallas as pl
from jax.experimental.pallas import tpu as pltpu
from jax.sharding import Mesh
from jax.sharding import PartitionSpec as P


gelu_coeff = 0.7978845608028654
cubic_coeff = 0.044715
norm_eps = 1e-05

AXES = ("zl", "c", "x", "y", "zh")
DIMS = (2, 2, 4, 4, 4)
D = 2048
R = 256
ROWS = 128
CHUNK = 16
F32 = jnp.float32
BF16 = jnp.bfloat16


def flat_perm(move):
    pairs = []
    for src, coords in enumerate(itertools.product(*[range(n) for n in DIMS])):
        dst = [v % n for v, n in zip(move(*coords), DIMS)]
        pairs.append((src, int(np.ravel_multi_index(dst, DIMS))))
    return pairs


def send_first(k):
    return flat_perm(
        lambda zl, c, x, y, zh: (zl, c, x + k, y, zh) if c == 0 else (zl, c, x, y + k, zh)
    )


def send_second(k):
    return flat_perm(
        lambda zl, c, x, y, zh: (zl, c, x, y + k, zh) if c == 0 else (zl, c, x + k, y, zh)
    )


SWAP = flat_perm(lambda zl, c, x, y, zh: (zl, c + 1, x, y, zh))


def shift(value, pairs):
    return lax.ppermute(value, AXES, pairs)


def dot(left, right, left_dim=1, right_dim=0):
    return lax.dot_general(
        left, right, (((left_dim,), (right_dim,)), ((), ())), preferred_element_type=F32
    )


def gelu_parts(v):
    inner = jnp.tanh(gelu_coeff * (v + cubic_coeff * v * v * v))
    return inner, (0.5 * v * (1.0 + inner)).astype(BF16)


def gelu_slope(v, inner):
    return 0.5 * (1.0 + inner) + 0.5 * v * (1.0 - inner * inner) * gelu_coeff * (
        1.0 + 3.0 * cubic_coeff * v * v
    )


def place_weights(s_ref, pieces, win, wout):
    mx, my, c = s_ref[0], s_ref[1], s_ref[2]
    for o in range(2):
        par = c if o == 0 else 1 - c
        for src, (b, first, count) in zip(pieces[o * PIECES : (o + 1) * PIECES], SPANS):

            def place(i, carry, par=par, src=src, b=b, first=first):
                a = first + i
                x = (mx + jnp.where(par == 0, a, b)) & 3
                y = (my + jnp.where(par == 0, b, a)) & 3
                xy = x * 4 + y
                win[par, pl.ds(xy * 8, 8)] = src[i, 0:8]
                for k in range(9):
                    wout[par, k, xy] = src[i, 8 + k]
                return carry

            lax.fori_loop(0, count, place, 0)


def gain_row(wout, par):
    return jnp.concatenate(
        [wout[par, 8, xy, 0:1, 0:128] for xy in range(16)], axis=1
    ).astype(F32)


def over_rows(step):
    def body(i, carry):
        step(pl.ds(pl.multiple_of(i * CHUNK, CHUNK), CHUNK))
        return carry

    lax.fori_loop(0, ROWS // CHUNK, body, 0, unroll=UNROLL)


def hat_pass(x_at, hat, keep_stat):
    def step(rows):
        xf = x_at(rows).astype(F32)
        mean = jnp.mean(xf, axis=-1, keepdims=True)
        centered = xf - mean
        variance = jnp.mean(centered * centered, axis=-1, keepdims=True)
        recip_std = lax.rsqrt(variance + norm_eps)
        hat[rows, :] = centered * recip_std
        keep_stat(rows, mean, recip_std)

    over_rows(step)


def spread(column):
    return jnp.broadcast_to(column, (CHUNK, 128))


def layer_out(x_at, act, wout, par, out_ref):
    for k in range(8):
        cols = pl.ds(k * 256, 256)
        out_ref[:, cols] = (
            x_at(cols).astype(F32) + dot(act, wout[par, k].reshape(R, 256))
        ).astype(BF16)


def layer_back(up_at, acts, slot, hat, rstd_at, preact, win, wout, par, gain, gnorm, gsum, up_out):
    inner, act = gelu_parts(preact)
    grad_act = jnp.zeros((ROWS, R), F32)
    for k in range(8):
        grad_act += dot(
            up_at(pl.ds(0, ROWS), pl.ds(k * 256, 256)), wout[par, k].reshape(R, 256), 1, 1
        )
    grad_pre = (grad_act * gelu_slope(preact, inner)).astype(BF16)
    acts[slot, 0:ROWS, ACT_AT : ACT_AT + R] = act
    acts[slot, 0:ROWS, PRE_AT : PRE_AT + R] = grad_pre
    for k in range(8):
        gnorm[:, pl.ds(k * 256, 256)] = dot(
            grad_pre, win[par, pl.ds(k * 16, 16)].reshape(256, R), 1, 1
        )
    gsum[...] = jnp.zeros((CHUNK, D), F32)

    def step(rows):
        grad_normed = gnorm[rows, :]
        hatted = hat[rows, :]
        product = grad_normed * hatted
        gsum[...] += product
        up = up_at(rows, pl.ds(0, D))
        acts[slot, rows, UP_AT : UP_AT + D] = up
        if up_out is not None:
            grad_hat = grad_normed * gain
            mean_hat = jnp.mean(grad_hat, axis=-1, keepdims=True)
            mean_both = jnp.mean(product * gain, axis=-1, keepdims=True)
            through = rstd_at(rows) * (grad_hat - mean_hat - hatted * mean_both)
            up_out[rows, :] = (up.astype(F32) + through).astype(BF16)

    over_rows(step)
    acts[slot, ROWS : ROWS + 16, 0:D] = jnp.broadcast_to(
        jnp.sum(gsum[...], axis=0, keepdims=True), (16, D)
    ).astype(BF16)


def kernel_low_forward(s_ref, xs, *refs):
    pieces, (x1, x2, win, wout, stats, pre, normed, hat) = refs[: 2 * PIECES], refs[2 * PIECES :]
    place_weights(s_ref, pieces, win, wout)
    c, zl = s_ref[2], s_ref[3]
    for par in range(2):

        def x_at(rows=slice(None), cols=slice(None), par=par):
            return xs[zl, c, rows, cols] if par == 0 else x1[rows, cols]

        def keep_stat(rows, mean, recip_std, par=par):
            stats[par, 0, rows, :] = spread(mean)
            stats[par, 1, rows, :] = spread(recip_std)

        hat_pass(x_at, hat, keep_stat)
        gain = gain_row(wout, par)

        def step(rows, gain=gain):
            normed[rows, :] = (hat[rows, :] * gain).astype(BF16)

        over_rows(step)
        pre[par] = dot(normed[...], win[par].reshape(D, R))
        act = gelu_parts(pre[par])[1]
        layer_out(lambda cols: x_at(slice(None), cols), act, wout, par, x2 if par else x1)


def kernel_high(s_ref, x2, cots, *refs):
    pieces = refs[: 2 * PIECES]
    up2, acts, win, wout, hat0, hat1, rstd, x3, up3, pre0, gnorm, gsum = refs[2 * PIECES :]
    place_weights(s_ref, pieces, win, wout)
    c, zl = s_ref[2], s_ref[3]
    gains = []
    for par, (src, hat) in enumerate(((x2, hat0), (x3, hat1))):

        def keep_stat(rows, mean, recip_std, par=par):
            rstd[par, rows, :] = spread(recip_std)

        hat_pass(lambda rows, src=src: src[rows, :], hat, keep_stat)
        gain = gain_row(wout, par)
        slot = jnp.where(c == par, 0, 1)

        def step(rows, gain=gain, hat=hat, slot=slot):
            acts[slot, rows, 0:D] = (hat[rows, :] * gain).astype(BF16)

        over_rows(step)
        preact = dot(acts[slot, 0:ROWS, 0:D], win[par].reshape(D, R))
        gains.append(gain)
        if par == 0:
            pre0[...] = preact
            layer_out(lambda cols: x2[:, cols], gelu_parts(preact)[1], wout, 0, x3)
    layer_back(
        lambda rows, cols: cots[zl, c, rows, cols],
        acts, jnp.where(c == 1, 0, 1), hat1, lambda rows: rstd[1, rows, 0:1],
        preact, win, wout, 1, gains[1], gnorm, gsum, up3,
    )
    layer_back(
        lambda rows, cols: up3[rows, cols],
        acts, jnp.where(c == 0, 0, 1), hat0, lambda rows: rstd[0, rows, 0:1],
        pre0[...], win, wout, 0, gains[0], gnorm, gsum, up2,
    )


def kernel_low_back(s_ref, xs, x1, up2, win, wout, stats, pre, acts, hat, up1, gnorm, gsum):
    c, zl = s_ref[2], s_ref[3]
    for par, up, up_out in ((1, up2, up1), (0, up1, None)):
        gain = gain_row(wout, par)
        slot = jnp.where(c == par, 0, 1)

        def step(rows, par=par, gain=gain, slot=slot):
            xf = (x1[rows, :] if par else xs[zl, c, rows, :]).astype(F32)
            hatted = (xf - stats[par, 0, rows, 0:1]) * stats[par, 1, rows, 0:1]
            hat[rows, :] = hatted
            acts[slot, rows, 0:D] = (hatted * gain).astype(BF16)

        over_rows(step)
        layer_back(
            lambda rows, cols, up=up: up[rows, cols],
            acts, slot, hat, lambda rows, par=par: stats[par, 1, rows, 0:1],
            pre[par], win, wout, par, gain, gnorm, gsum, up_out,
        )


def kernel_grads(s_ref, acts, got, out, up, down):
    mx, my, c = s_ref[0], s_ref[1], s_ref[2]
    places = []
    for xy in range(16):
        xr = (xy // 4 - mx) & 3
        yr = (xy % 4 - my) & 3
        places.append(jnp.where(c == 0, xr * 4 + yr, yr * 4 + xr))

    def both(start, size):
        cols = pl.ds(start, size)
        return jnp.concatenate([acts[0, 0:ROWS, cols], got[0:ROWS, cols]], axis=0)

    grad_pre = both(PRE_AT, R)
    for xy in range(16):
        block = dot(both(xy * 128, 128).T, grad_pre)
        out[places[xy], 0:8] = block.astype(BF16).reshape(8, 16, 256)
    act_t = both(ACT_AT, R).T
    for k in range(8):
        block = dot(act_t, both(UP_AT + k * 256, 256)).astype(BF16).reshape(16, 16, 256)
        for xy in range(16):
            out[places[xy], 8 + k] = block[xy]
    for xy in range(16):
        cols = pl.ds(xy * 128, 128)
        part = acts[0, ROWS : ROWS + 16, cols].astype(F32) + got[ROWS : ROWS + 16, cols].astype(F32)
        out[places[xy], 16] = jnp.concatenate([part, part], axis=1).astype(BF16)


    up[...] = out[8:10]
    down[...] = out[10:12]


def over_groups(step):
    def body(g, carry):
        step(g)
        return carry

    lax.fori_loop(0, 17, body, 0)


def kernel_sides(s_ref, grads, up, down, after, before):
    def step(g):
        for i in range(2):
            after[i, g] = (grads[4 + i, g].astype(F32) + up[i, g].astype(F32)).astype(BF16)
            after[2 + i, g] = grads[6 + i, g]
            before[i, g] = grads[12 + i, g]
            before[2 + i, g] = (grads[14 + i, g].astype(F32) + down[i, g].astype(F32)).astype(BF16)

    over_groups(step)


def kernel_sum(s_ref, own, a, b, *pieces):
    def step(g):
        for k in range(4):
            pieces[k][g] = (
                own[k, g].astype(F32) + a[k, g].astype(F32) + b[k, g].astype(F32)
            ).astype(BF16)

    over_groups(step)


def vmem(*shape, kind=BF16):
    return pltpu.VMEM(shape, kind)


def array(*shape, kind=BF16):
    return jax.ShapeDtypeStruct(shape, kind)


UNROLL = 8
SPANS = tuple((b, 0, 4) for b in range(4))
PIECES = len(SPANS)
UP_AT, ACT_AT, PRE_AT, WIDE = D, 2 * D, 2 * D + R, 2 * D + 2 * R
ACT = (ROWS, D)
WIN, WOUT = (2, 128, 16, 256), (2, 9, 16, 16, 256)
ACTS = (2, ROWS + 16, WIDE)
HAT = vmem(ROWS, D, kind=F32)
GSUM = vmem(CHUNK, D, kind=F32)
LOW_SCRATCH = [vmem(*ACT), HAT]
HIGH_SCRATCH = [
    vmem(*WIN), vmem(*WOUT), HAT, HAT, vmem(2, ROWS, 128, kind=F32),
    vmem(*ACT), vmem(*ACT), vmem(ROWS, R, kind=F32), HAT, GSUM,
]
BACK_SCRATCH = [HAT, vmem(*ACT), HAT, GSUM]
WHOLE = pl.BlockSpec(memory_space=pltpu.VMEM)


def call(body, scalars, args, out_shape, scratch):
    return pl.pallas_call(
        body,
        in_specs=[pl.BlockSpec(memory_space=pltpu.SMEM)] + [WHOLE] * len(args),
        out_specs=jax.tree.map(lambda s: WHOLE, out_shape),
        scratch_shapes=scratch,
        out_shape=out_shape,
        compiler_params=pltpu.CompilerParams(vmem_limit_bytes=20 * 1024 * 1024),
    )(scalars, *args)


def add_up(first, got):
    return functools.reduce(lambda p, q: p + q.astype(F32), got, first.astype(F32)).astype(BF16)


def scatter_first(scalars, acts, got):
    half = array(2, 17, 16, 256)
    grads, up, down = call(
        kernel_grads, scalars, [acts, got], [array(16, 17, 16, 256), half, half], []
    )
    return grads, shift(up, send_first(1)), shift(down, send_first(-1))


def scatter_sides(scalars, grads, up, down):
    row = array(4, 17, 16, 256)
    after, before = call(kernel_sides, scalars, [grads, up, down], [row, row], [])
    return grads, shift(after, send_first(1)), shift(before, send_first(-1))


def scatter_second(scalars, parts):
    piece = array(17, 16, 256)
    own, *pieces = call(kernel_sum, scalars, parts, [piece] * 4, [])
    got = [shift(pieces[k - 1], send_second(k)) for k in (2, 1, 3)]
    return add_up(own, got)


def device_body(inputs, cotangent, norm_gain, proj_in, proj_out):
    where = [lax.axis_index(n).astype(jnp.int32) for n in ("x", "y", "c", "zl")]
    scalars = jnp.stack(where)
    shard = jnp.concatenate(
        [
            proj_in[0],
            proj_out[0].reshape(4, 8, 256).transpose(1, 0, 2).reshape(32, 256),
            jnp.pad(norm_gain, ((0, 7), (0, 224))),
        ],
        axis=0,
    )
    column = lax.all_to_all(
        jnp.broadcast_to(shard[None], (8, 72, 256)), ("zl", "zh"), 0, 0
    ).reshape(2, 4, 72, 256)
    gain = jnp.pad(column[:, :, 64, :32].reshape(2, 1, 1, 128), ((0, 0), (0, 0), (0, 15), (0, 128)))
    block = jnp.concatenate(
        [
            column[:, :, :32].reshape(2, 8, 16, 256),
            column[:, :, 32:64].reshape(2, 4, 8, 4, 256).transpose(0, 2, 1, 3, 4).reshape(2, 8, 16, 256),
            gain,
        ],
        axis=1,
    )
    near = [block] + [shift(block, send_first(-k)) for k in (1, 2, 3)]
    pairs = []
    for p in range(2):
        row = jnp.stack([v[p] for v in near])
        rows = [row] + [shift(row, send_second(-k)) for k in (1, 2, 3)]
        pairs.append(rows + [shift(v, SWAP) for v in rows])
    x1, x2, win, wout, stats, pre = call(
        kernel_low_forward,
        scalars,
        [inputs, *pairs[0]],
        [
            array(*ACT), array(*ACT), array(*WIN), array(*WOUT),
            array(2, 2, ROWS, 128, kind=F32), array(2, ROWS, R, kind=F32),
        ],
        LOW_SCRATCH,
    )
    up2, acts1 = call(
        kernel_high, scalars, [x2, cotangent, *pairs[1]], [array(*ACT), array(*ACTS)], HIGH_SCRATCH
    )
    got1 = shift(acts1[1], SWAP)
    acts0 = call(
        kernel_low_back,
        scalars,
        [inputs, x1, up2, win, wout, stats, pre],
        array(*ACTS),
        BACK_SCRATCH,
    )
    got0 = shift(acts0[1], SWAP)
    first1 = scatter_first(scalars, acts1, got1)
    first0 = scatter_first(scalars, acts0, got0)
    sides1 = scatter_sides(scalars, *first1)
    sides0 = scatter_sides(scalars, *first0)
    high = scatter_second(scalars, sides1)
    low = scatter_second(scalars, sides0)
    grads = jnp.stack([low, high])
    parts = jnp.concatenate(
        [
            grads[:, :8].reshape(2, 4, 32, 256),
            grads[:, 8:16].reshape(2, 8, 4, 4, 256).transpose(0, 2, 1, 3, 4).reshape(2, 4, 32, 256),
            jnp.pad(grads[:, 16, 0, :128].reshape(2, 4, 1, 32), ((0, 0), (0, 0), (0, 7), (0, 224))),
        ],
        axis=2,
    ).reshape(8, 72, 256)
    total = jnp.sum(lax.all_to_all(parts, ("zl", "zh"), 0, 0).astype(F32), axis=0)
    grad_in = total[:32]
    grad_out = total[32:64].reshape(8, 4, 256).transpose(1, 0, 2).reshape(4, 2048)
    return (total[64:65, :32], grad_in[None], grad_out[None])


def solution(mesh):
    fine = Mesh(mesh.devices.reshape(DIMS), AXES)
    zero = ("x", "y", "zh")
    segment = ("zl", "c")
    return jax.shard_map(
        device_body,
        mesh=fine,
        in_specs=(
            P(None, None, zero, None),
            P(None, None, zero, None),
            P(segment, zero),
            P(segment, zero, None),
            P(segment, zero, None),
        ),
        out_specs=(P(segment, zero), P(segment, zero, None), P(segment, zero, None)),
        check_vma=False,
    )
```

```python
import functools
import itertools

import jax
import jax.numpy as jnp
import numpy as np
from jax import lax
from jax.experimental import pallas as pl
from jax.experimental.pallas import tpu as pltpu
from jax.sharding import Mesh
from jax.sharding import PartitionSpec as P


gelu_coeff = 0.7978845608028654
cubic_coeff = 0.044715
norm_eps = 1e-05

AXES = ("zl", "c", "x", "y", "zh")
DIMS = (2, 2, 4, 4, 4)
D = 2048
R = 256
ROWS = 128
CHUNK = 16
F32 = jnp.float32
BF16 = jnp.bfloat16


def flat_perm(move):
    pairs = []
    for src, coords in enumerate(itertools.product(*[range(n) for n in DIMS])):
        dst = [v % n for v, n in zip(move(*coords), DIMS)]
        pairs.append((src, int(np.ravel_multi_index(dst, DIMS))))
    return pairs


def send_first(k):
    return flat_perm(
        lambda zl, c, x, y, zh: (zl, c, x + k, y, zh) if c == 0 else (zl, c, x, y + k, zh)
    )


def send_second(k):
    return flat_perm(
        lambda zl, c, x, y, zh: (zl, c, x, y + k, zh) if c == 0 else (zl, c, x + k, y, zh)
    )


SWAP = flat_perm(lambda zl, c, x, y, zh: (zl, c + 1, x, y, zh))


def shift(value, pairs):
    return lax.ppermute(value, AXES, pairs)


def dot(left, right, left_dim=1, right_dim=0):
    return lax.dot_general(
        left, right, (((left_dim,), (right_dim,)), ((), ())), preferred_element_type=F32
    )


def gelu_parts(v):
    inner = jnp.tanh(gelu_coeff * (v + cubic_coeff * v * v * v))
    return inner, (0.5 * v * (1.0 + inner)).astype(BF16)


def gelu_slope(v, inner):
    return 0.5 * (1.0 + inner) + 0.5 * v * (1.0 - inner * inner) * gelu_coeff * (
        1.0 + 3.0 * cubic_coeff * v * v
    )


def place_weights(s_ref, pieces, win, wout):
    mx, my, c = s_ref[0], s_ref[1], s_ref[2]
    for o in range(2):
        par = c if o == 0 else 1 - c
        for src, (b, first, count) in zip(pieces[o * PIECES : (o + 1) * PIECES], SPANS):

            def place(i, carry, par=par, src=src, b=b, first=first):
                a = first + i
                x = (mx + jnp.where(par == 0, a, b)) & 3
                y = (my + jnp.where(par == 0, b, a)) & 3
                xy = x * 4 + y
                win[par, pl.ds(xy * 8, 8)] = src[i, 0:8]
                for k in range(9):
                    wout[par, k, xy] = src[i, 8 + k]
                return carry

            lax.fori_loop(0, count, place, 0)


def gain_row(wout, par):
    return jnp.concatenate(
        [wout[par, 8, xy, 0:1, 0:128] for xy in range(16)], axis=1
    ).astype(F32)


def over_rows(step):
    def body(i, carry):
        step(pl.ds(pl.multiple_of(i * CHUNK, CHUNK), CHUNK))
        return carry

    lax.fori_loop(0, ROWS // CHUNK, body, 0, unroll=UNROLL)


def hat_pass(x_at, hat, keep_stat):
    def step(rows):
        xf = x_at(rows).astype(F32)
        mean = jnp.mean(xf, axis=-1, keepdims=True)
        centered = xf - mean
        variance = jnp.mean(centered * centered, axis=-1, keepdims=True)
        recip_std = lax.rsqrt(variance + norm_eps)
        hat[rows, :] = centered * recip_std
        keep_stat(rows, mean, recip_std)

    over_rows(step)


def spread(column):
    return jnp.broadcast_to(column, (CHUNK, 128))


def layer_out(x_at, act, wout, par, out_ref):
    for k in range(8):
        cols = pl.ds(k * 256, 256)
        out_ref[:, cols] = (
            x_at(cols).astype(F32) + dot(act, wout[par, k].reshape(R, 256))
        ).astype(BF16)


def layer_back(up_at, acts, slot, hat, rstd_at, preact, win, wout, par, gain, gnorm, gsum, up_out):
    inner, act = gelu_parts(preact)
    grad_act = jnp.zeros((ROWS, R), F32)
    for k in range(8):
        grad_act += dot(
            up_at(pl.ds(0, ROWS), pl.ds(k * 256, 256)), wout[par, k].reshape(R, 256), 1, 1
        )
    grad_pre = (grad_act * gelu_slope(preact, inner)).astype(BF16)
    acts[slot, 0:ROWS, ACT_AT : ACT_AT + R] = act
    acts[slot, 0:ROWS, PRE_AT : PRE_AT + R] = grad_pre
    for k in range(8):
        gnorm[:, pl.ds(k * 256, 256)] = dot(
            grad_pre, win[par, pl.ds(k * 16, 16)].reshape(256, R), 1, 1
        )
    gsum[...] = jnp.zeros((CHUNK, D), F32)

    def step(rows):
        grad_normed = gnorm[rows, :]
        hatted = hat[rows, :]
        product = grad_normed * hatted
        gsum[...] += product
        up = up_at(rows, pl.ds(0, D))
        acts[slot, rows, UP_AT : UP_AT + D] = up
        if up_out is not None:
            grad_hat = grad_normed * gain
            mean_hat = jnp.mean(grad_hat, axis=-1, keepdims=True)
            mean_both = jnp.mean(product * gain, axis=-1, keepdims=True)
            through = rstd_at(rows) * (grad_hat - mean_hat - hatted * mean_both)
            up_out[rows, :] = (up.astype(F32) + through).astype(BF16)

    over_rows(step)
    acts[slot, ROWS : ROWS + 16, 0:D] = jnp.broadcast_to(
        jnp.sum(gsum[...], axis=0, keepdims=True), (16, D)
    ).astype(BF16)


def kernel_low_forward(s_ref, xs, *refs):
    pieces, (x1, x2, win, wout, stats, pre, normed, hat) = refs[: 2 * PIECES], refs[2 * PIECES :]
    place_weights(s_ref, pieces, win, wout)
    c, zl = s_ref[2], s_ref[3]
    for par in range(2):

        def x_at(rows=slice(None), cols=slice(None), par=par):
            return xs[zl, c, rows, cols] if par == 0 else x1[rows, cols]

        def keep_stat(rows, mean, recip_std, par=par):
            stats[par, 0, rows, :] = spread(mean)
            stats[par, 1, rows, :] = spread(recip_std)

        hat_pass(x_at, hat, keep_stat)
        gain = gain_row(wout, par)

        def step(rows, gain=gain):
            normed[rows, :] = (hat[rows, :] * gain).astype(BF16)

        over_rows(step)
        pre[par] = dot(normed[...], win[par].reshape(D, R))
        act = gelu_parts(pre[par])[1]
        layer_out(lambda cols: x_at(slice(None), cols), act, wout, par, x2 if par else x1)


def kernel_high(s_ref, x2, cots, *refs):
    pieces = refs[: 2 * PIECES]
    up2, acts, win, wout, hat0, hat1, rstd, x3, up3, pre0, gnorm, gsum = refs[2 * PIECES :]
    place_weights(s_ref, pieces, win, wout)
    c, zl = s_ref[2], s_ref[3]
    gains = []
    for par, (src, hat) in enumerate(((x2, hat0), (x3, hat1))):

        def keep_stat(rows, mean, recip_std, par=par):
            rstd[par, rows, :] = spread(recip_std)

        hat_pass(lambda rows, src=src: src[rows, :], hat, keep_stat)
        gain = gain_row(wout, par)
        slot = jnp.where(c == par, 0, 1)

        def step(rows, gain=gain, hat=hat, slot=slot):
            acts[slot, rows, 0:D] = (hat[rows, :] * gain).astype(BF16)

        over_rows(step)
        preact = dot(acts[slot, 0:ROWS, 0:D], win[par].reshape(D, R))
        gains.append(gain)
        if par == 0:
            pre0[...] = preact
            layer_out(lambda cols: x2[:, cols], gelu_parts(preact)[1], wout, 0, x3)
    layer_back(
        lambda rows, cols: cots[zl, c, rows, cols],
        acts, jnp.where(c == 1, 0, 1), hat1, lambda rows: rstd[1, rows, 0:1],
        preact, win, wout, 1, gains[1], gnorm, gsum, up3,
    )
    layer_back(
        lambda rows, cols: up3[rows, cols],
        acts, jnp.where(c == 0, 0, 1), hat0, lambda rows: rstd[0, rows, 0:1],
        pre0[...], win, wout, 0, gains[0], gnorm, gsum, up2,
    )


def kernel_low_back(s_ref, xs, x1, up2, win, wout, stats, pre, acts, hat, up1, gnorm, gsum):
    c, zl = s_ref[2], s_ref[3]
    for par, up, up_out in ((1, up2, up1), (0, up1, None)):
        gain = gain_row(wout, par)
        slot = jnp.where(c == par, 0, 1)

        def step(rows, par=par, gain=gain, slot=slot):
            xf = (x1[rows, :] if par else xs[zl, c, rows, :]).astype(F32)
            hatted = (xf - stats[par, 0, rows, 0:1]) * stats[par, 1, rows, 0:1]
            hat[rows, :] = hatted
            acts[slot, rows, 0:D] = (hatted * gain).astype(BF16)

        over_rows(step)
        layer_back(
            lambda rows, cols, up=up: up[rows, cols],
            acts, slot, hat, lambda rows, par=par: stats[par, 1, rows, 0:1],
            pre[par], win, wout, par, gain, gnorm, gsum, up_out,
        )


def kernel_grads(s_ref, acts, got, out, up, down):
    mx, my, c = s_ref[0], s_ref[1], s_ref[2]
    places = []
    for xy in range(16):
        xr = (xy // 4 - mx) & 3
        yr = (xy % 4 - my) & 3
        places.append(jnp.where(c == 0, xr * 4 + yr, yr * 4 + xr))

    def both(start, size):
        cols = pl.ds(start, size)
        return jnp.concatenate([acts[0, 0:ROWS, cols], got[0:ROWS, cols]], axis=0)

    grad_pre = both(PRE_AT, R)
    for xy in range(16):
        block = dot(both(xy * 128, 128).T, grad_pre)
        out[places[xy], 0:8] = block.astype(BF16).reshape(8, 16, 256)
    act_t = both(ACT_AT, R).T
    for k in range(8):
        block = dot(act_t, both(UP_AT + k * 256, 256)).astype(BF16).reshape(16, 16, 256)
        for xy in range(16):
            out[places[xy], 8 + k] = block[xy]
    for xy in range(16):
        cols = pl.ds(xy * 128, 128)
        part = acts[0, ROWS : ROWS + 16, cols].astype(F32) + got[ROWS : ROWS + 16, cols].astype(F32)
        out[places[xy], 16] = jnp.concatenate([part, part], axis=1).astype(BF16)


    up[...] = out[8:10]
    down[...] = out[10:12]


def over_groups(step):
    def body(g, carry):
        step(g)
        return carry

    lax.fori_loop(0, 17, body, 0)


def kernel_sides(s_ref, grads, up, down, after, before):
    def step(g):
        for i in range(2):
            after[i, g] = (grads[4 + i, g].astype(F32) + up[i, g].astype(F32)).astype(BF16)
            after[2 + i, g] = grads[6 + i, g]
            before[i, g] = grads[12 + i, g]
            before[2 + i, g] = (grads[14 + i, g].astype(F32) + down[i, g].astype(F32)).astype(BF16)

    over_groups(step)


def kernel_sum(s_ref, own, a, b, *pieces):
    def step(g):
        for k in range(4):
            pieces[k][g] = (
                own[k, g].astype(F32) + a[k, g].astype(F32) + b[k, g].astype(F32)
            ).astype(BF16)

    over_groups(step)


def kernel_finish(s_ref, parts, gain, grad_in, grad_out):
    total = parts[0].astype(F32)
    for i in range(1, 8):
        total += parts[i].astype(F32)
    grad_in[0] = total[0:32]
    for k in range(8):
        grad_out[0, :, pl.ds(k * 256, 256)] = total[32 + 4 * k : 36 + 4 * k]
    gain[...] = total[64:65, 0:32]


def vmem(*shape, kind=BF16):
    return pltpu.VMEM(shape, kind)


def array(*shape, kind=BF16):
    return jax.ShapeDtypeStruct(shape, kind)


UNROLL = 8
SPANS = tuple((b, 0, 4) for b in range(4))
PIECES = len(SPANS)
UP_AT, ACT_AT, PRE_AT, WIDE = D, 2 * D, 2 * D + R, 2 * D + 2 * R
ACT = (ROWS, D)
WIN, WOUT = (2, 128, 16, 256), (2, 9, 16, 16, 256)
ACTS = (2, ROWS + 16, WIDE)
HAT = vmem(ROWS, D, kind=F32)
GSUM = vmem(CHUNK, D, kind=F32)
LOW_SCRATCH = [vmem(*ACT), HAT]
HIGH_SCRATCH = [
    vmem(*WIN), vmem(*WOUT), HAT, HAT, vmem(2, ROWS, 128, kind=F32),
    vmem(*ACT), vmem(*ACT), vmem(ROWS, R, kind=F32), HAT, GSUM,
]
BACK_SCRATCH = [HAT, vmem(*ACT), HAT, GSUM]
WHOLE = pl.BlockSpec(memory_space=pltpu.VMEM)


def call(body, scalars, args, out_shape, scratch):
    return pl.pallas_call(
        body,
        in_specs=[pl.BlockSpec(memory_space=pltpu.SMEM)] + [WHOLE] * len(args),
        out_specs=jax.tree.map(lambda s: WHOLE, out_shape),
        scratch_shapes=scratch,
        out_shape=out_shape,
        compiler_params=pltpu.CompilerParams(vmem_limit_bytes=20 * 1024 * 1024),
    )(scalars, *args)


def add_up(first, got):
    return functools.reduce(lambda p, q: p + q.astype(F32), got, first.astype(F32)).astype(BF16)


def scatter_first(scalars, acts, got):
    half = array(2, 17, 16, 256)
    grads, up, down = call(
        kernel_grads, scalars, [acts, got], [array(16, 17, 16, 256), half, half], []
    )
    return grads, shift(up, send_first(1)), shift(down, send_first(-1))


def scatter_sides(scalars, grads, up, down):
    row = array(4, 17, 16, 256)
    after, before = call(kernel_sides, scalars, [grads, up, down], [row, row], [])
    return grads, shift(after, send_first(1)), shift(before, send_first(-1))


def scatter_second(scalars, parts):
    piece = array(17, 16, 256)
    own, *pieces = call(kernel_sum, scalars, parts, [piece] * 4, [])
    got = [shift(pieces[k - 1], send_second(k)) for k in (2, 1, 3)]
    return add_up(own, got)


def device_body(inputs, cotangent, norm_gain, proj_in, proj_out):
    where = [lax.axis_index(n).astype(jnp.int32) for n in ("x", "y", "c", "zl")]
    scalars = jnp.stack(where)
    shard = jnp.concatenate(
        [
            proj_in[0],
            proj_out[0].reshape(4, 8, 256).transpose(1, 0, 2).reshape(32, 256),
            jnp.pad(norm_gain, ((0, 7), (0, 224))),
        ],
        axis=0,
    )
    column = lax.all_to_all(
        jnp.broadcast_to(shard[None], (8, 72, 256)), ("zl", "zh"), 0, 0
    ).reshape(2, 4, 72, 256)
    gain = jnp.pad(column[:, :, 64, :32].reshape(2, 1, 1, 128), ((0, 0), (0, 0), (0, 15), (0, 128)))
    block = jnp.concatenate(
        [
            column[:, :, :32].reshape(2, 8, 16, 256),
            column[:, :, 32:64].reshape(2, 4, 8, 4, 256).transpose(0, 2, 1, 3, 4).reshape(2, 8, 16, 256),
            gain,
        ],
        axis=1,
    )
    near = []
    for p in range(2):
        near.append([block[p]] + [shift(block[p], send_first(-k)) for k in (1, 2, 3)])
    pairs = []
    for p in range(2):
        row = jnp.stack(near[p])
        rows = [row] + [shift(row, send_second(-k)) for k in (1, 2, 3)]
        pairs.append(rows + [shift(v, SWAP) for v in rows])
    x1, x2, win, wout, stats, pre = call(
        kernel_low_forward,
        scalars,
        [inputs, *pairs[0]],
        [
            array(*ACT), array(*ACT), array(*WIN), array(*WOUT),
            array(2, 2, ROWS, 128, kind=F32), array(2, ROWS, R, kind=F32),
        ],
        LOW_SCRATCH,
    )
    up2, acts1 = call(
        kernel_high, scalars, [x2, cotangent, *pairs[1]], [array(*ACT), array(*ACTS)], HIGH_SCRATCH
    )
    got1 = shift(acts1[1], SWAP)
    acts0 = call(
        kernel_low_back,
        scalars,
        [inputs, x1, up2, win, wout, stats, pre],
        array(*ACTS),
        BACK_SCRATCH,
    )
    got0 = shift(acts0[1], SWAP)
    first1 = scatter_first(scalars, acts1, got1)
    first0 = scatter_first(scalars, acts0, got0)
    sides1 = scatter_sides(scalars, *first1)
    sides0 = scatter_sides(scalars, *first0)
    high = scatter_second(scalars, sides1)
    low = scatter_second(scalars, sides0)
    grads = jnp.stack([low, high])
    parts = jnp.concatenate(
        [
            grads[:, :8].reshape(2, 4, 32, 256),
            grads[:, 8:16].reshape(2, 8, 4, 4, 256).transpose(0, 2, 1, 3, 4).reshape(2, 4, 32, 256),
            jnp.pad(grads[:, 16, 0, :128].reshape(2, 4, 1, 32), ((0, 0), (0, 0), (0, 7), (0, 224))),
        ],
        axis=2,
    ).reshape(8, 72, 256)
    return call(
        kernel_finish,
        scalars,
        [lax.all_to_all(parts, ("zl", "zh"), 0, 0)],
        (array(1, 32, kind=F32), array(1, 32, 256, kind=F32), array(1, 4, 2048, kind=F32)),
        [],
    )


def solution(mesh):
    fine = Mesh(mesh.devices.reshape(DIMS), AXES)
    zero = ("x", "y", "zh")
    segment = ("zl", "c")
    return jax.shard_map(
        device_body,
        mesh=fine,
        in_specs=(
            P(None, None, zero, None),
            P(None, None, zero, None),
            P(segment, zero),
            P(segment, zero, None),
            P(segment, zero, None),
        ),
        out_specs=(P(segment, zero), P(segment, zero, None), P(segment, zero, None)),
        check_vma=False,
    )
```

```python
import functools
import itertools

import jax
import jax.numpy as jnp
import numpy as np
from jax import lax
from jax.experimental import pallas as pl
from jax.experimental.pallas import tpu as pltpu
from jax.sharding import Mesh
from jax.sharding import PartitionSpec as P


gelu_coeff = 0.7978845608028654
cubic_coeff = 0.044715
norm_eps = 1e-05

AXES = ("zl", "c", "x", "y", "zh")
DIMS = (2, 2, 4, 4, 4)
D = 2048
R = 256
ROWS = 128
CHUNK = 16
F32 = jnp.float32
BF16 = jnp.bfloat16


def flat_perm(move):
    pairs = []
    for src, coords in enumerate(itertools.product(*[range(n) for n in DIMS])):
        dst = [v % n for v, n in zip(move(*coords), DIMS)]
        pairs.append((src, int(np.ravel_multi_index(dst, DIMS))))
    return pairs


def send_first(k):
    return flat_perm(
        lambda zl, c, x, y, zh: (zl, c, x + k, y, zh) if c == 0 else (zl, c, x, y + k, zh)
    )


def send_second(k):
    return flat_perm(
        lambda zl, c, x, y, zh: (zl, c, x, y + k, zh) if c == 0 else (zl, c, x + k, y, zh)
    )


SWAP = flat_perm(lambda zl, c, x, y, zh: (zl, c + 1, x, y, zh))


def shift(value, pairs):
    return lax.ppermute(value, AXES, pairs)


def dot(left, right, left_dim=1, right_dim=0):
    return lax.dot_general(
        left, right, (((left_dim,), (right_dim,)), ((), ())), preferred_element_type=F32
    )


def gelu_parts(v):
    inner = jnp.tanh(gelu_coeff * (v + cubic_coeff * v * v * v))
    return inner, (0.5 * v * (1.0 + inner)).astype(BF16)


def gelu_slope(v, inner):
    return 0.5 * (1.0 + inner) + 0.5 * v * (1.0 - inner * inner) * gelu_coeff * (
        1.0 + 3.0 * cubic_coeff * v * v
    )


def place_weights(s_ref, pieces, win, wout):
    mx, my, c = s_ref[0], s_ref[1], s_ref[2]
    for o in range(2):
        par = c if o == 0 else 1 - c
        for src, (b, first, count) in zip(pieces[o * PIECES : (o + 1) * PIECES], SPANS):

            def place(i, carry, par=par, src=src, b=b, first=first):
                a = first + i
                x = (mx + jnp.where(par == 0, a, b)) & 3
                y = (my + jnp.where(par == 0, b, a)) & 3
                xy = x * 4 + y
                win[par, pl.ds(xy * 8, 8)] = src[i, 0:8]
                for k in range(9):
                    wout[par, k, xy] = src[i, 8 + k]
                return carry

            lax.fori_loop(0, count, place, 0)


def gain_row(wout, par):
    return jnp.concatenate(
        [wout[par, 8, xy, 0:1, 0:128] for xy in range(16)], axis=1
    ).astype(F32)


def over_rows(step):
    def body(i, carry):
        step(pl.ds(pl.multiple_of(i * CHUNK, CHUNK), CHUNK))
        return carry

    lax.fori_loop(0, ROWS // CHUNK, body, 0, unroll=UNROLL)


def hat_pass(x_at, hat, keep_stat):
    def step(rows):
        xf = x_at(rows).astype(F32)
        mean = jnp.mean(xf, axis=-1, keepdims=True)
        centered = xf - mean
        variance = jnp.mean(centered * centered, axis=-1, keepdims=True)
        recip_std = lax.rsqrt(variance + norm_eps)
        hat[rows, :] = centered * recip_std
        keep_stat(rows, mean, recip_std)

    over_rows(step)


def spread(column):
    return jnp.broadcast_to(column, (CHUNK, 128))


def layer_out(x_at, act, wout, par, out_ref):
    for k in range(8):
        cols = pl.ds(k * 256, 256)
        out_ref[:, cols] = (
            x_at(cols).astype(F32) + dot(act, wout[par, k].reshape(R, 256))
        ).astype(BF16)


def layer_back(up_at, acts, slot, hat, rstd_at, preact, win, wout, par, gain, gnorm, gsum, up_out):
    inner, act = gelu_parts(preact)
    grad_act = jnp.zeros((ROWS, R), F32)
    for k in range(8):
        grad_act += dot(
            up_at(pl.ds(0, ROWS), pl.ds(k * 256, 256)), wout[par, k].reshape(R, 256), 1, 1
        )
    grad_pre = (grad_act * gelu_slope(preact, inner)).astype(BF16)
    acts[slot, 0:ROWS, ACT_AT : ACT_AT + R] = act
    acts[slot, 0:ROWS, PRE_AT : PRE_AT + R] = grad_pre
    for k in range(8):
        gnorm[:, pl.ds(k * 256, 256)] = dot(
            grad_pre, win[par, pl.ds(k * 16, 16)].reshape(256, R), 1, 1
        )
    gsum[...] = jnp.zeros((CHUNK, D), F32)

    def step(rows):
        grad_normed = gnorm[rows, :]
        hatted = hat[rows, :]
        product = grad_normed * hatted
        gsum[...] += product
        up = up_at(rows, pl.ds(0, D))
        acts[slot, rows, UP_AT : UP_AT + D] = up
        if up_out is not None:
            grad_hat = grad_normed * gain
            mean_hat = jnp.mean(grad_hat, axis=-1, keepdims=True)
            mean_both = jnp.mean(product * gain, axis=-1, keepdims=True)
            through = rstd_at(rows) * (grad_hat - mean_hat - hatted * mean_both)
            up_out[rows, :] = (up.astype(F32) + through).astype(BF16)

    over_rows(step)
    acts[slot, ROWS : ROWS + 16, 0:D] = jnp.broadcast_to(
        jnp.sum(gsum[...], axis=0, keepdims=True), (16, D)
    ).astype(BF16)


def kernel_pack(s_ref, gain, weight_in, weight_out, out):
    groups = [weight_out[0, :, pl.ds(k * 256, 256)].astype(F32) for k in range(8)]
    across = jnp.concatenate(groups, axis=0).astype(BF16)
    along = jnp.broadcast_to(gain[...].astype(F32), (8, 32)).astype(BF16)
    for i in range(8):
        out[i, 0:32] = weight_in[0]
        out[i, 32:64] = across
        out[i, 64:72, 0:32] = along


def kernel_stats(s_ref, xs, hat, stat):
    c, zl = s_ref[2], s_ref[3]

    def keep_stat(rows, mean, recip_std):
        stat[0, rows, :] = spread(mean)
        stat[1, rows, :] = spread(recip_std)

    hat_pass(lambda rows: xs[zl, c, rows, :], hat, keep_stat)


def kernel_low_forward(s_ref, xs, hat0, *refs):
    pieces = refs[: 2 * PIECES]
    x1, x2, win, wout, stat1, pre, normed, hat1 = refs[2 * PIECES :]
    place_weights(s_ref, pieces, win, wout)
    c, zl = s_ref[2], s_ref[3]

    def keep_stat(rows, mean, recip_std):
        stat1[0, rows, :] = spread(mean)
        stat1[1, rows, :] = spread(recip_std)

    for par, hat in enumerate((hat0, hat1)):
        if par:
            hat_pass(lambda rows: x1[rows, :], hat1, keep_stat)
        gain = gain_row(wout, par)

        def step(rows, gain=gain, hat=hat):
            normed[rows, :] = (hat[rows, :] * gain).astype(BF16)

        over_rows(step)
        pre[par] = dot(normed[...], win[par].reshape(D, R))
        act = gelu_parts(pre[par])[1]
        if par:
            layer_out(lambda cols: x1[:, cols], act, wout, par, x2)
        else:
            layer_out(lambda cols: xs[zl, c, :, cols], act, wout, par, x1)


def kernel_high(s_ref, x2, cots, *refs):
    pieces = refs[: 2 * PIECES]
    up2, acts, win, wout, hat0, hat1, rstd, x3, up3, pre0, gnorm, gsum = refs[2 * PIECES :]
    place_weights(s_ref, pieces, win, wout)
    c, zl = s_ref[2], s_ref[3]
    gains = []
    for par, (src, hat) in enumerate(((x2, hat0), (x3, hat1))):

        def keep_stat(rows, mean, recip_std, par=par):
            rstd[par, rows, :] = spread(recip_std)

        hat_pass(lambda rows, src=src: src[rows, :], hat, keep_stat)
        gain = gain_row(wout, par)
        slot = jnp.where(c == par, 0, 1)

        def step(rows, gain=gain, hat=hat, slot=slot):
            acts[slot, rows, 0:D] = (hat[rows, :] * gain).astype(BF16)

        over_rows(step)
        preact = dot(acts[slot, 0:ROWS, 0:D], win[par].reshape(D, R))
        gains.append(gain)
        if par == 0:
            pre0[...] = preact
            layer_out(lambda cols: x2[:, cols], gelu_parts(preact)[1], wout, 0, x3)
    layer_back(
        lambda rows, cols: cots[zl, c, rows, cols],
        acts, jnp.where(c == 1, 0, 1), hat1, lambda rows: rstd[1, rows, 0:1],
        preact, win, wout, 1, gains[1], gnorm, gsum, up3,
    )
    layer_back(
        lambda rows, cols: up3[rows, cols],
        acts, jnp.where(c == 0, 0, 1), hat0, lambda rows: rstd[0, rows, 0:1],
        pre0[...], win, wout, 0, gains[0], gnorm, gsum, up2,
    )


def kernel_low_back(s_ref, xs, x1, up2, win, wout, stat0, stat1, pre, acts, hat, up1, gnorm, gsum):
    c, zl = s_ref[2], s_ref[3]
    for par, stat, up, up_out in ((1, stat1, up2, up1), (0, stat0, up1, None)):
        gain = gain_row(wout, par)
        slot = jnp.where(c == par, 0, 1)

        def step(rows, par=par, stat=stat, gain=gain, slot=slot):
            xf = (x1[rows, :] if par else xs[zl, c, rows, :]).astype(F32)
            hatted = (xf - stat[0, rows, 0:1]) * stat[1, rows, 0:1]
            hat[rows, :] = hatted
            acts[slot, rows, 0:D] = (hatted * gain).astype(BF16)

        over_rows(step)
        layer_back(
            lambda rows, cols, up=up: up[rows, cols],
            acts, slot, hat, lambda rows, stat=stat: stat[1, rows, 0:1],
            pre[par], win, wout, par, gain, gnorm, gsum, up_out,
        )


def kernel_grads(s_ref, acts, got, out, *pieces):
    mx, my, c = s_ref[0], s_ref[1], s_ref[2]
    places = []
    for xy in range(16):
        xr = (xy // 4 - mx) & 3
        yr = (xy % 4 - my) & 3
        places.append(jnp.where(c == 0, xr * 4 + yr, yr * 4 + xr))

    def both(start, size):
        cols = pl.ds(start, size)
        return jnp.concatenate([acts[0, 0:ROWS, cols], got[0:ROWS, cols]], axis=0)

    grad_pre = both(PRE_AT, R)
    for xy in range(16):
        block = dot(both(xy * 128, 128).T, grad_pre)
        out[places[xy], 0:8] = block.astype(BF16).reshape(8, 16, 256)
    act_t = both(ACT_AT, R).T
    for k in range(8):
        block = dot(act_t, both(UP_AT + k * 256, 256)).astype(BF16).reshape(16, 16, 256)
        for xy in range(16):
            out[places[xy], 8 + k] = block[xy]
    for xy in range(16):
        cols = pl.ds(xy * 128, 128)
        part = acts[0, ROWS : ROWS + 16, cols].astype(F32) + got[ROWS : ROWS + 16, cols].astype(F32)
        out[places[xy], 16] = jnp.concatenate([part, part], axis=1).astype(BF16)


    if len(pieces) == 2:
        pieces[0][...] = out[8:10]
        pieces[1][...] = out[10:12]
    else:
        for k in range(3):
            pieces[k][...] = out[4 * k + 4 : 4 * k + 8]


def over_groups(step):
    def body(g, carry):
        step(g)
        return carry

    lax.fori_loop(0, 17, body, 0)


def kernel_sides(s_ref, grads, up, down, after, before):
    def step(g):
        for i in range(2):
            after[i, g] = (grads[4 + i, g].astype(F32) + up[i, g].astype(F32)).astype(BF16)
            after[2 + i, g] = grads[6 + i, g]
            before[i, g] = grads[12 + i, g]
            before[2 + i, g] = (grads[14 + i, g].astype(F32) + down[i, g].astype(F32)).astype(BF16)

    over_groups(step)


def kernel_sum(s_ref, own, *refs):
    got, pieces = refs[:-4], refs[-4:]

    def step(g):
        for k in range(4):
            total = own[k, g].astype(F32)
            for part in got:
                total += part[k, g].astype(F32)
            pieces[k][g] = total.astype(BF16)

    over_groups(step)


def kernel_finish(s_ref, parts, gain, grad_in, grad_out):
    total = parts[0].astype(F32)
    for i in range(1, 8):
        total += parts[i].astype(F32)
    grad_in[0] = total[0:32]
    for k in range(8):
        grad_out[0, :, pl.ds(k * 256, 256)] = total[32 + 4 * k : 36 + 4 * k]
    gain[...] = total[64:65, 0:32]


def vmem(*shape, kind=BF16):
    return pltpu.VMEM(shape, kind)


def array(*shape, kind=BF16):
    return jax.ShapeDtypeStruct(shape, kind)


UNROLL = 8
SPANS = tuple((b, 0, 4) for b in range(4))
PIECES = len(SPANS)
UP_AT, ACT_AT, PRE_AT, WIDE = D, 2 * D, 2 * D + R, 2 * D + 2 * R
ACT = (ROWS, D)
WIN, WOUT = (2, 128, 16, 256), (2, 9, 16, 16, 256)
ACTS = (2, ROWS + 16, WIDE)
HAT = vmem(ROWS, D, kind=F32)
GSUM = vmem(CHUNK, D, kind=F32)
LOW_SCRATCH = [vmem(*ACT), HAT]
HIGH_SCRATCH = [
    vmem(*WIN), vmem(*WOUT), HAT, HAT, vmem(2, ROWS, 128, kind=F32),
    vmem(*ACT), vmem(*ACT), vmem(ROWS, R, kind=F32), HAT, GSUM,
]
BACK_SCRATCH = [HAT, vmem(*ACT), HAT, GSUM]
WHOLE = pl.BlockSpec(memory_space=pltpu.VMEM)


def call(body, scalars, args, out_shape, scratch):
    return pl.pallas_call(
        body,
        in_specs=[pl.BlockSpec(memory_space=pltpu.SMEM)] + [WHOLE] * len(args),
        out_specs=jax.tree.map(lambda s: WHOLE, out_shape),
        scratch_shapes=scratch,
        out_shape=out_shape,
        compiler_params=pltpu.CompilerParams(vmem_limit_bytes=20 * 1024 * 1024),
    )(scalars, *args)


def add_up(first, got):
    return functools.reduce(lambda p, q: p + q.astype(F32), got, first.astype(F32)).astype(BF16)


def scatter_first(scalars, acts, got):
    half = array(2, 17, 16, 256)
    grads, up, down = call(
        kernel_grads, scalars, [acts, got], [array(16, 17, 16, 256), half, half], []
    )
    return grads, shift(up, send_first(1)), shift(down, send_first(-1))


def scatter_direct(scalars, acts, got):
    row = array(4, 17, 16, 256)
    grads, *pieces = call(
        kernel_grads, scalars, [acts, got], [array(16, 17, 16, 256)] + [row] * 3, []
    )
    return [grads] + [shift(pieces[k - 1], send_first(k)) for k in (2, 1, 3)]


def scatter_sides(scalars, grads, up, down):
    row = array(4, 17, 16, 256)
    after, before = call(kernel_sides, scalars, [grads, up, down], [row, row], [])
    return grads, shift(after, send_first(1)), shift(before, send_first(-1))


def scatter_second(scalars, parts):
    piece = array(17, 16, 256)
    own, *pieces = call(kernel_sum, scalars, parts, [piece] * 4, [])
    got = [shift(pieces[k - 1], send_second(k)) for k in (2, 1, 3)]
    return add_up(own, got)


def device_body(inputs, cotangent, norm_gain, proj_in, proj_out):
    where = [lax.axis_index(n).astype(jnp.int32) for n in ("x", "y", "c", "zl")]
    scalars = jnp.stack(where)
    shard = call(kernel_pack, scalars, [norm_gain, proj_in, proj_out], array(8, 72, 256), [])
    column = lax.all_to_all(shard, ("zl", "zh"), 0, 0).reshape(2, 4, 72, 256)
    gain = jnp.pad(column[:, :, 64, :32].reshape(2, 1, 1, 128), ((0, 0), (0, 0), (0, 15), (0, 128)))
    block = jnp.concatenate(
        [
            column[:, :, :32].reshape(2, 8, 16, 256),
            column[:, :, 32:64].reshape(2, 4, 8, 4, 256).transpose(0, 2, 1, 3, 4).reshape(2, 8, 16, 256),
            gain,
        ],
        axis=1,
    )
    hat0, stat0 = call(
        kernel_stats, scalars, [inputs], [array(*ACT, kind=F32), array(2, ROWS, 128, kind=F32)], []
    )
    near = []
    for p in range(2):
        near.append([block[p]] + [shift(block[p], send_first(-k)) for k in (1, 2, 3)])
    pairs = []
    for p in range(2):
        row = jnp.stack(near[p])
        rows = [row] + [shift(row, send_second(-k)) for k in (1, 2, 3)]
        pairs.append(rows + [shift(v, SWAP) for v in rows])
    x1, x2, win, wout, stat1, pre = call(
        kernel_low_forward,
        scalars,
        [inputs, hat0, *pairs[0]],
        [
            array(*ACT), array(*ACT), array(*WIN), array(*WOUT),
            array(2, ROWS, 128, kind=F32), array(2, ROWS, R, kind=F32),
        ],
        LOW_SCRATCH,
    )
    up2, acts1 = call(
        kernel_high, scalars, [x2, cotangent, *pairs[1]], [array(*ACT), array(*ACTS)], HIGH_SCRATCH
    )
    got1 = shift(acts1[1], SWAP)
    acts0 = call(
        kernel_low_back,
        scalars,
        [inputs, x1, up2, win, wout, stat0, stat1, pre],
        array(*ACTS),
        BACK_SCRATCH,
    )
    got0 = shift(acts0[1], SWAP)
    sides1 = scatter_direct(scalars, acts1, got1)
    first0 = scatter_first(scalars, acts0, got0)
    sides0 = scatter_sides(scalars, *first0)
    high = scatter_second(scalars, sides1)
    low = scatter_second(scalars, sides0)
    grads = jnp.stack([low, high])
    parts = jnp.concatenate(
        [
            grads[:, :8].reshape(2, 4, 32, 256),
            grads[:, 8:16].reshape(2, 8, 4, 4, 256).transpose(0, 2, 1, 3, 4).reshape(2, 4, 32, 256),
            jnp.pad(grads[:, 16, 0, :128].reshape(2, 4, 1, 32), ((0, 0), (0, 0), (0, 7), (0, 224))),
        ],
        axis=2,
    ).reshape(8, 72, 256)
    return call(
        kernel_finish,
        scalars,
        [lax.all_to_all(parts, ("zl", "zh"), 0, 0)],
        (array(1, 32, kind=F32), array(1, 32, 256, kind=F32), array(1, 4, 2048, kind=F32)),
        [],
    )


def solution(mesh):
    fine = Mesh(mesh.devices.reshape(DIMS), AXES)
    zero = ("x", "y", "zh")
    segment = ("zl", "c")
    return jax.shard_map(
        device_body,
        mesh=fine,
        in_specs=(
            P(None, None, zero, None),
            P(None, None, zero, None),
            P(segment, zero),
            P(segment, zero, None),
            P(segment, zero, None),
        ),
        out_specs=(P(segment, zero), P(segment, zero, None), P(segment, zero, None)),
        check_vma=False,
    )
```

```python
import functools
import itertools

import jax
import jax.numpy as jnp
import numpy as np
from jax import lax
from jax.experimental import pallas as pl
from jax.experimental.pallas import tpu as pltpu
from jax.sharding import Mesh
from jax.sharding import PartitionSpec as P


gelu_coeff = 0.7978845608028654
cubic_coeff = 0.044715
norm_eps = 1e-05

AXES = ("zl", "c", "x", "y", "zh")
DIMS = (2, 2, 4, 4, 4)
D = 2048
R = 256
ROWS = 128
CHUNK = 16
F32 = jnp.float32
BF16 = jnp.bfloat16


def flat_perm(move):
    pairs = []
    for src, coords in enumerate(itertools.product(*[range(n) for n in DIMS])):
        dst = [v % n for v, n in zip(move(*coords), DIMS)]
        pairs.append((src, int(np.ravel_multi_index(dst, DIMS))))
    return pairs


def send_first(k):
    return flat_perm(
        lambda zl, c, x, y, zh: (zl, c, x + k, y, zh) if c == 0 else (zl, c, x, y + k, zh)
    )


def send_second(k):
    return flat_perm(
        lambda zl, c, x, y, zh: (zl, c, x, y + k, zh) if c == 0 else (zl, c, x + k, y, zh)
    )


SWAP = flat_perm(lambda zl, c, x, y, zh: (zl, c + 1, x, y, zh))


def shift(value, pairs):
    return lax.ppermute(value, AXES, pairs)


def dot(left, right, left_dim=1, right_dim=0):
    return lax.dot_general(
        left, right, (((left_dim,), (right_dim,)), ((), ())), preferred_element_type=F32
    )


def gelu_parts(v):
    inner = jnp.tanh(gelu_coeff * (v + cubic_coeff * v * v * v))
    return inner, (0.5 * v * (1.0 + inner)).astype(BF16)


def gelu_slope(v, inner):
    return 0.5 * (1.0 + inner) + 0.5 * v * (1.0 - inner * inner) * gelu_coeff * (
        1.0 + 3.0 * cubic_coeff * v * v
    )


def place_weights(s_ref, pieces, win, wout):
    mx, my, c = s_ref[0], s_ref[1], s_ref[2]
    for o in range(2):
        par = c if o == 0 else 1 - c
        for src, (b, first, count) in zip(pieces[o * PIECES : (o + 1) * PIECES], SPANS):

            def place(i, carry, par=par, src=src, b=b, first=first):
                a = first + i
                x = (mx + jnp.where(par == 0, a, b)) & 3
                y = (my + jnp.where(par == 0, b, a)) & 3
                xy = x * 4 + y
                win[par, pl.ds(xy * 8, 8)] = src[i, 0:8]
                for k in range(9):
                    wout[par, k, xy] = src[i, 8 + k]
                return carry

            lax.fori_loop(0, count, place, 0)


def gain_row(wout, par):
    return jnp.concatenate(
        [wout[par, 8, xy, 0:1, 0:128] for xy in range(16)], axis=1
    ).astype(F32)


def over_rows(step):
    def body(i, carry):
        step(pl.ds(pl.multiple_of(i * CHUNK, CHUNK), CHUNK))
        return carry

    lax.fori_loop(0, ROWS // CHUNK, body, 0, unroll=UNROLL)


def hat_pass(x_at, hat, keep_stat):
    def step(rows):
        xf = x_at(rows).astype(F32)
        mean = jnp.mean(xf, axis=-1, keepdims=True)
        centered = xf - mean
        variance = jnp.mean(centered * centered, axis=-1, keepdims=True)
        recip_std = lax.rsqrt(variance + norm_eps)
        hat[rows, :] = centered * recip_std
        keep_stat(rows, mean, recip_std)

    over_rows(step)


def spread(column):
    return jnp.broadcast_to(column, (CHUNK, 128))


def layer_out(x_at, act, wout, par, out_ref):
    for k in range(8):
        cols = pl.ds(k * 256, 256)
        out_ref[:, cols] = (
            x_at(cols).astype(F32) + dot(act, wout[par, k].reshape(R, 256))
        ).astype(BF16)


def layer_back(up_at, acts, slot, hat, rstd_at, preact, win, wout, par, gain, gnorm, gsum, up_out):
    inner, act = gelu_parts(preact)
    grad_act = jnp.zeros((ROWS, R), F32)
    for k in range(8):
        grad_act += dot(
            up_at(pl.ds(0, ROWS), pl.ds(k * 256, 256)), wout[par, k].reshape(R, 256), 1, 1
        )
    grad_pre = (grad_act * gelu_slope(preact, inner)).astype(BF16)
    acts[slot, 0:ROWS, ACT_AT : ACT_AT + R] = act
    acts[slot, 0:ROWS, PRE_AT : PRE_AT + R] = grad_pre
    for k in range(8):
        gnorm[:, pl.ds(k * 256, 256)] = dot(
            grad_pre, win[par, pl.ds(k * 16, 16)].reshape(256, R), 1, 1
        )
    gsum[...] = jnp.zeros((CHUNK, D), F32)

    def step(rows):
        grad_normed = gnorm[rows, :]
        hatted = hat[rows, :]
        product = grad_normed * hatted
        gsum[...] += product
        up = up_at(rows, pl.ds(0, D))
        acts[slot, rows, UP_AT : UP_AT + D] = up
        if up_out is not None:
            grad_hat = grad_normed * gain
            mean_hat = jnp.mean(grad_hat, axis=-1, keepdims=True)
            mean_both = jnp.mean(product * gain, axis=-1, keepdims=True)
            through = rstd_at(rows) * (grad_hat - mean_hat - hatted * mean_both)
            up_out[rows, :] = (up.astype(F32) + through).astype(BF16)

    over_rows(step)
    acts[slot, ROWS : ROWS + 16, 0:D] = jnp.broadcast_to(
        jnp.sum(gsum[...], axis=0, keepdims=True), (16, D)
    ).astype(BF16)


def kernel_stats(s_ref, xs, hat, stat):
    c, zl = s_ref[2], s_ref[3]

    def keep_stat(rows, mean, recip_std):
        stat[0, rows, :] = spread(mean)
        stat[1, rows, :] = spread(recip_std)

    hat_pass(lambda rows: xs[zl, c, rows, :], hat, keep_stat)


def kernel_low_forward(s_ref, xs, hat0, *refs):
    pieces = refs[: 2 * PIECES]
    x1, x2, win, wout, stat1, pre, normed, hat1 = refs[2 * PIECES :]
    place_weights(s_ref, pieces, win, wout)
    c, zl = s_ref[2], s_ref[3]

    def keep_stat(rows, mean, recip_std):
        stat1[0, rows, :] = spread(mean)
        stat1[1, rows, :] = spread(recip_std)

    for par, hat in enumerate((hat0, hat1)):
        if par:
            hat_pass(lambda rows: x1[rows, :], hat1, keep_stat)
        gain = gain_row(wout, par)

        def step(rows, gain=gain, hat=hat):
            normed[rows, :] = (hat[rows, :] * gain).astype(BF16)

        over_rows(step)
        pre[par] = dot(normed[...], win[par].reshape(D, R))
        act = gelu_parts(pre[par])[1]
        if par:
            layer_out(lambda cols: x1[:, cols], act, wout, par, x2)
        else:
            layer_out(lambda cols: xs[zl, c, :, cols], act, wout, par, x1)


def kernel_high(s_ref, x2, cots, *refs):
    pieces = refs[: 2 * PIECES]
    up2, acts, win, wout, hat0, hat1, rstd, x3, up3, pre0, gnorm, gsum = refs[2 * PIECES :]
    place_weights(s_ref, pieces, win, wout)
    c, zl = s_ref[2], s_ref[3]
    gains = []
    for par, (src, hat) in enumerate(((x2, hat0), (x3, hat1))):

        def keep_stat(rows, mean, recip_std, par=par):
            rstd[par, rows, :] = spread(recip_std)

        hat_pass(lambda rows, src=src: src[rows, :], hat, keep_stat)
        gain = gain_row(wout, par)
        slot = jnp.where(c == par, 0, 1)

        def step(rows, gain=gain, hat=hat, slot=slot):
            acts[slot, rows, 0:D] = (hat[rows, :] * gain).astype(BF16)

        over_rows(step)
        preact = dot(acts[slot, 0:ROWS, 0:D], win[par].reshape(D, R))
        gains.append(gain)
        if par == 0:
            pre0[...] = preact
            layer_out(lambda cols: x2[:, cols], gelu_parts(preact)[1], wout, 0, x3)
    layer_back(
        lambda rows, cols: cots[zl, c, rows, cols],
        acts, jnp.where(c == 1, 0, 1), hat1, lambda rows: rstd[1, rows, 0:1],
        preact, win, wout, 1, gains[1], gnorm, gsum, up3,
    )
    layer_back(
        lambda rows, cols: up3[rows, cols],
        acts, jnp.where(c == 0, 0, 1), hat0, lambda rows: rstd[0, rows, 0:1],
        pre0[...], win, wout, 0, gains[0], gnorm, gsum, up2,
    )


def kernel_low_back(s_ref, xs, x1, up2, win, wout, stat0, stat1, pre, acts, hat, up1, gnorm, gsum):
    c, zl = s_ref[2], s_ref[3]
    for par, stat, up, up_out in ((1, stat1, up2, up1), (0, stat0, up1, None)):
        gain = gain_row(wout, par)
        slot = jnp.where(c == par, 0, 1)

        def step(rows, par=par, stat=stat, gain=gain, slot=slot):
            xf = (x1[rows, :] if par else xs[zl, c, rows, :]).astype(F32)
            hatted = (xf - stat[0, rows, 0:1]) * stat[1, rows, 0:1]
            hat[rows, :] = hatted
            acts[slot, rows, 0:D] = (hatted * gain).astype(BF16)

        over_rows(step)
        layer_back(
            lambda rows, cols, up=up: up[rows, cols],
            acts, slot, hat, lambda rows, stat=stat: stat[1, rows, 0:1],
            pre[par], win, wout, par, gain, gnorm, gsum, up_out,
        )


def kernel_grads(s_ref, acts, got, out, up, down):
    mx, my, c = s_ref[0], s_ref[1], s_ref[2]
    places = []
    for xy in range(16):
        xr = (xy // 4 - mx) & 3
        yr = (xy % 4 - my) & 3
        places.append(jnp.where(c == 0, xr * 4 + yr, yr * 4 + xr))

    def both(start, size):
        cols = pl.ds(start, size)
        return jnp.concatenate([acts[0, 0:ROWS, cols], got[0:ROWS, cols]], axis=0)

    grad_pre = both(PRE_AT, R)
    for xy in range(16):
        block = dot(both(xy * 128, 128).T, grad_pre)
        out[places[xy], 0:8] = block.astype(BF16).reshape(8, 16, 256)
    act_t = both(ACT_AT, R).T
    for k in range(8):
        block = dot(act_t, both(UP_AT + k * 256, 256)).astype(BF16).reshape(16, 16, 256)
        for xy in range(16):
            out[places[xy], 8 + k] = block[xy]
    for xy in range(16):
        cols = pl.ds(xy * 128, 128)
        part = acts[0, ROWS : ROWS + 16, cols].astype(F32) + got[ROWS : ROWS + 16, cols].astype(F32)
        out[places[xy], 16] = jnp.concatenate([part, part], axis=1).astype(BF16)


    up[...] = out[8:10]
    down[...] = out[10:12]


def over_groups(step):
    def body(g, carry):
        step(g)
        return carry

    lax.fori_loop(0, 17, body, 0)


def kernel_sides(s_ref, grads, up, down, after, before):
    def step(g):
        for i in range(2):
            after[i, g] = (grads[4 + i, g].astype(F32) + up[i, g].astype(F32)).astype(BF16)
            after[2 + i, g] = grads[6 + i, g]
            before[i, g] = grads[12 + i, g]
            before[2 + i, g] = (grads[14 + i, g].astype(F32) + down[i, g].astype(F32)).astype(BF16)

    over_groups(step)


def kernel_sum(s_ref, own, a, b, *pieces):
    def step(g):
        for k in range(4):
            pieces[k][g] = (
                own[k, g].astype(F32) + a[k, g].astype(F32) + b[k, g].astype(F32)
            ).astype(BF16)

    over_groups(step)


def kernel_finish(s_ref, parts, gain, grad_in, grad_out):
    total = parts[0].astype(F32)
    for i in range(1, 8):
        total += parts[i].astype(F32)
    grad_in[0] = total[0:32]
    for k in range(8):
        grad_out[0, :, pl.ds(k * 256, 256)] = total[32 + 4 * k : 36 + 4 * k]
    gain[...] = total[64:65, 0:32]


def vmem(*shape, kind=BF16):
    return pltpu.VMEM(shape, kind)


def array(*shape, kind=BF16):
    return jax.ShapeDtypeStruct(shape, kind)


UNROLL = 8
SPANS = tuple((b, 0, 4) for b in range(4))
PIECES = len(SPANS)
UP_AT, ACT_AT, PRE_AT, WIDE = D, 2 * D, 2 * D + R, 2 * D + 2 * R
ACT = (ROWS, D)
WIN, WOUT = (2, 128, 16, 256), (2, 9, 16, 16, 256)
ACTS = (2, ROWS + 16, WIDE)
HAT = vmem(ROWS, D, kind=F32)
GSUM = vmem(CHUNK, D, kind=F32)
LOW_SCRATCH = [vmem(*ACT), HAT]
HIGH_SCRATCH = [
    vmem(*WIN), vmem(*WOUT), HAT, HAT, vmem(2, ROWS, 128, kind=F32),
    vmem(*ACT), vmem(*ACT), vmem(ROWS, R, kind=F32), HAT, GSUM,
]
BACK_SCRATCH = [HAT, vmem(*ACT), HAT, GSUM]
WHOLE = pl.BlockSpec(memory_space=pltpu.VMEM)


def call(body, scalars, args, out_shape, scratch):
    return pl.pallas_call(
        body,
        in_specs=[pl.BlockSpec(memory_space=pltpu.SMEM)] + [WHOLE] * len(args),
        out_specs=jax.tree.map(lambda s: WHOLE, out_shape),
        scratch_shapes=scratch,
        out_shape=out_shape,
        compiler_params=pltpu.CompilerParams(vmem_limit_bytes=20 * 1024 * 1024),
    )(scalars, *args)


def add_up(first, got):
    return functools.reduce(lambda p, q: p + q.astype(F32), got, first.astype(F32)).astype(BF16)


def scatter_first(scalars, acts, got):
    half = array(2, 17, 16, 256)
    grads, up, down = call(
        kernel_grads, scalars, [acts, got], [array(16, 17, 16, 256), half, half], []
    )
    return grads, shift(up, send_first(1)), shift(down, send_first(-1))


def scatter_sides(scalars, grads, up, down):
    row = array(4, 17, 16, 256)
    after, before = call(kernel_sides, scalars, [grads, up, down], [row, row], [])
    return grads, shift(after, send_first(1)), shift(before, send_first(-1))


def scatter_second(scalars, parts):
    piece = array(17, 16, 256)
    own, *pieces = call(kernel_sum, scalars, parts, [piece] * 4, [])
    got = [shift(pieces[k - 1], send_second(k)) for k in (2, 1, 3)]
    return add_up(own, got)


def device_body(inputs, cotangent, norm_gain, proj_in, proj_out):
    where = [lax.axis_index(n).astype(jnp.int32) for n in ("x", "y", "c", "zl")]
    scalars = jnp.stack(where)
    shard = jnp.concatenate(
        [
            proj_in[0],
            proj_out[0].reshape(4, 8, 256).transpose(1, 0, 2).reshape(32, 256),
            jnp.pad(norm_gain, ((0, 7), (0, 224))),
        ],
        axis=0,
    )
    column = lax.all_to_all(
        jnp.broadcast_to(shard[None], (8, 72, 256)), ("zl", "zh"), 0, 0
    ).reshape(2, 4, 72, 256)
    gain = jnp.pad(column[:, :, 64, :32].reshape(2, 1, 1, 128), ((0, 0), (0, 0), (0, 15), (0, 128)))
    block = jnp.concatenate(
        [
            column[:, :, :32].reshape(2, 8, 16, 256),
            column[:, :, 32:64].reshape(2, 4, 8, 4, 256).transpose(0, 2, 1, 3, 4).reshape(2, 8, 16, 256),
            gain,
        ],
        axis=1,
    )
    hat0, stat0 = call(
        kernel_stats, scalars, [inputs], [array(*ACT, kind=F32), array(2, ROWS, 128, kind=F32)], []
    )
    near = []
    for p in range(2):
        near.append([block[p]] + [shift(block[p], send_first(-k)) for k in (1, 2, 3)])
    pairs = []
    for p in range(2):
        row = jnp.stack(near[p])
        rows = [row] + [shift(row, send_second(-k)) for k in (1, 2, 3)]
        pairs.append(rows + [shift(v, SWAP) for v in rows])
    x1, x2, win, wout, stat1, pre = call(
        kernel_low_forward,
        scalars,
        [inputs, hat0, *pairs[0]],
        [
            array(*ACT), array(*ACT), array(*WIN), array(*WOUT),
            array(2, ROWS, 128, kind=F32), array(2, ROWS, R, kind=F32),
        ],
        LOW_SCRATCH,
    )
    up2, acts1 = call(
        kernel_high, scalars, [x2, cotangent, *pairs[1]], [array(*ACT), array(*ACTS)], HIGH_SCRATCH
    )
    got1 = shift(acts1[1], SWAP)
    acts0 = call(
        kernel_low_back,
        scalars,
        [inputs, x1, up2, win, wout, stat0, stat1, pre],
        array(*ACTS),
        BACK_SCRATCH,
    )
    got0 = shift(acts0[1], SWAP)
    first1 = scatter_first(scalars, acts1, got1)
    first0 = scatter_first(scalars, acts0, got0)
    sides1 = scatter_sides(scalars, *first1)
    sides0 = scatter_sides(scalars, *first0)
    high = scatter_second(scalars, sides1)
    low = scatter_second(scalars, sides0)
    grads = jnp.stack([low, high])
    parts = jnp.concatenate(
        [
            grads[:, :8].reshape(2, 4, 32, 256),
            grads[:, 8:16].reshape(2, 8, 4, 4, 256).transpose(0, 2, 1, 3, 4).reshape(2, 4, 32, 256),
            jnp.pad(grads[:, 16, 0, :128].reshape(2, 4, 1, 32), ((0, 0), (0, 0), (0, 7), (0, 224))),
        ],
        axis=2,
    ).reshape(8, 72, 256)
    return call(
        kernel_finish,
        scalars,
        [lax.all_to_all(parts, ("zl", "zh"), 0, 0)],
        (array(1, 32, kind=F32), array(1, 32, 256, kind=F32), array(1, 4, 2048, kind=F32)),
        [],
    )


def solution(mesh):
    fine = Mesh(mesh.devices.reshape(DIMS), AXES)
    zero = ("x", "y", "zh")
    segment = ("zl", "c")
    return jax.shard_map(
        device_body,
        mesh=fine,
        in_specs=(
            P(None, None, zero, None),
            P(None, None, zero, None),
            P(segment, zero),
            P(segment, zero, None),
            P(segment, zero, None),
        ),
        out_specs=(P(segment, zero), P(segment, zero, None), P(segment, zero, None)),
        check_vma=False,
    )
```

```python
import functools
import itertools

import jax
import jax.numpy as jnp
import numpy as np
from jax import lax
from jax.experimental import pallas as pl
from jax.experimental.pallas import tpu as pltpu
from jax.sharding import Mesh
from jax.sharding import PartitionSpec as P


gelu_coeff = 0.7978845608028654
cubic_coeff = 0.044715
norm_eps = 1e-05

AXES = ("zl", "c", "x", "y", "zh")
DIMS = (2, 2, 4, 4, 4)
D = 2048
R = 256
ROWS = 128
CHUNK = 16
F32 = jnp.float32
BF16 = jnp.bfloat16


def flat_perm(move):
    pairs = []
    for src, coords in enumerate(itertools.product(*[range(n) for n in DIMS])):
        dst = [v % n for v, n in zip(move(*coords), DIMS)]
        pairs.append((src, int(np.ravel_multi_index(dst, DIMS))))
    return pairs


def send_first(k):
    return flat_perm(
        lambda zl, c, x, y, zh: (zl, c, x + k, y, zh) if c == 0 else (zl, c, x, y + k, zh)
    )


def send_second(k):
    return flat_perm(
        lambda zl, c, x, y, zh: (zl, c, x, y + k, zh) if c == 0 else (zl, c, x + k, y, zh)
    )


SWAP = flat_perm(lambda zl, c, x, y, zh: (zl, c + 1, x, y, zh))


def shift(value, pairs):
    return lax.ppermute(value, AXES, pairs)


def dot(left, right, left_dim=1, right_dim=0):
    return lax.dot_general(
        left, right, (((left_dim,), (right_dim,)), ((), ())), preferred_element_type=F32
    )


def gelu_parts(v):
    inner = jnp.tanh(gelu_coeff * (v + cubic_coeff * v * v * v))
    return inner, (0.5 * v * (1.0 + inner)).astype(BF16)


def gelu_slope(v, inner):
    return 0.5 * (1.0 + inner) + 0.5 * v * (1.0 - inner * inner) * gelu_coeff * (
        1.0 + 3.0 * cubic_coeff * v * v
    )


def place_weights(s_ref, pieces, win, wout):
    mx, my, c = s_ref[0], s_ref[1], s_ref[2]
    for o in range(2):
        par = c if o == 0 else 1 - c
        for src, (b, first, count) in zip(pieces[o * PIECES : (o + 1) * PIECES], SPANS):

            def place(i, carry, par=par, src=src, b=b, first=first):
                a = first + i
                x = (mx + jnp.where(par == 0, a, b)) & 3
                y = (my + jnp.where(par == 0, b, a)) & 3
                xy = x * 4 + y
                win[par, pl.ds(xy * 8, 8)] = src[i, 0:8]
                for k in range(9):
                    wout[par, k, xy] = src[i, 8 + k]
                return carry

            lax.fori_loop(0, count, place, 0)


def gain_row(wout, par):
    return jnp.concatenate(
        [wout[par, 8, xy, 0:1, 0:128] for xy in range(16)], axis=1
    ).astype(F32)


def over_rows(step):
    def body(i, carry):
        step(pl.ds(pl.multiple_of(i * CHUNK, CHUNK), CHUNK))
        return carry

    lax.fori_loop(0, ROWS // CHUNK, body, 0, unroll=UNROLL)


def hat_pass(x_at, hat, keep_stat):
    def step(rows):
        xf = x_at(rows).astype(F32)
        mean = jnp.mean(xf, axis=-1, keepdims=True)
        centered = xf - mean
        variance = jnp.mean(centered * centered, axis=-1, keepdims=True)
        recip_std = lax.rsqrt(variance + norm_eps)
        hat[rows, :] = centered * recip_std
        keep_stat(rows, mean, recip_std)

    over_rows(step)


def spread(column):
    return jnp.broadcast_to(column, (CHUNK, 128))


def layer_out(x_at, act, wout, par, out_ref):
    for k in range(8):
        cols = pl.ds(k * 256, 256)
        out_ref[:, cols] = (
            x_at(cols).astype(F32) + dot(act, wout[par, k].reshape(R, 256))
        ).astype(BF16)


def layer_back(up_at, acts, slot, hat, rstd_at, preact, win, wout, par, gain, gnorm, gsum, up_out):
    inner, act = gelu_parts(preact)
    grad_act = jnp.zeros((ROWS, R), F32)
    for k in range(8):
        grad_act += dot(
            up_at(pl.ds(0, ROWS), pl.ds(k * 256, 256)), wout[par, k].reshape(R, 256), 1, 1
        )
    grad_pre = (grad_act * gelu_slope(preact, inner)).astype(BF16)
    acts[slot, 0:ROWS, ACT_AT : ACT_AT + R] = act
    acts[slot, 0:ROWS, PRE_AT : PRE_AT + R] = grad_pre
    for k in range(8):
        gnorm[:, pl.ds(k * 256, 256)] = dot(
            grad_pre, win[par, pl.ds(k * 16, 16)].reshape(256, R), 1, 1
        )
    gsum[...] = jnp.zeros((CHUNK, D), F32)

    def step(rows):
        grad_normed = gnorm[rows, :]
        hatted = hat[rows, :]
        product = grad_normed * hatted
        gsum[...] += product
        up = up_at(rows, pl.ds(0, D))
        acts[slot, rows, UP_AT : UP_AT + D] = up
        if up_out is not None:
            grad_hat = grad_normed * gain
            mean_hat = jnp.mean(grad_hat, axis=-1, keepdims=True)
            mean_both = jnp.mean(product * gain, axis=-1, keepdims=True)
            through = rstd_at(rows) * (grad_hat - mean_hat - hatted * mean_both)
            up_out[rows, :] = (up.astype(F32) + through).astype(BF16)

    over_rows(step)
    acts[slot, ROWS : ROWS + 16, 0:D] = jnp.broadcast_to(
        jnp.sum(gsum[...], axis=0, keepdims=True), (16, D)
    ).astype(BF16)


def kernel_stats(s_ref, xs, hat, stat):
    c, zl = s_ref[2], s_ref[3]

    def keep_stat(rows, mean, recip_std):
        stat[0, rows, :] = spread(mean)
        stat[1, rows, :] = spread(recip_std)

    hat_pass(lambda rows: xs[zl, c, rows, :], hat, keep_stat)


def kernel_halves(s_ref, after, before, low, high):
    low[...] = after[0:2]
    high[...] = before[2:4]


def kernel_low_forward(s_ref, xs, hat0, *refs):
    pieces = refs[: 2 * PIECES]
    x1, x2, win, wout, stat1, pre, normed, hat1 = refs[2 * PIECES :]
    place_weights(s_ref, pieces, win, wout)
    c, zl = s_ref[2], s_ref[3]

    def keep_stat(rows, mean, recip_std):
        stat1[0, rows, :] = spread(mean)
        stat1[1, rows, :] = spread(recip_std)

    for par, hat in enumerate((hat0, hat1)):
        if par:
            hat_pass(lambda rows: x1[rows, :], hat1, keep_stat)
        gain = gain_row(wout, par)

        def step(rows, gain=gain, hat=hat):
            normed[rows, :] = (hat[rows, :] * gain).astype(BF16)

        over_rows(step)
        pre[par] = dot(normed[...], win[par].reshape(D, R))
        act = gelu_parts(pre[par])[1]
        if par:
            layer_out(lambda cols: x1[:, cols], act, wout, par, x2)
        else:
            layer_out(lambda cols: xs[zl, c, :, cols], act, wout, par, x1)


def kernel_high(s_ref, x2, cots, *refs):
    pieces = refs[: 2 * PIECES]
    up2, acts, win, wout, hat0, hat1, rstd, x3, up3, pre0, gnorm, gsum = refs[2 * PIECES :]
    place_weights(s_ref, pieces, win, wout)
    c, zl = s_ref[2], s_ref[3]
    gains = []
    for par, (src, hat) in enumerate(((x2, hat0), (x3, hat1))):

        def keep_stat(rows, mean, recip_std, par=par):
            rstd[par, rows, :] = spread(recip_std)

        hat_pass(lambda rows, src=src: src[rows, :], hat, keep_stat)
        gain = gain_row(wout, par)
        slot = jnp.where(c == par, 0, 1)

        def step(rows, gain=gain, hat=hat, slot=slot):
            acts[slot, rows, 0:D] = (hat[rows, :] * gain).astype(BF16)

        over_rows(step)
        preact = dot(acts[slot, 0:ROWS, 0:D], win[par].reshape(D, R))
        gains.append(gain)
        if par == 0:
            pre0[...] = preact
            layer_out(lambda cols: x2[:, cols], gelu_parts(preact)[1], wout, 0, x3)
    layer_back(
        lambda rows, cols: cots[zl, c, rows, cols],
        acts, jnp.where(c == 1, 0, 1), hat1, lambda rows: rstd[1, rows, 0:1],
        preact, win, wout, 1, gains[1], gnorm, gsum, up3,
    )
    layer_back(
        lambda rows, cols: up3[rows, cols],
        acts, jnp.where(c == 0, 0, 1), hat0, lambda rows: rstd[0, rows, 0:1],
        pre0[...], win, wout, 0, gains[0], gnorm, gsum, up2,
    )


def kernel_low_back(s_ref, xs, x1, up2, win, wout, stat0, stat1, pre, acts, hat, up1, gnorm, gsum):
    c, zl = s_ref[2], s_ref[3]
    for par, stat, up, up_out in ((1, stat1, up2, up1), (0, stat0, up1, None)):
        gain = gain_row(wout, par)
        slot = jnp.where(c == par, 0, 1)

        def step(rows, par=par, stat=stat, gain=gain, slot=slot):
            xf = (x1[rows, :] if par else xs[zl, c, rows, :]).astype(F32)
            hatted = (xf - stat[0, rows, 0:1]) * stat[1, rows, 0:1]
            hat[rows, :] = hatted
            acts[slot, rows, 0:D] = (hatted * gain).astype(BF16)

        over_rows(step)
        layer_back(
            lambda rows, cols, up=up: up[rows, cols],
            acts, slot, hat, lambda rows, stat=stat: stat[1, rows, 0:1],
            pre[par], win, wout, par, gain, gnorm, gsum, up_out,
        )


def kernel_grads(s_ref, acts, got, out, up, down):
    mx, my, c = s_ref[0], s_ref[1], s_ref[2]
    places = []
    for xy in range(16):
        xr = (xy // 4 - mx) & 3
        yr = (xy % 4 - my) & 3
        places.append(jnp.where(c == 0, xr * 4 + yr, yr * 4 + xr))

    def both(start, size):
        cols = pl.ds(start, size)
        return jnp.concatenate([acts[0, 0:ROWS, cols], got[0:ROWS, cols]], axis=0)

    grad_pre = both(PRE_AT, R)
    for xy in range(16):
        block = dot(both(xy * 128, 128).T, grad_pre)
        out[places[xy], 0:8] = block.astype(BF16).reshape(8, 16, 256)
    act_t = both(ACT_AT, R).T
    for k in range(8):
        block = dot(act_t, both(UP_AT + k * 256, 256)).astype(BF16).reshape(16, 16, 256)
        for xy in range(16):
            out[places[xy], 8 + k] = block[xy]
    for xy in range(16):
        cols = pl.ds(xy * 128, 128)
        part = acts[0, ROWS : ROWS + 16, cols].astype(F32) + got[ROWS : ROWS + 16, cols].astype(F32)
        out[places[xy], 16] = jnp.concatenate([part, part], axis=1).astype(BF16)


    up[...] = out[8:10]
    down[...] = out[10:12]


def over_groups(step):
    def body(g, carry):
        step(g)
        return carry

    lax.fori_loop(0, 17, body, 0)


def kernel_sides(s_ref, grads, up, down, after, before):
    def step(g):
        for i in range(2):
            after[i, g] = (grads[4 + i, g].astype(F32) + up[i, g].astype(F32)).astype(BF16)
            after[2 + i, g] = grads[6 + i, g]
            before[i, g] = grads[12 + i, g]
            before[2 + i, g] = (grads[14 + i, g].astype(F32) + down[i, g].astype(F32)).astype(BF16)

    over_groups(step)


def kernel_sum(s_ref, low, low_a, low_b, high, high_a, high_b, *pieces):
    def step(g):
        for p, (own, a, b) in enumerate(((low, low_a, low_b), (high, high_a, high_b))):
            for k in range(4):
                pieces[k][p, g] = (
                    own[k, g].astype(F32) + a[k, g].astype(F32) + b[k, g].astype(F32)
                ).astype(BF16)

    over_groups(step)


def kernel_finish(s_ref, parts, gain, grad_in, grad_out):
    total = parts[0].astype(F32)
    for i in range(1, 8):
        total += parts[i].astype(F32)
    grad_in[0] = total[0:32]
    for k in range(8):
        grad_out[0, :, pl.ds(k * 256, 256)] = total[32 + 4 * k : 36 + 4 * k]
    gain[...] = total[64:65, 0:32]


def vmem(*shape, kind=BF16):
    return pltpu.VMEM(shape, kind)


def array(*shape, kind=BF16):
    return jax.ShapeDtypeStruct(shape, kind)


UNROLL = 8
SPANS = ((0, 0, 4), (1, 0, 4), (3, 0, 4), (2, 0, 2), (2, 2, 2))
PIECES = len(SPANS)
UP_AT, ACT_AT, PRE_AT, WIDE = D, 2 * D, 2 * D + R, 2 * D + 2 * R
ACT = (ROWS, D)
WIN, WOUT = (2, 128, 16, 256), (2, 9, 16, 16, 256)
ACTS = (2, ROWS + 16, WIDE)
HAT = vmem(ROWS, D, kind=F32)
GSUM = vmem(CHUNK, D, kind=F32)
LOW_SCRATCH = [vmem(*ACT), HAT]
HIGH_SCRATCH = [
    vmem(*WIN), vmem(*WOUT), HAT, HAT, vmem(2, ROWS, 128, kind=F32),
    vmem(*ACT), vmem(*ACT), vmem(ROWS, R, kind=F32), HAT, GSUM,
]
BACK_SCRATCH = [HAT, vmem(*ACT), HAT, GSUM]
WHOLE = pl.BlockSpec(memory_space=pltpu.VMEM)


def call(body, scalars, args, out_shape, scratch):
    return pl.pallas_call(
        body,
        in_specs=[pl.BlockSpec(memory_space=pltpu.SMEM)] + [WHOLE] * len(args),
        out_specs=jax.tree.map(lambda s: WHOLE, out_shape),
        scratch_shapes=scratch,
        out_shape=out_shape,
        compiler_params=pltpu.CompilerParams(vmem_limit_bytes=20 * 1024 * 1024),
    )(scalars, *args)


def add_up(first, got):
    return functools.reduce(lambda p, q: p + q.astype(F32), got, first.astype(F32)).astype(BF16)


def scatter_first(scalars, acts, got):
    half = array(2, 17, 16, 256)
    grads, up, down = call(
        kernel_grads, scalars, [acts, got], [array(16, 17, 16, 256), half, half], []
    )
    return grads, shift(up, send_first(1)), shift(down, send_first(-1))


def scatter_sides(scalars, grads, up, down):
    row = array(4, 17, 16, 256)
    after, before = call(kernel_sides, scalars, [grads, up, down], [row, row], [])
    return grads, shift(after, send_first(1)), shift(before, send_first(-1))


def scatter_second(scalars, low, high):
    piece = array(2, 17, 16, 256)
    own, *pieces = call(kernel_sum, scalars, [*low, *high], [piece] * 4, [])
    got = [shift(pieces[k - 1], send_second(k)) for k in (2, 1, 3)]
    return add_up(own, got)


def device_body(inputs, cotangent, norm_gain, proj_in, proj_out):
    where = [lax.axis_index(n).astype(jnp.int32) for n in ("x", "y", "c", "zl")]
    scalars = jnp.stack(where)
    shard = jnp.concatenate(
        [
            proj_in[0],
            proj_out[0].reshape(4, 8, 256).transpose(1, 0, 2).reshape(32, 256),
            jnp.pad(norm_gain, ((0, 7), (0, 224))),
        ],
        axis=0,
    )
    column = lax.all_to_all(
        jnp.broadcast_to(shard[None], (8, 72, 256)), ("zl", "zh"), 0, 0
    ).reshape(2, 4, 72, 256)
    gain = jnp.pad(column[:, :, 64, :32].reshape(2, 1, 1, 128), ((0, 0), (0, 0), (0, 15), (0, 128)))
    block = jnp.concatenate(
        [
            column[:, :, :32].reshape(2, 8, 16, 256),
            column[:, :, 32:64].reshape(2, 4, 8, 4, 256).transpose(0, 2, 1, 3, 4).reshape(2, 8, 16, 256),
            gain,
        ],
        axis=1,
    )
    hat0, stat0 = call(
        kernel_stats, scalars, [inputs], [array(*ACT, kind=F32), array(2, ROWS, 128, kind=F32)], []
    )
    near = []
    for p in range(2):
        near.append([block[p]] + [shift(block[p], send_first(-k)) for k in (1, 2, 3)])
    pairs = []
    half = array(2, 17, 16, 256)
    for p in range(2):
        row = jnp.stack(near[p])
        after, before = shift(row, send_second(-1)), shift(row, send_second(1))
        low, high = call(kernel_halves, scalars, [after, before], [half, half], [])
        across = [shift(low, send_second(-1)), shift(high, send_second(1))]
        rows = [row, after, before, *across]
        pairs.append(rows + [shift(v, SWAP) for v in rows])
    x1, x2, win, wout, stat1, pre = call(
        kernel_low_forward,
        scalars,
        [inputs, hat0, *pairs[0]],
        [
            array(*ACT), array(*ACT), array(*WIN), array(*WOUT),
            array(2, ROWS, 128, kind=F32), array(2, ROWS, R, kind=F32),
        ],
        LOW_SCRATCH,
    )
    up2, acts1 = call(
        kernel_high, scalars, [x2, cotangent, *pairs[1]], [array(*ACT), array(*ACTS)], HIGH_SCRATCH
    )
    got1 = shift(acts1[1], SWAP)
    acts0 = call(
        kernel_low_back,
        scalars,
        [inputs, x1, up2, win, wout, stat0, stat1, pre],
        array(*ACTS),
        BACK_SCRATCH,
    )
    got0 = shift(acts0[1], SWAP)
    first1 = scatter_first(scalars, acts1, got1)
    first0 = scatter_first(scalars, acts0, got0)
    sides1 = scatter_sides(scalars, *first1)
    sides0 = scatter_sides(scalars, *first0)
    grads = scatter_second(scalars, sides0, sides1)
    parts = jnp.concatenate(
        [
            grads[:, :8].reshape(2, 4, 32, 256),
            grads[:, 8:16].reshape(2, 8, 4, 4, 256).transpose(0, 2, 1, 3, 4).reshape(2, 4, 32, 256),
            jnp.pad(grads[:, 16, 0, :128].reshape(2, 4, 1, 32), ((0, 0), (0, 0), (0, 7), (0, 224))),
        ],
        axis=2,
    ).reshape(8, 72, 256)
    return call(
        kernel_finish,
        scalars,
        [lax.all_to_all(parts, ("zl", "zh"), 0, 0)],
        (array(1, 32, kind=F32), array(1, 32, 256, kind=F32), array(1, 4, 2048, kind=F32)),
        [],
    )


def solution(mesh):
    fine = Mesh(mesh.devices.reshape(DIMS), AXES)
    zero = ("x", "y", "zh")
    segment = ("zl", "c")
    return jax.shard_map(
        device_body,
        mesh=fine,
        in_specs=(
            P(None, None, zero, None),
            P(None, None, zero, None),
            P(segment, zero),
            P(segment, zero, None),
            P(segment, zero, None),
        ),
        out_specs=(P(segment, zero), P(segment, zero, None), P(segment, zero, None)),
        check_vma=False,
    )
```

```python
import functools
import itertools

import jax
import jax.numpy as jnp
import numpy as np
from jax import lax
from jax.experimental import pallas as pl
from jax.experimental.pallas import tpu as pltpu
from jax.sharding import Mesh
from jax.sharding import PartitionSpec as P


gelu_coeff = 0.7978845608028654
cubic_coeff = 0.044715
norm_eps = 1e-05

AXES = ("zl", "c", "x", "y", "zh")
DIMS = (2, 2, 4, 4, 4)
D = 2048
R = 256
ROWS = 128
CHUNK = 16
F32 = jnp.float32
BF16 = jnp.bfloat16


def flat_perm(move):
    pairs = []
    for src, coords in enumerate(itertools.product(*[range(n) for n in DIMS])):
        dst = [v % n for v, n in zip(move(*coords), DIMS)]
        pairs.append((src, int(np.ravel_multi_index(dst, DIMS))))
    return pairs


def send_first(k):
    return flat_perm(
        lambda zl, c, x, y, zh: (zl, c, x + k, y, zh) if c == 0 else (zl, c, x, y + k, zh)
    )


def send_second(k):
    return flat_perm(
        lambda zl, c, x, y, zh: (zl, c, x, y + k, zh) if c == 0 else (zl, c, x + k, y, zh)
    )


SWAP = flat_perm(lambda zl, c, x, y, zh: (zl, c + 1, x, y, zh))


def shift(value, pairs):
    return lax.ppermute(value, AXES, pairs)


def dot(left, right, left_dim=1, right_dim=0):
    return lax.dot_general(
        left, right, (((left_dim,), (right_dim,)), ((), ())), preferred_element_type=F32
    )


def gelu_parts(v):
    inner = jnp.tanh(gelu_coeff * (v + cubic_coeff * v * v * v))
    return inner, (0.5 * v * (1.0 + inner)).astype(BF16)


def gelu_slope(v, inner):
    return 0.5 * (1.0 + inner) + 0.5 * v * (1.0 - inner * inner) * gelu_coeff * (
        1.0 + 3.0 * cubic_coeff * v * v
    )


def place_weights(s_ref, pieces, win, wout):
    mx, my, c = s_ref[0], s_ref[1], s_ref[2]
    for o in range(2):
        par = c if o == 0 else 1 - c
        for src, (b, first, count) in zip(pieces[o * PIECES : (o + 1) * PIECES], SPANS):

            def place(i, carry, par=par, src=src, b=b, first=first):
                a = first + i
                x = (mx + jnp.where(par == 0, a, b)) & 3
                y = (my + jnp.where(par == 0, b, a)) & 3
                xy = x * 4 + y
                win[par, pl.ds(xy * 8, 8)] = src[i, 0:8]
                for k in range(9):
                    wout[par, k, xy] = src[i, 8 + k]
                return carry

            lax.fori_loop(0, count, place, 0)


def gain_row(wout, par):
    return jnp.concatenate(
        [wout[par, 8, xy, 0:1, 0:128] for xy in range(16)], axis=1
    ).astype(F32)


def over_rows(step):
    def body(i, carry):
        step(pl.ds(pl.multiple_of(i * CHUNK, CHUNK), CHUNK))
        return carry

    lax.fori_loop(0, ROWS // CHUNK, body, 0, unroll=UNROLL)


def hat_pass(x_at, hat, keep_stat):
    def step(rows):
        xf = x_at(rows).astype(F32)
        mean = jnp.mean(xf, axis=-1, keepdims=True)
        centered = xf - mean
        variance = jnp.mean(centered * centered, axis=-1, keepdims=True)
        recip_std = lax.rsqrt(variance + norm_eps)
        hat[rows, :] = centered * recip_std
        keep_stat(rows, mean, recip_std)

    over_rows(step)


def spread(column):
    return jnp.broadcast_to(column, (CHUNK, 128))


def layer_out(x_at, act, wout, par, out_ref):
    for k in range(8):
        cols = pl.ds(k * 256, 256)
        out_ref[:, cols] = (
            x_at(cols).astype(F32) + dot(act, wout[par, k].reshape(R, 256))
        ).astype(BF16)


def layer_back(up_at, acts, slot, hat, rstd_at, preact, win, wout, par, gain, gnorm, gsum, up_out):
    inner, act = gelu_parts(preact)
    grad_act = jnp.zeros((ROWS, R), F32)
    for k in range(8):
        grad_act += dot(
            up_at(pl.ds(0, ROWS), pl.ds(k * 256, 256)), wout[par, k].reshape(R, 256), 1, 1
        )
    grad_pre = (grad_act * gelu_slope(preact, inner)).astype(BF16)
    acts[slot, 0:ROWS, ACT_AT : ACT_AT + R] = act
    acts[slot, 0:ROWS, PRE_AT : PRE_AT + R] = grad_pre
    for k in range(8):
        gnorm[:, pl.ds(k * 256, 256)] = dot(
            grad_pre, win[par, pl.ds(k * 16, 16)].reshape(256, R), 1, 1
        )
    gsum[...] = jnp.zeros((CHUNK, D), F32)

    def step(rows):
        grad_normed = gnorm[rows, :]
        hatted = hat[rows, :]
        product = grad_normed * hatted
        gsum[...] += product
        up = up_at(rows, pl.ds(0, D))
        acts[slot, rows, UP_AT : UP_AT + D] = up
        if up_out is not None:
            grad_hat = grad_normed * gain
            mean_hat = jnp.mean(grad_hat, axis=-1, keepdims=True)
            mean_both = jnp.mean(product * gain, axis=-1, keepdims=True)
            through = rstd_at(rows) * (grad_hat - mean_hat - hatted * mean_both)
            up_out[rows, :] = (up.astype(F32) + through).astype(BF16)

    over_rows(step)
    acts[slot, ROWS : ROWS + 16, 0:D] = jnp.broadcast_to(
        jnp.sum(gsum[...], axis=0, keepdims=True), (16, D)
    ).astype(BF16)


def kernel_stats(s_ref, xs, hat, stat):
    c, zl = s_ref[2], s_ref[3]

    def keep_stat(rows, mean, recip_std):
        stat[0, rows, :] = spread(mean)
        stat[1, rows, :] = spread(recip_std)

    hat_pass(lambda rows: xs[zl, c, rows, :], hat, keep_stat)


def kernel_low_forward(s_ref, xs, hat0, *refs):
    pieces = refs[: 2 * PIECES]
    x1, x2, win, wout, stat1, pre, normed, hat1 = refs[2 * PIECES :]
    place_weights(s_ref, pieces, win, wout)
    c, zl = s_ref[2], s_ref[3]

    def keep_stat(rows, mean, recip_std):
        stat1[0, rows, :] = spread(mean)
        stat1[1, rows, :] = spread(recip_std)

    for par, hat in enumerate((hat0, hat1)):
        if par:
            hat_pass(lambda rows: x1[rows, :], hat1, keep_stat)
        gain = gain_row(wout, par)

        def step(rows, gain=gain, hat=hat):
            normed[rows, :] = (hat[rows, :] * gain).astype(BF16)

        over_rows(step)
        pre[par] = dot(normed[...], win[par].reshape(D, R))
        act = gelu_parts(pre[par])[1]
        if par:
            layer_out(lambda cols: x1[:, cols], act, wout, par, x2)
        else:
            layer_out(lambda cols: xs[zl, c, :, cols], act, wout, par, x1)


def kernel_high(s_ref, x2, cots, *refs):
    pieces = refs[: 2 * PIECES]
    up2, acts, win, wout, hat0, hat1, rstd, x3, up3, pre0, gnorm, gsum = refs[2 * PIECES :]
    place_weights(s_ref, pieces, win, wout)
    c, zl = s_ref[2], s_ref[3]
    gains = []
    for par, (src, hat) in enumerate(((x2, hat0), (x3, hat1))):

        def keep_stat(rows, mean, recip_std, par=par):
            rstd[par, rows, :] = spread(recip_std)

        hat_pass(lambda rows, src=src: src[rows, :], hat, keep_stat)
        gain = gain_row(wout, par)
        slot = jnp.where(c == par, 0, 1)

        def step(rows, gain=gain, hat=hat, slot=slot):
            acts[slot, rows, 0:D] = (hat[rows, :] * gain).astype(BF16)

        over_rows(step)
        preact = dot(acts[slot, 0:ROWS, 0:D], win[par].reshape(D, R))
        gains.append(gain)
        if par == 0:
            pre0[...] = preact
            layer_out(lambda cols: x2[:, cols], gelu_parts(preact)[1], wout, 0, x3)
    layer_back(
        lambda rows, cols: cots[zl, c, rows, cols],
        acts, jnp.where(c == 1, 0, 1), hat1, lambda rows: rstd[1, rows, 0:1],
        preact, win, wout, 1, gains[1], gnorm, gsum, up3,
    )
    layer_back(
        lambda rows, cols: up3[rows, cols],
        acts, jnp.where(c == 0, 0, 1), hat0, lambda rows: rstd[0, rows, 0:1],
        pre0[...], win, wout, 0, gains[0], gnorm, gsum, up2,
    )


def kernel_low_back(s_ref, xs, x1, up2, win, wout, stat0, stat1, pre, acts, hat, up1, gnorm, gsum):
    c, zl = s_ref[2], s_ref[3]
    for par, stat, up, up_out in ((1, stat1, up2, up1), (0, stat0, up1, None)):
        gain = gain_row(wout, par)
        slot = jnp.where(c == par, 0, 1)

        def step(rows, par=par, stat=stat, gain=gain, slot=slot):
            xf = (x1[rows, :] if par else xs[zl, c, rows, :]).astype(F32)
            hatted = (xf - stat[0, rows, 0:1]) * stat[1, rows, 0:1]
            hat[rows, :] = hatted
            acts[slot, rows, 0:D] = (hatted * gain).astype(BF16)

        over_rows(step)
        layer_back(
            lambda rows, cols, up=up: up[rows, cols],
            acts, slot, hat, lambda rows, stat=stat: stat[1, rows, 0:1],
            pre[par], win, wout, par, gain, gnorm, gsum, up_out,
        )


def kernel_grads(s_ref, acts, got, out, up, down):
    mx, my, c = s_ref[0], s_ref[1], s_ref[2]
    places = []
    for xy in range(16):
        xr = (xy // 4 - mx) & 3
        yr = (xy % 4 - my) & 3
        places.append(jnp.where(c == 0, xr * 4 + yr, yr * 4 + xr))

    def both(start, size):
        cols = pl.ds(start, size)
        return jnp.concatenate([acts[0, 0:ROWS, cols], got[0:ROWS, cols]], axis=0)

    grad_pre = both(PRE_AT, R)
    for xy in range(16):
        block = dot(both(xy * 128, 128).T, grad_pre)
        out[places[xy], 0:8] = block.astype(BF16).reshape(8, 16, 256)
    act_t = both(ACT_AT, R).T
    for k in range(8):
        block = dot(act_t, both(UP_AT + k * 256, 256)).astype(BF16).reshape(16, 16, 256)
        for xy in range(16):
            out[places[xy], 8 + k] = block[xy]
    for xy in range(16):
        cols = pl.ds(xy * 128, 128)
        part = acts[0, ROWS : ROWS + 16, cols].astype(F32) + got[ROWS : ROWS + 16, cols].astype(F32)
        out[places[xy], 16] = jnp.concatenate([part, part], axis=1).astype(BF16)


    up[...] = out[8:10]
    down[...] = out[10:12]


def over_groups(step):
    def body(g, carry):
        step(g)
        return carry

    lax.fori_loop(0, 17, body, 0)


def kernel_sides(s_ref, grads, up, down, after, before):
    def step(g):
        for i in range(2):
            after[i, g] = (grads[4 + i, g].astype(F32) + up[i, g].astype(F32)).astype(BF16)
            after[2 + i, g] = grads[6 + i, g]
            before[i, g] = grads[12 + i, g]
            before[2 + i, g] = (grads[14 + i, g].astype(F32) + down[i, g].astype(F32)).astype(BF16)

    over_groups(step)


def kernel_sum(s_ref, low, low_a, low_b, high, high_a, high_b, *pieces):
    def step(g):
        for p, (own, a, b) in enumerate(((low, low_a, low_b), (high, high_a, high_b))):
            for k in range(4):
                pieces[k][p, g] = (
                    own[k, g].astype(F32) + a[k, g].astype(F32) + b[k, g].astype(F32)
                ).astype(BF16)

    over_groups(step)


def kernel_finish(s_ref, parts, gain, grad_in, grad_out):
    total = parts[0].astype(F32)
    for i in range(1, 8):
        total += parts[i].astype(F32)
    grad_in[0] = total[0:32]
    for k in range(8):
        grad_out[0, :, pl.ds(k * 256, 256)] = total[32 + 4 * k : 36 + 4 * k]
    gain[...] = total[64:65, 0:32]


def vmem(*shape, kind=BF16):
    return pltpu.VMEM(shape, kind)


def array(*shape, kind=BF16):
    return jax.ShapeDtypeStruct(shape, kind)


UNROLL = 8
SPANS = tuple((b, 0, 4) for b in range(4))
PIECES = len(SPANS)
UP_AT, ACT_AT, PRE_AT, WIDE = D, 2 * D, 2 * D + R, 2 * D + 2 * R
ACT = (ROWS, D)
WIN, WOUT = (2, 128, 16, 256), (2, 9, 16, 16, 256)
ACTS = (2, ROWS + 16, WIDE)
HAT = vmem(ROWS, D, kind=F32)
GSUM = vmem(CHUNK, D, kind=F32)
LOW_SCRATCH = [vmem(*ACT), HAT]
HIGH_SCRATCH = [
    vmem(*WIN), vmem(*WOUT), HAT, HAT, vmem(2, ROWS, 128, kind=F32),
    vmem(*ACT), vmem(*ACT), vmem(ROWS, R, kind=F32), HAT, GSUM,
]
BACK_SCRATCH = [HAT, vmem(*ACT), HAT, GSUM]
WHOLE = pl.BlockSpec(memory_space=pltpu.VMEM)


def call(body, scalars, args, out_shape, scratch):
    return pl.pallas_call(
        body,
        in_specs=[pl.BlockSpec(memory_space=pltpu.SMEM)] + [WHOLE] * len(args),
        out_specs=jax.tree.map(lambda s: WHOLE, out_shape),
        scratch_shapes=scratch,
        out_shape=out_shape,
        compiler_params=pltpu.CompilerParams(vmem_limit_bytes=20 * 1024 * 1024),
    )(scalars, *args)


def add_up(first, got):
    return functools.reduce(lambda p, q: p + q.astype(F32), got, first.astype(F32)).astype(BF16)


def scatter_first(scalars, acts, got):
    half = array(2, 17, 16, 256)
    grads, up, down = call(
        kernel_grads, scalars, [acts, got], [array(16, 17, 16, 256), half, half], []
    )
    return grads, shift(up, send_first(1)), shift(down, send_first(-1))


def scatter_sides(scalars, grads, up, down):
    row = array(4, 17, 16, 256)
    after, before = call(kernel_sides, scalars, [grads, up, down], [row, row], [])
    return grads, shift(after, send_first(1)), shift(before, send_first(-1))


def scatter_second(scalars, low, high):
    piece = array(2, 17, 16, 256)
    own, *pieces = call(kernel_sum, scalars, [*low, *high], [piece] * 4, [])
    got = [shift(pieces[k - 1], send_second(k)) for k in (2, 1, 3)]
    return add_up(own, got)


def device_body(inputs, cotangent, norm_gain, proj_in, proj_out):
    where = [lax.axis_index(n).astype(jnp.int32) for n in ("x", "y", "c", "zl")]
    scalars = jnp.stack(where)
    shard = jnp.concatenate(
        [
            proj_in[0],
            proj_out[0].reshape(4, 8, 256).transpose(1, 0, 2).reshape(32, 256),
            jnp.pad(norm_gain, ((0, 7), (0, 224))),
        ],
        axis=0,
    )
    column = lax.all_to_all(
        jnp.broadcast_to(shard[None], (8, 72, 256)), ("zl", "zh"), 0, 0
    ).reshape(2, 4, 72, 256)
    gain = jnp.pad(column[:, :, 64, :32].reshape(2, 1, 1, 128), ((0, 0), (0, 0), (0, 15), (0, 128)))
    block = jnp.concatenate(
        [
            column[:, :, :32].reshape(2, 8, 16, 256),
            column[:, :, 32:64].reshape(2, 4, 8, 4, 256).transpose(0, 2, 1, 3, 4).reshape(2, 8, 16, 256),
            gain,
        ],
        axis=1,
    )
    hat0, stat0 = call(
        kernel_stats, scalars, [inputs], [array(*ACT, kind=F32), array(2, ROWS, 128, kind=F32)], []
    )
    near = []
    for p in range(2):
        near.append([block[p]] + [shift(block[p], send_first(-k)) for k in (1, 2, 3)])
    pairs = []
    for p in range(2):
        row = jnp.stack(near[p])
        rows = [row] + [shift(row, send_second(-k)) for k in (1, 2, 3)]
        pairs.append(rows + [shift(v, SWAP) for v in rows])
    x1, x2, win, wout, stat1, pre = call(
        kernel_low_forward,
        scalars,
        [inputs, hat0, *pairs[0]],
        [
            array(*ACT), array(*ACT), array(*WIN), array(*WOUT),
            array(2, ROWS, 128, kind=F32), array(2, ROWS, R, kind=F32),
        ],
        LOW_SCRATCH,
    )
    up2, acts1 = call(
        kernel_high, scalars, [x2, cotangent, *pairs[1]], [array(*ACT), array(*ACTS)], HIGH_SCRATCH
    )
    got1 = shift(acts1[1], SWAP)
    acts0 = call(
        kernel_low_back,
        scalars,
        [inputs, x1, up2, win, wout, stat0, stat1, pre],
        array(*ACTS),
        BACK_SCRATCH,
    )
    got0 = shift(acts0[1], SWAP)
    first1 = scatter_first(scalars, acts1, got1)
    first0 = scatter_first(scalars, acts0, got0)
    sides1 = scatter_sides(scalars, *first1)
    sides0 = scatter_sides(scalars, *first0)
    grads = scatter_second(scalars, sides0, sides1)
    parts = jnp.concatenate(
        [
            grads[:, :8].reshape(2, 4, 32, 256),
            grads[:, 8:16].reshape(2, 8, 4, 4, 256).transpose(0, 2, 1, 3, 4).reshape(2, 4, 32, 256),
            jnp.pad(grads[:, 16, 0, :128].reshape(2, 4, 1, 32), ((0, 0), (0, 0), (0, 7), (0, 224))),
        ],
        axis=2,
    ).reshape(8, 72, 256)
    return call(
        kernel_finish,
        scalars,
        [lax.all_to_all(parts, ("zl", "zh"), 0, 0)],
        (array(1, 32, kind=F32), array(1, 32, 256, kind=F32), array(1, 4, 2048, kind=F32)),
        [],
    )


def solution(mesh):
    fine = Mesh(mesh.devices.reshape(DIMS), AXES)
    zero = ("x", "y", "zh")
    segment = ("zl", "c")
    return jax.shard_map(
        device_body,
        mesh=fine,
        in_specs=(
            P(None, None, zero, None),
            P(None, None, zero, None),
            P(segment, zero),
            P(segment, zero, None),
            P(segment, zero, None),
        ),
        out_specs=(P(segment, zero), P(segment, zero, None), P(segment, zero, None)),
        check_vma=False,
    )
```

```python
import functools
import itertools

import jax
import jax.numpy as jnp
import numpy as np
from jax import lax
from jax.experimental import pallas as pl
from jax.experimental.pallas import tpu as pltpu
from jax.sharding import Mesh
from jax.sharding import PartitionSpec as P


gelu_coeff = 0.7978845608028654
cubic_coeff = 0.044715
norm_eps = 1e-05

AXES = ("zl", "c", "x", "y", "zh")
DIMS = (2, 2, 4, 4, 4)
D = 2048
R = 256
ROWS = 128
CHUNK = 16
F32 = jnp.float32
BF16 = jnp.bfloat16


def flat_perm(move):
    pairs = []
    for src, coords in enumerate(itertools.product(*[range(n) for n in DIMS])):
        dst = [v % n for v, n in zip(move(*coords), DIMS)]
        pairs.append((src, int(np.ravel_multi_index(dst, DIMS))))
    return pairs


def send_first(k):
    return flat_perm(
        lambda zl, c, x, y, zh: (zl, c, x + k, y, zh) if c == 0 else (zl, c, x, y + k, zh)
    )


def send_second(k):
    return flat_perm(
        lambda zl, c, x, y, zh: (zl, c, x, y + k, zh) if c == 0 else (zl, c, x + k, y, zh)
    )


SWAP = flat_perm(lambda zl, c, x, y, zh: (zl, c + 1, x, y, zh))


def shift(value, pairs):
    return lax.ppermute(value, AXES, pairs)


def around(value, send):
    across = shift(value, send(-2))
    return [shift(value, send(-1)), across, shift(value, send(-3))]


def dot(left, right, left_dim=1, right_dim=0):
    return lax.dot_general(
        left, right, (((left_dim,), (right_dim,)), ((), ())), preferred_element_type=F32
    )


def gelu_parts(v):
    inner = jnp.tanh(gelu_coeff * (v + cubic_coeff * v * v * v))
    return inner, (0.5 * v * (1.0 + inner)).astype(BF16)


def gelu_slope(v, inner):
    return 0.5 * (1.0 + inner) + 0.5 * v * (1.0 - inner * inner) * gelu_coeff * (
        1.0 + 3.0 * cubic_coeff * v * v
    )


def place_weights(s_ref, pieces, win, wout):
    mx, my, c = s_ref[0], s_ref[1], s_ref[2]
    for o in range(2):
        par = c if o == 0 else 1 - c
        for src, (b, first, count) in zip(pieces[o * PIECES : (o + 1) * PIECES], SPANS):

            def place(i, carry, par=par, src=src, b=b, first=first):
                a = first + i
                x = (mx + jnp.where(par == 0, a, b)) & 3
                y = (my + jnp.where(par == 0, b, a)) & 3
                xy = x * 4 + y
                win[par, pl.ds(xy * 8, 8)] = src[i, 0:8]
                for k in range(9):
                    wout[par, k, xy] = src[i, 8 + k]
                return carry

            lax.fori_loop(0, count, place, 0)


def gain_row(wout, par):
    return jnp.concatenate(
        [wout[par, 8, xy, 0:1, 0:128] for xy in range(16)], axis=1
    ).astype(F32)


def over_rows(step):
    def body(i, carry):
        step(pl.ds(pl.multiple_of(i * CHUNK, CHUNK), CHUNK))
        return carry

    lax.fori_loop(0, ROWS // CHUNK, body, 0, unroll=UNROLL)


def hat_pass(x_at, hat, keep_stat):
    def step(rows):
        xf = x_at(rows).astype(F32)
        mean = jnp.mean(xf, axis=-1, keepdims=True)
        centered = xf - mean
        variance = jnp.mean(centered * centered, axis=-1, keepdims=True)
        recip_std = lax.rsqrt(variance + norm_eps)
        hat[rows, :] = centered * recip_std
        keep_stat(rows, mean, recip_std)

    over_rows(step)


def spread(column):
    return jnp.broadcast_to(column, (CHUNK, 128))


def layer_out(x_at, act, wout, par, out_ref):
    for k in range(8):
        cols = pl.ds(k * 256, 256)
        out_ref[:, cols] = (
            x_at(cols).astype(F32) + dot(act, wout[par, k].reshape(R, 256))
        ).astype(BF16)


def layer_back(up_at, acts, slot, hat, rstd_at, preact, win, wout, par, gain, gnorm, gsum, up_out):
    inner, act = gelu_parts(preact)
    grad_act = jnp.zeros((ROWS, R), F32)
    for k in range(8):
        grad_act += dot(
            up_at(pl.ds(0, ROWS), pl.ds(k * 256, 256)), wout[par, k].reshape(R, 256), 1, 1
        )
    grad_pre = (grad_act * gelu_slope(preact, inner)).astype(BF16)
    acts[slot, 0:ROWS, ACT_AT : ACT_AT + R] = act
    acts[slot, 0:ROWS, PRE_AT : PRE_AT + R] = grad_pre
    for k in range(8):
        gnorm[:, pl.ds(k * 256, 256)] = dot(
            grad_pre, win[par, pl.ds(k * 16, 16)].reshape(256, R), 1, 1
        )
    gsum[...] = jnp.zeros((CHUNK, D), F32)

    def step(rows):
        grad_normed = gnorm[rows, :]
        hatted = hat[rows, :]
        product = grad_normed * hatted
        gsum[...] += product
        up = up_at(rows, pl.ds(0, D))
        acts[slot, rows, UP_AT : UP_AT + D] = up
        if up_out is not None:
            grad_hat = grad_normed * gain
            mean_hat = jnp.mean(grad_hat, axis=-1, keepdims=True)
            mean_both = jnp.mean(product * gain, axis=-1, keepdims=True)
            through = rstd_at(rows) * (grad_hat - mean_hat - hatted * mean_both)
            up_out[rows, :] = (up.astype(F32) + through).astype(BF16)

    over_rows(step)
    acts[slot, ROWS : ROWS + 16, 0:D] = jnp.broadcast_to(
        jnp.sum(gsum[...], axis=0, keepdims=True), (16, D)
    ).astype(BF16)


def kernel_stats(s_ref, xs, hat, stat):
    c, zl = s_ref[2], s_ref[3]

    def keep_stat(rows, mean, recip_std):
        stat[0, rows, :] = spread(mean)
        stat[1, rows, :] = spread(recip_std)

    hat_pass(lambda rows: xs[zl, c, rows, :], hat, keep_stat)


def kernel_low_forward(s_ref, xs, hat0, *refs):
    pieces = refs[: 2 * PIECES]
    x1, x2, win, wout, stat1, pre, hat2, rstd2, normed, hat1 = refs[2 * PIECES :]
    place_weights(s_ref, pieces, win, wout)
    c, zl = s_ref[2], s_ref[3]

    def keep_stat(rows, mean, recip_std):
        stat1[0, rows, :] = spread(mean)
        stat1[1, rows, :] = spread(recip_std)

    for par, hat in enumerate((hat0, hat1)):
        if par:
            hat_pass(lambda rows: x1[rows, :], hat1, keep_stat)
        gain = gain_row(wout, par)

        def step(rows, gain=gain, hat=hat):
            normed[rows, :] = (hat[rows, :] * gain).astype(BF16)

        over_rows(step)
        pre[par] = dot(normed[...], win[par].reshape(D, R))
        act = gelu_parts(pre[par])[1]
        if par:
            layer_out(lambda cols: x1[:, cols], act, wout, par, x2)
        else:
            layer_out(lambda cols: xs[zl, c, :, cols], act, wout, par, x1)

    def keep_rstd(rows, mean, recip_std):
        rstd2[rows, :] = spread(recip_std)

    hat_pass(lambda rows: x2[rows, :], hat2, keep_rstd)


def kernel_high(s_ref, x2, hat0, rstd0, cots, *refs):
    pieces = refs[: 2 * PIECES]
    up2, acts, win, wout, hat1, rstd1, x3, up3, pre0, gnorm, gsum = refs[2 * PIECES :]
    place_weights(s_ref, pieces, win, wout)
    c, zl = s_ref[2], s_ref[3]
    gains = []

    def keep_rstd(rows, mean, recip_std):
        rstd1[rows, :] = spread(recip_std)

    for par, hat in enumerate((hat0, hat1)):
        if par:
            hat_pass(lambda rows: x3[rows, :], hat1, keep_rstd)
        gain = gain_row(wout, par)
        slot = jnp.where(c == par, 0, 1)

        def step(rows, gain=gain, hat=hat, slot=slot):
            acts[slot, rows, 0:D] = (hat[rows, :] * gain).astype(BF16)

        over_rows(step)
        preact = dot(acts[slot, 0:ROWS, 0:D], win[par].reshape(D, R))
        gains.append(gain)
        if par == 0:
            pre0[...] = preact
            layer_out(lambda cols: x2[:, cols], gelu_parts(preact)[1], wout, 0, x3)
    layer_back(
        lambda rows, cols: cots[zl, c, rows, cols],
        acts, jnp.where(c == 1, 0, 1), hat1, lambda rows: rstd1[rows, 0:1],
        preact, win, wout, 1, gains[1], gnorm, gsum, up3,
    )
    layer_back(
        lambda rows, cols: up3[rows, cols],
        acts, jnp.where(c == 0, 0, 1), hat0, lambda rows: rstd0[rows, 0:1],
        pre0[...], win, wout, 0, gains[0], gnorm, gsum, up2,
    )


def kernel_low_back(s_ref, xs, x1, up2, win, wout, stat0, stat1, pre, acts, hat, up1, gnorm, gsum):
    c, zl = s_ref[2], s_ref[3]
    for par, stat, up, up_out in ((1, stat1, up2, up1), (0, stat0, up1, None)):
        gain = gain_row(wout, par)
        slot = jnp.where(c == par, 0, 1)

        def step(rows, par=par, stat=stat, gain=gain, slot=slot):
            xf = (x1[rows, :] if par else xs[zl, c, rows, :]).astype(F32)
            hatted = (xf - stat[0, rows, 0:1]) * stat[1, rows, 0:1]
            hat[rows, :] = hatted
            acts[slot, rows, 0:D] = (hatted * gain).astype(BF16)

        over_rows(step)
        layer_back(
            lambda rows, cols, up=up: up[rows, cols],
            acts, slot, hat, lambda rows, stat=stat: stat[1, rows, 0:1],
            pre[par], win, wout, par, gain, gnorm, gsum, up_out,
        )


def kernel_grads(s_ref, acts, got, out, up, down):
    mx, my, c = s_ref[0], s_ref[1], s_ref[2]
    places = []
    for xy in range(16):
        xr = (xy // 4 - mx) & 3
        yr = (xy % 4 - my) & 3
        places.append(jnp.where(c == 0, xr * 4 + yr, yr * 4 + xr))

    def both(start, size):
        cols = pl.ds(start, size)
        return jnp.concatenate([acts[0, 0:ROWS, cols], got[0:ROWS, cols]], axis=0)

    grad_pre = both(PRE_AT, R)
    for xy in range(16):
        block = dot(both(xy * 128, 128).T, grad_pre)
        out[places[xy], 0:8] = block.astype(BF16).reshape(8, 16, 256)
    act_t = both(ACT_AT, R).T
    for k in range(8):
        block = dot(act_t, both(UP_AT + k * 256, 256)).astype(BF16).reshape(16, 16, 256)
        for xy in range(16):
            out[places[xy], 8 + k] = block[xy]
    for xy in range(16):
        cols = pl.ds(xy * 128, 128)
        part = acts[0, ROWS : ROWS + 16, cols].astype(F32) + got[ROWS : ROWS + 16, cols].astype(F32)
        out[places[xy], 16] = jnp.concatenate([part, part], axis=1).astype(BF16)


    up[...] = out[8:10]
    down[...] = out[10:12]


def over_groups(step):
    def body(g, carry):
        step(g)
        return carry

    lax.fori_loop(0, 17, body, 0)


def kernel_sides(s_ref, grads, up, down, after, before):
    def step(g):
        for i in range(2):
            after[i, g] = (grads[4 + i, g].astype(F32) + up[i, g].astype(F32)).astype(BF16)
            after[2 + i, g] = grads[6 + i, g]
            before[i, g] = grads[12 + i, g]
            before[2 + i, g] = (grads[14 + i, g].astype(F32) + down[i, g].astype(F32)).astype(BF16)

    over_groups(step)


def kernel_sum(s_ref, low, low_a, low_b, high, high_a, high_b, *pieces):
    def step(g):
        for p, (own, a, b) in enumerate(((low, low_a, low_b), (high, high_a, high_b))):
            for k in range(4):
                pieces[k][p, g] = (
                    own[k, g].astype(F32) + a[k, g].astype(F32) + b[k, g].astype(F32)
                ).astype(BF16)

    over_groups(step)


def kernel_finish(s_ref, parts, gain, grad_in, grad_out):
    total = parts[0].astype(F32)
    for i in range(1, 8):
        total += parts[i].astype(F32)
    grad_in[0] = total[0:32]
    for k in range(8):
        grad_out[0, :, pl.ds(k * 256, 256)] = total[32 + 4 * k : 36 + 4 * k]
    gain[...] = total[64:65, 0:32]


def vmem(*shape, kind=BF16):
    return pltpu.VMEM(shape, kind)


def array(*shape, kind=BF16):
    return jax.ShapeDtypeStruct(shape, kind)


UNROLL = 8
SPANS = tuple((b, 0, 4) for b in range(4))
PIECES = len(SPANS)
UP_AT, ACT_AT, PRE_AT, WIDE = D, 2 * D, 2 * D + R, 2 * D + 2 * R
ACT = (ROWS, D)
WIN, WOUT = (2, 128, 16, 256), (2, 9, 16, 16, 256)
ACTS = (2, ROWS + 16, WIDE)
HAT = vmem(ROWS, D, kind=F32)
GSUM = vmem(CHUNK, D, kind=F32)
LOW_SCRATCH = [vmem(*ACT), HAT]
HIGH_SCRATCH = [
    vmem(*WIN), vmem(*WOUT), HAT, vmem(ROWS, 128, kind=F32),
    vmem(*ACT), vmem(*ACT), vmem(ROWS, R, kind=F32), HAT, GSUM,
]
BACK_SCRATCH = [HAT, vmem(*ACT), HAT, GSUM]
WHOLE = pl.BlockSpec(memory_space=pltpu.VMEM)


def call(body, scalars, args, out_shape, scratch):
    return pl.pallas_call(
        body,
        in_specs=[pl.BlockSpec(memory_space=pltpu.SMEM)] + [WHOLE] * len(args),
        out_specs=jax.tree.map(lambda s: WHOLE, out_shape),
        scratch_shapes=scratch,
        out_shape=out_shape,
        compiler_params=pltpu.CompilerParams(vmem_limit_bytes=20 * 1024 * 1024),
    )(scalars, *args)


def add_up(first, got):
    return functools.reduce(lambda p, q: p + q.astype(F32), got, first.astype(F32)).astype(BF16)


def scatter_first(scalars, acts, got):
    half = array(2, 17, 16, 256)
    grads, up, down = call(
        kernel_grads, scalars, [acts, got], [array(16, 17, 16, 256), half, half], []
    )
    return grads, shift(up, send_first(1)), shift(down, send_first(-1))


def scatter_sides(scalars, grads, up, down):
    row = array(4, 17, 16, 256)
    after, before = call(kernel_sides, scalars, [grads, up, down], [row, row], [])
    return grads, shift(after, send_first(1)), shift(before, send_first(-1))


def scatter_second(scalars, low, high):
    piece = array(2, 17, 16, 256)
    own, *pieces = call(kernel_sum, scalars, [*low, *high], [piece] * 4, [])
    got = [shift(pieces[k - 1], send_second(k)) for k in (2, 1, 3)]
    return add_up(own, got)


def device_body(inputs, cotangent, norm_gain, proj_in, proj_out):
    where = [lax.axis_index(n).astype(jnp.int32) for n in ("x", "y", "c", "zl")]
    scalars = jnp.stack(where)
    shard = jnp.concatenate(
        [
            proj_in[0],
            proj_out[0].reshape(4, 8, 256).transpose(1, 0, 2).reshape(32, 256),
            jnp.pad(norm_gain, ((0, 7), (0, 224))),
        ],
        axis=0,
    )
    column = lax.all_to_all(
        jnp.broadcast_to(shard[None], (8, 72, 256)), ("zl", "zh"), 0, 0
    ).reshape(2, 4, 72, 256)
    gain = jnp.pad(column[:, :, 64, :32].reshape(2, 1, 1, 128), ((0, 0), (0, 0), (0, 15), (0, 128)))
    block = jnp.concatenate(
        [
            column[:, :, :32].reshape(2, 8, 16, 256),
            column[:, :, 32:64].reshape(2, 4, 8, 4, 256).transpose(0, 2, 1, 3, 4).reshape(2, 8, 16, 256),
            gain,
        ],
        axis=1,
    )
    hat0, stat0 = call(
        kernel_stats, scalars, [inputs], [array(*ACT, kind=F32), array(2, ROWS, 128, kind=F32)], []
    )
    near = []
    for p in range(2):
        near.append([block[p]] + around(block[p], send_first))
    pairs = []
    for p in range(2):
        row = jnp.stack(near[p])
        rows = [row] + around(row, send_second)
        pairs.append(rows + [shift(v, SWAP) for v in rows])
    x1, x2, win, wout, stat1, pre, hat2, rstd2 = call(
        kernel_low_forward,
        scalars,
        [inputs, hat0, *pairs[0]],
        [
            array(*ACT), array(*ACT), array(*WIN), array(*WOUT),
            array(2, ROWS, 128, kind=F32), array(2, ROWS, R, kind=F32),
            array(*ACT, kind=F32), array(ROWS, 128, kind=F32),
        ],
        LOW_SCRATCH,
    )
    up2, acts1 = call(
        kernel_high,
        scalars,
        [x2, hat2, rstd2, cotangent, *pairs[1]],
        [array(*ACT), array(*ACTS)],
        HIGH_SCRATCH,
    )
    got1 = shift(acts1[1], SWAP)
    acts0 = call(
        kernel_low_back,
        scalars,
        [inputs, x1, up2, win, wout, stat0, stat1, pre],
        array(*ACTS),
        BACK_SCRATCH,
    )
    got0 = shift(acts0[1], SWAP)
    first1 = scatter_first(scalars, acts1, got1)
    first0 = scatter_first(scalars, acts0, got0)
    sides1 = scatter_sides(scalars, *first1)
    sides0 = scatter_sides(scalars, *first0)
    grads = scatter_second(scalars, sides0, sides1)
    parts = jnp.concatenate(
        [
            grads[:, :8].reshape(2, 4, 32, 256),
            grads[:, 8:16].reshape(2, 8, 4, 4, 256).transpose(0, 2, 1, 3, 4).reshape(2, 4, 32, 256),
            jnp.pad(grads[:, 16, 0, :128].reshape(2, 4, 1, 32), ((0, 0), (0, 0), (0, 7), (0, 224))),
        ],
        axis=2,
    ).reshape(8, 72, 256)
    return call(
        kernel_finish,
        scalars,
        [lax.all_to_all(parts, ("zl", "zh"), 0, 0)],
        (array(1, 32, kind=F32), array(1, 32, 256, kind=F32), array(1, 4, 2048, kind=F32)),
        [],
    )


def solution(mesh):
    fine = Mesh(mesh.devices.reshape(DIMS), AXES)
    zero = ("x", "y", "zh")
    segment = ("zl", "c")
    return jax.shard_map(
        device_body,
        mesh=fine,
        in_specs=(
            P(None, None, zero, None),
            P(None, None, zero, None),
            P(segment, zero),
            P(segment, zero, None),
            P(segment, zero, None),
        ),
        out_specs=(P(segment, zero), P(segment, zero, None), P(segment, zero, None)),
        check_vma=False,
    )
```

```python
import functools
import itertools

import jax
import jax.numpy as jnp
import numpy as np
from jax import lax
from jax.experimental import pallas as pl
from jax.experimental.pallas import tpu as pltpu
from jax.sharding import Mesh
from jax.sharding import PartitionSpec as P


gelu_coeff = 0.7978845608028654
cubic_coeff = 0.044715
norm_eps = 1e-05

AXES = ("zl", "c", "x", "y", "zh")
DIMS = (2, 2, 4, 4, 4)
D = 2048
R = 256
ROWS = 128
CHUNK = 16
F32 = jnp.float32
BF16 = jnp.bfloat16


def flat_perm(move):
    pairs = []
    for src, coords in enumerate(itertools.product(*[range(n) for n in DIMS])):
        dst = [v % n for v, n in zip(move(*coords), DIMS)]
        pairs.append((src, int(np.ravel_multi_index(dst, DIMS))))
    return pairs


def send_first(k):
    return flat_perm(
        lambda zl, c, x, y, zh: (zl, c, x + k, y, zh) if c == 0 else (zl, c, x, y + k, zh)
    )


def send_second(k):
    return flat_perm(
        lambda zl, c, x, y, zh: (zl, c, x, y + k, zh) if c == 0 else (zl, c, x + k, y, zh)
    )


SWAP = flat_perm(lambda zl, c, x, y, zh: (zl, c + 1, x, y, zh))


def shift(value, pairs):
    return lax.ppermute(value, AXES, pairs)


def around(value, send):
    after, before = shift(value, send(-1)), shift(value, send(-3))
    return [after, shift(value, send(-2)), before]


def dot(left, right, left_dim=1, right_dim=0):
    return lax.dot_general(
        left, right, (((left_dim,), (right_dim,)), ((), ())), preferred_element_type=F32
    )


def gelu_parts(v):
    inner = jnp.tanh(gelu_coeff * (v + cubic_coeff * v * v * v))
    return inner, (0.5 * v * (1.0 + inner)).astype(BF16)


def gelu_slope(v, inner):
    return 0.5 * (1.0 + inner) + 0.5 * v * (1.0 - inner * inner) * gelu_coeff * (
        1.0 + 3.0 * cubic_coeff * v * v
    )


def place_weights(s_ref, pieces, win, wout):
    mx, my, c = s_ref[0], s_ref[1], s_ref[2]
    for o in range(2):
        par = c if o == 0 else 1 - c
        for src, (b, first, count) in zip(pieces[o * PIECES : (o + 1) * PIECES], SPANS):

            def place(i, carry, par=par, src=src, b=b, first=first):
                a = first + i
                x = (mx + jnp.where(par == 0, a, b)) & 3
                y = (my + jnp.where(par == 0, b, a)) & 3
                xy = x * 4 + y
                win[par, pl.ds(xy * 8, 8)] = src[i, 0:8]
                for k in range(9):
                    wout[par, k, xy] = src[i, 8 + k]
                return carry

            lax.fori_loop(0, count, place, 0)


def gain_row(wout, par):
    return jnp.concatenate(
        [wout[par, 8, xy, 0:1, 0:128] for xy in range(16)], axis=1
    ).astype(F32)


def over_rows(step):
    def body(i, carry):
        step(pl.ds(pl.multiple_of(i * CHUNK, CHUNK), CHUNK))
        return carry

    lax.fori_loop(0, ROWS // CHUNK, body, 0, unroll=UNROLL)


def hat_pass(x_at, hat, keep_stat):
    def step(rows):
        xf = x_at(rows).astype(F32)
        mean = jnp.mean(xf, axis=-1, keepdims=True)
        centered = xf - mean
        variance = jnp.mean(centered * centered, axis=-1, keepdims=True)
        recip_std = lax.rsqrt(variance + norm_eps)
        hat[rows, :] = centered * recip_std
        keep_stat(rows, mean, recip_std)

    over_rows(step)


def spread(column):
    return jnp.broadcast_to(column, (CHUNK, 128))


def layer_out(x_at, act, wout, par, out_ref):
    for k in range(8):
        cols = pl.ds(k * 256, 256)
        out_ref[:, cols] = (
            x_at(cols).astype(F32) + dot(act, wout[par, k].reshape(R, 256))
        ).astype(BF16)


def layer_back(up_at, acts, slot, hat, rstd_at, preact, win, wout, par, gain, gnorm, gsum, up_out):
    inner, act = gelu_parts(preact)
    grad_act = jnp.zeros((ROWS, R), F32)
    for k in range(8):
        grad_act += dot(
            up_at(pl.ds(0, ROWS), pl.ds(k * 256, 256)), wout[par, k].reshape(R, 256), 1, 1
        )
    grad_pre = (grad_act * gelu_slope(preact, inner)).astype(BF16)
    acts[slot, 0:ROWS, ACT_AT : ACT_AT + R] = act
    acts[slot, 0:ROWS, PRE_AT : PRE_AT + R] = grad_pre
    for k in range(8):
        gnorm[:, pl.ds(k * 256, 256)] = dot(
            grad_pre, win[par, pl.ds(k * 16, 16)].reshape(256, R), 1, 1
        )
    gsum[...] = jnp.zeros((CHUNK, D), F32)

    def step(rows):
        grad_normed = gnorm[rows, :]
        hatted = hat[rows, :]
        product = grad_normed * hatted
        gsum[...] += product
        up = up_at(rows, pl.ds(0, D))
        acts[slot, rows, UP_AT : UP_AT + D] = up
        if up_out is not None:
            grad_hat = grad_normed * gain
            mean_hat = jnp.mean(grad_hat, axis=-1, keepdims=True)
            mean_both = jnp.mean(product * gain, axis=-1, keepdims=True)
            through = rstd_at(rows) * (grad_hat - mean_hat - hatted * mean_both)
            up_out[rows, :] = (up.astype(F32) + through).astype(BF16)

    over_rows(step)
    acts[slot, ROWS : ROWS + 16, 0:D] = jnp.broadcast_to(
        jnp.sum(gsum[...], axis=0, keepdims=True), (16, D)
    ).astype(BF16)


def kernel_stats(s_ref, xs, hat, stat):
    c, zl = s_ref[2], s_ref[3]

    def keep_stat(rows, mean, recip_std):
        stat[0, rows, :] = spread(mean)
        stat[1, rows, :] = spread(recip_std)

    hat_pass(lambda rows: xs[zl, c, rows, :], hat, keep_stat)


def kernel_low_forward(s_ref, xs, hat0, *refs):
    pieces = refs[: 2 * PIECES]
    x1, x2, win, wout, stat1, pre, hat2, rstd2, normed, hat1 = refs[2 * PIECES :]
    place_weights(s_ref, pieces, win, wout)
    c, zl = s_ref[2], s_ref[3]

    def keep_stat(rows, mean, recip_std):
        stat1[0, rows, :] = spread(mean)
        stat1[1, rows, :] = spread(recip_std)

    for par, hat in enumerate((hat0, hat1)):
        if par:
            hat_pass(lambda rows: x1[rows, :], hat1, keep_stat)
        gain = gain_row(wout, par)

        def step(rows, gain=gain, hat=hat):
            normed[rows, :] = (hat[rows, :] * gain).astype(BF16)

        over_rows(step)
        pre[par] = dot(normed[...], win[par].reshape(D, R))
        act = gelu_parts(pre[par])[1]
        if par:
            layer_out(lambda cols: x1[:, cols], act, wout, par, x2)
        else:
            layer_out(lambda cols: xs[zl, c, :, cols], act, wout, par, x1)

    def keep_rstd(rows, mean, recip_std):
        rstd2[rows, :] = spread(recip_std)

    hat_pass(lambda rows: x2[rows, :], hat2, keep_rstd)


def kernel_high(s_ref, x2, hat0, rstd0, cots, *refs):
    pieces = refs[: 2 * PIECES]
    up2, acts, win, wout, hat1, rstd1, x3, up3, pre0, gnorm, gsum = refs[2 * PIECES :]
    place_weights(s_ref, pieces, win, wout)
    c, zl = s_ref[2], s_ref[3]
    gains = []

    def keep_rstd(rows, mean, recip_std):
        rstd1[rows, :] = spread(recip_std)

    for par, hat in enumerate((hat0, hat1)):
        if par:
            hat_pass(lambda rows: x3[rows, :], hat1, keep_rstd)
        gain = gain_row(wout, par)
        slot = jnp.where(c == par, 0, 1)

        def step(rows, gain=gain, hat=hat, slot=slot):
            acts[slot, rows, 0:D] = (hat[rows, :] * gain).astype(BF16)

        over_rows(step)
        preact = dot(acts[slot, 0:ROWS, 0:D], win[par].reshape(D, R))
        gains.append(gain)
        if par == 0:
            pre0[...] = preact
            layer_out(lambda cols: x2[:, cols], gelu_parts(preact)[1], wout, 0, x3)
    layer_back(
        lambda rows, cols: cots[zl, c, rows, cols],
        acts, jnp.where(c == 1, 0, 1), hat1, lambda rows: rstd1[rows, 0:1],
        preact, win, wout, 1, gains[1], gnorm, gsum, up3,
    )
    layer_back(
        lambda rows, cols: up3[rows, cols],
        acts, jnp.where(c == 0, 0, 1), hat0, lambda rows: rstd0[rows, 0:1],
        pre0[...], win, wout, 0, gains[0], gnorm, gsum, up2,
    )


def kernel_low_back(s_ref, xs, x1, up2, win, wout, stat0, stat1, pre, acts, hat, up1, gnorm, gsum):
    c, zl = s_ref[2], s_ref[3]
    for par, stat, up, up_out in ((1, stat1, up2, up1), (0, stat0, up1, None)):
        gain = gain_row(wout, par)
        slot = jnp.where(c == par, 0, 1)

        def step(rows, par=par, stat=stat, gain=gain, slot=slot):
            xf = (x1[rows, :] if par else xs[zl, c, rows, :]).astype(F32)
            hatted = (xf - stat[0, rows, 0:1]) * stat[1, rows, 0:1]
            hat[rows, :] = hatted
            acts[slot, rows, 0:D] = (hatted * gain).astype(BF16)

        over_rows(step)
        layer_back(
            lambda rows, cols, up=up: up[rows, cols],
            acts, slot, hat, lambda rows, stat=stat: stat[1, rows, 0:1],
            pre[par], win, wout, par, gain, gnorm, gsum, up_out,
        )


def kernel_grads(s_ref, acts, got, out, up, down):
    mx, my, c = s_ref[0], s_ref[1], s_ref[2]
    places = []
    for xy in range(16):
        xr = (xy // 4 - mx) & 3
        yr = (xy % 4 - my) & 3
        places.append(jnp.where(c == 0, xr * 4 + yr, yr * 4 + xr))

    def both(start, size):
        cols = pl.ds(start, size)
        return jnp.concatenate([acts[0, 0:ROWS, cols], got[0:ROWS, cols]], axis=0)

    grad_pre = both(PRE_AT, R)
    for xy in range(16):
        block = dot(both(xy * 128, 128).T, grad_pre)
        out[places[xy], 0:8] = block.astype(BF16).reshape(8, 16, 256)
    act_t = both(ACT_AT, R).T
    for k in range(8):
        block = dot(act_t, both(UP_AT + k * 256, 256)).astype(BF16).reshape(16, 16, 256)
        for xy in range(16):
            out[places[xy], 8 + k] = block[xy]
    for xy in range(16):
        cols = pl.ds(xy * 128, 128)
        part = acts[0, ROWS : ROWS + 16, cols].astype(F32) + got[ROWS : ROWS + 16, cols].astype(F32)
        out[places[xy], 16] = jnp.concatenate([part, part], axis=1).astype(BF16)


    up[...] = out[8:10]
    down[...] = out[10:12]


def over_groups(step):
    def body(g, carry):
        step(g)
        return carry

    lax.fori_loop(0, 17, body, 0)


def kernel_sides(s_ref, grads, up, down, after, before):
    def step(g):
        for i in range(2):
            after[i, g] = (grads[4 + i, g].astype(F32) + up[i, g].astype(F32)).astype(BF16)
            after[2 + i, g] = grads[6 + i, g]
            before[i, g] = grads[12 + i, g]
            before[2 + i, g] = (grads[14 + i, g].astype(F32) + down[i, g].astype(F32)).astype(BF16)

    over_groups(step)


def kernel_sum(s_ref, low, low_a, low_b, high, high_a, high_b, *pieces):
    def step(g):
        for p, (own, a, b) in enumerate(((low, low_a, low_b), (high, high_a, high_b))):
            for k in range(4):
                pieces[k][p, g] = (
                    own[k, g].astype(F32) + a[k, g].astype(F32) + b[k, g].astype(F32)
                ).astype(BF16)

    over_groups(step)


def kernel_finish(s_ref, parts, gain, grad_in, grad_out):
    total = parts[0].astype(F32)
    for i in range(1, 8):
        total += parts[i].astype(F32)
    grad_in[0] = total[0:32]
    for k in range(8):
        grad_out[0, :, pl.ds(k * 256, 256)] = total[32 + 4 * k : 36 + 4 * k]
    gain[...] = total[64:65, 0:32]


def vmem(*shape, kind=BF16):
    return pltpu.VMEM(shape, kind)


def array(*shape, kind=BF16):
    return jax.ShapeDtypeStruct(shape, kind)


UNROLL = 8
SPANS = tuple((b, 0, 4) for b in range(4))
PIECES = len(SPANS)
UP_AT, ACT_AT, PRE_AT, WIDE = D, 2 * D, 2 * D + R, 2 * D + 2 * R
ACT = (ROWS, D)
WIN, WOUT = (2, 128, 16, 256), (2, 9, 16, 16, 256)
ACTS = (2, ROWS + 16, WIDE)
HAT = vmem(ROWS, D, kind=F32)
GSUM = vmem(CHUNK, D, kind=F32)
LOW_SCRATCH = [vmem(*ACT), HAT]
HIGH_SCRATCH = [
    vmem(*WIN), vmem(*WOUT), HAT, vmem(ROWS, 128, kind=F32),
    vmem(*ACT), vmem(*ACT), vmem(ROWS, R, kind=F32), HAT, GSUM,
]
BACK_SCRATCH = [HAT, vmem(*ACT), HAT, GSUM]
WHOLE = pl.BlockSpec(memory_space=pltpu.VMEM)


def call(body, scalars, args, out_shape, scratch):
    return pl.pallas_call(
        body,
        in_specs=[pl.BlockSpec(memory_space=pltpu.SMEM)] + [WHOLE] * len(args),
        out_specs=jax.tree.map(lambda s: WHOLE, out_shape),
        scratch_shapes=scratch,
        out_shape=out_shape,
        compiler_params=pltpu.CompilerParams(vmem_limit_bytes=20 * 1024 * 1024),
    )(scalars, *args)


def add_up(first, got):
    return functools.reduce(lambda p, q: p + q.astype(F32), got, first.astype(F32)).astype(BF16)


def scatter_first(scalars, acts, got):
    half = array(2, 17, 16, 256)
    grads, up, down = call(
        kernel_grads, scalars, [acts, got], [array(16, 17, 16, 256), half, half], []
    )
    return grads, shift(up, send_first(1)), shift(down, send_first(-1))


def scatter_sides(scalars, grads, up, down):
    row = array(4, 17, 16, 256)
    after, before = call(kernel_sides, scalars, [grads, up, down], [row, row], [])
    return grads, shift(after, send_first(1)), shift(before, send_first(-1))


def scatter_second(scalars, low, high):
    piece = array(2, 17, 16, 256)
    own, *pieces = call(kernel_sum, scalars, [*low, *high], [piece] * 4, [])
    got = [shift(pieces[k - 1], send_second(k)) for k in (1, 3)]
    got.append(shift(pieces[1], send_second(2)))
    return add_up(own, got)


def device_body(inputs, cotangent, norm_gain, proj_in, proj_out):
    where = [lax.axis_index(n).astype(jnp.int32) for n in ("x", "y", "c", "zl")]
    scalars = jnp.stack(where)
    shard = jnp.concatenate(
        [
            proj_in[0],
            proj_out[0].reshape(4, 8, 256).transpose(1, 0, 2).reshape(32, 256),
            jnp.pad(norm_gain, ((0, 7), (0, 224))),
        ],
        axis=0,
    )
    column = lax.all_to_all(
        jnp.broadcast_to(shard[None], (8, 72, 256)), ("zl", "zh"), 0, 0
    ).reshape(2, 4, 72, 256)
    gain = jnp.pad(column[:, :, 64, :32].reshape(2, 1, 1, 128), ((0, 0), (0, 0), (0, 15), (0, 128)))
    block = jnp.concatenate(
        [
            column[:, :, :32].reshape(2, 8, 16, 256),
            column[:, :, 32:64].reshape(2, 4, 8, 4, 256).transpose(0, 2, 1, 3, 4).reshape(2, 8, 16, 256),
            gain,
        ],
        axis=1,
    )
    hat0, stat0 = call(
        kernel_stats, scalars, [inputs], [array(*ACT, kind=F32), array(2, ROWS, 128, kind=F32)], []
    )
    near = []
    for p in range(2):
        near.append([block[p]] + around(block[p], send_first))
    pairs = []
    for p in range(2):
        row = jnp.stack(near[p])
        rows = [row] + around(row, send_second)
        pairs.append(rows + [shift(v, SWAP) for v in rows])
    x1, x2, win, wout, stat1, pre, hat2, rstd2 = call(
        kernel_low_forward,
        scalars,
        [inputs, hat0, *pairs[0]],
        [
            array(*ACT), array(*ACT), array(*WIN), array(*WOUT),
            array(2, ROWS, 128, kind=F32), array(2, ROWS, R, kind=F32),
            array(*ACT, kind=F32), array(ROWS, 128, kind=F32),
        ],
        LOW_SCRATCH,
    )
    up2, acts1 = call(
        kernel_high,
        scalars,
        [x2, hat2, rstd2, cotangent, *pairs[1]],
        [array(*ACT), array(*ACTS)],
        HIGH_SCRATCH,
    )
    got1 = shift(acts1[1], SWAP)
    acts0 = call(
        kernel_low_back,
        scalars,
        [inputs, x1, up2, win, wout, stat0, stat1, pre],
        array(*ACTS),
        BACK_SCRATCH,
    )
    got0 = shift(acts0[1], SWAP)
    first1 = scatter_first(scalars, acts1, got1)
    first0 = scatter_first(scalars, acts0, got0)
    sides1 = scatter_sides(scalars, *first1)
    sides0 = scatter_sides(scalars, *first0)
    grads = scatter_second(scalars, sides0, sides1)
    parts = jnp.concatenate(
        [
            grads[:, :8].reshape(2, 4, 32, 256),
            grads[:, 8:16].reshape(2, 8, 4, 4, 256).transpose(0, 2, 1, 3, 4).reshape(2, 4, 32, 256),
            jnp.pad(grads[:, 16, 0, :128].reshape(2, 4, 1, 32), ((0, 0), (0, 0), (0, 7), (0, 224))),
        ],
        axis=2,
    ).reshape(8, 72, 256)
    return call(
        kernel_finish,
        scalars,
        [lax.all_to_all(parts, ("zl", "zh"), 0, 0)],
        (array(1, 32, kind=F32), array(1, 32, 256, kind=F32), array(1, 4, 2048, kind=F32)),
        [],
    )


def solution(mesh):
    fine = Mesh(mesh.devices.reshape(DIMS), AXES)
    zero = ("x", "y", "zh")
    segment = ("zl", "c")
    return jax.shard_map(
        device_body,
        mesh=fine,
        in_specs=(
            P(None, None, zero, None),
            P(None, None, zero, None),
            P(segment, zero),
            P(segment, zero, None),
            P(segment, zero, None),
        ),
        out_specs=(P(segment, zero), P(segment, zero, None), P(segment, zero, None)),
        check_vma=False,
    )
```
